32 devices in a mesh: wide: 16 (over z, x, core), narrow: 2 (over y).
Axes of the slice: x: 2, y: 2, z: 4, core: 2. Of those that a mesh axis runs over, the one named last changes fastest.
Arguments:
- decoder_input: bfloat16 [64, 232, 1024], P(('wide', 'narrow')), may hold values from -6 to 6
- memory: bfloat16 [64, 1024, 1024], P(('wide', 'narrow')), may hold values from -6 to 6
- decoder_mask: int32 [64, 232], P(('wide', 'narrow')), may hold values from 0 to 1, as said below
- memory_length: int32 [64], P(('wide', 'narrow')), may hold values from 51 to 1024, as said below
- self_weights: bfloat16 [4, 1024, 1024], P(None, 'wide', 'narrow')
- cross_weights: bfloat16 [4, 1024, 1024], P(None, 'wide', 'narrow')
- feed_weights: bfloat16 [2, 1024, 4096], P(None, 'wide', 'narrow')
- vectors: float32 [13, 1024], P(None, 'narrow')
- hidden_bias: float32 [1, 4096], P(None, 'narrow'), may hold values from -3 to 3
- cotangent: bfloat16 [64, 232, 1024], P(('wide', 'narrow')), may hold values from -6 to 6
Outputs:
- layer_output: bfloat16 [64, 232, 1024], P(('wide', 'narrow'))
- input_grad: float32 [64, 232, 1024], P(('wide', 'narrow'))
- memory_grad: float32 [64, 1024, 1024], P(('wide', 'narrow'))
- self_weight_gradient: float32 [4, 1024, 1024], P(None, 'wide', 'narrow')
- cross_grad: float32 [4, 1024, 1024], P(None, 'wide', 'narrow')
- feed_grad: float32 [2, 1024, 4096], P(None, 'wide', 'narrow')
- vectors_grad: float32 [13, 1024], P(None, 'narrow')
- hidden_bias_grad: float32 [1, 4096], P(None, 'narrow')
The draws below stay inside these ranges and needn't reach their ends.
Inputs may be any that keep to these rules, and one draw needn't show every extreme that they name: `decoder_mask`: each row is ones followed by zeros, with 116 or more ones; some row has all 232 ones and some row exactly 116. `memory_length`: memory slots from this length on are padding; some sequence has every slot valid and some has the fewest.
All inputs are finite; a program needn't handle non-finite values.
Results may differ from the reference program's by a relative error of at most 0.029.
The reference program's roundings to bfloat16 on the way count: a program that leaves them out, or rounds other values in their place, can miss the bound.
Values may be sent and summed in bfloat16 or wider, within the bound.
A program may use at most 256 MiB of HBM per device.

```python
import math
import jax
import jax.numpy as jnp
from jax import lax

D = 1024
HEADS = 16
HEAD_DIM = 64
FF = 4096
L_DEC = 232
MEM = 1024
NVEC = 13
SEQ_DEV = 2
BATCH = 64


def normal_noise(key, shape):
    return jax.random.normal(key, shape, jnp.float32)


def scaled(noise, factors):
    return (noise * jnp.array(factors, jnp.float32)[:, None, None]).astype(jnp.bfloat16)


def draw_self_weights(key, part):
    base = 1.0 / math.sqrt(D)
    noise = normal_noise(key, (4, D, D))
    return scaled(noise, [1.5 * base, 1.5 * base, base, 4.0 * base])


def draw_cross_weights(key, part):
    base = 1.0 / math.sqrt(D)
    noise = normal_noise(key, (4, D, D))
    return scaled(noise, [1.5 * base, 1.5 * base, base, 6.0 * base])


def draw_feed_weights(key, part):
    noise = normal_noise(key, (2, D, FF))
    return scaled(noise, [1.0 / math.sqrt(D), 1.5 / math.sqrt(FF)])


def draw_vectors(key, part):
    gain_key, shift_key = jax.random.split(key)
    gains = jax.random.uniform(gain_key, (NVEC, D), jnp.float32, 0.5, 1.5)
    shifts = 0.3 * jax.random.normal(shift_key, (NVEC, D), jnp.float32)
    row_index = jnp.arange(NVEC)[:, None]
    is_gain = (row_index == 3) | (row_index == 8) | (row_index == 11)
    return jnp.where(is_gain, gains, shifts).astype(jnp.float32)


def draw_decoder_mask(key, part):
    lengths = jax.random.randint(key, (BATCH,), L_DEC // 2, L_DEC + 1)
    lengths = lengths.at[0].set(L_DEC).at[1].set(L_DEC // 2)
    positions = jnp.arange(L_DEC)
    return (positions[None, :] < lengths[:, None]).astype(jnp.int32)


def draw_memory_length(key, part):
    lowest = max(1, MEM // 20)
    lengths = jax.random.randint(key, (BATCH,), lowest, MEM + 1)
    return lengths.at[0].set(MEM).at[1].set(lowest).astype(jnp.int32)


def level_of(own_key, shape, cuts, low, largest):
    level = 1.0
    for axis_at, parts in cuts:
        heights = jax.random.uniform(jax.random.fold_in(jax.random.fold_in(own_key, 6), axis_at), (parts,), jnp.float32, low / len(cuts), largest / len(cuts))
        level = level * jnp.repeat(jnp.exp(heights), shape[axis_at] // parts).reshape((-1,) + (1,) * (len(shape) - 1 - axis_at))
    return level


def centred(rng, extent, scale, limit, pieces=(), held_as=jnp.bfloat16):
    level = level_of(rng, extent, pieces, -0.22, 0.18) if pieces else 1.0
    drawn = jax.random.normal(rng, extent, jnp.float32) * scale * level
    return jnp.minimum(jnp.maximum(drawn, -limit), limit).astype(held_as)


def setup_inputs(seed: int = 0) -> dict:
    key_list = jax.random.split(jax.random.key(seed), 11)
    return {
        "decoder_input": centred(key_list[0], (BATCH, L_DEC, D), 1.0, 6.0, ((0, 32),)),
        "memory": centred(key_list[1], (BATCH, MEM, D), 1.0, 6.0, ((0, 32),)),
        "decoder_mask": draw_decoder_mask(jax.random.fold_in(key_list[10], 71), 0),
        "memory_length": draw_memory_length(jax.random.fold_in(key_list[10], 71), 0),
        "self_weights": draw_self_weights(jax.random.fold_in(key_list[10], 71), 0),
        "cross_weights": draw_cross_weights(jax.random.fold_in(key_list[10], 71), 0),
        "feed_weights": draw_feed_weights(jax.random.fold_in(key_list[10], 71), 0),
        "vectors": draw_vectors(jax.random.fold_in(key_list[10], 71), 0),
        "hidden_bias": centred(key_list[8], (1, FF), 0.5, 3.0, ((1, 2),), jnp.float32),
        "cotangent": centred(key_list[9], (BATCH, L_DEC, D), 1.0, 6.0, ((0, 32),)),
    }


NEGATIVE = -1000000000.0
EPSILON = 1e-05
PRECISION_HIGH = lax.Precision.HIGHEST

@jax.custom_vjp
def low(v):
    return lax.optimization_barrier(v.astype(jnp.bfloat16)).astype(jnp.float32)

@jax.custom_vjp
def low_back(v):
    return v

def low_keep(v):
    return (low(v), None)

def low_pass(kept, grad):
    return (grad,)

def back_keep(v):
    return (v, None)

def back_low(kept, grad):
    return (low(grad),)
low.defvjp(low_keep, low_pass)
low_back.defvjp(back_keep, back_low)

def rounded(value):
    return low_back(low(value))

def matmul(left, right):
    return jnp.dot(left, right, precision=PRECISION_HIGH)

def layer_norm(hidden, gain, shift):
    centre = hidden - lax.optimization_barrier(jnp.mean(hidden, axis=-1, keepdims=True))
    spread = lax.optimization_barrier(jnp.mean(centre * centre, axis=-1, keepdims=True))
    return centre * lax.rsqrt(spread + EPSILON) * gain + shift

def attend(items):
    query_rows, key_matrix_rows, value_matrix_rows, allowed = items
    score_matrix = jnp.einsum('qkv,wkv->kqw', query_rows, key_matrix_rows, precision=PRECISION_HIGH)
    score_matrix = low_back(jnp.where(allowed[None], score_matrix, NEGATIVE))
    weight_matrices = low(jax.nn.softmax(score_matrix, axis=-1))
    return jnp.einsum('uqv,vup->qup', weight_matrices, value_matrix_rows, precision=PRECISION_HIGH)

def heads_of(rows, count):
    return rows.reshape(count, -1, HEADS, HEAD_DIM)

def layer(inputs, memories, self_w, cross_w, feed_w, vector_rows, hidden_b, masks, lengths):
    count, seq_length, model_width = inputs.shape
    span = memories.shape[1]
    scale = HEAD_DIM ** (-0.5)
    flat = inputs.reshape(count * seq_length, model_width)
    mem_flat = memories.reshape(count * span, model_width)
    positions = jnp.arange(seq_length)
    causal = positions[:, None] >= positions[None, :]
    self_allowed = causal[None] & (masks[:, None, :] == 1)
    cross_allowed = (jnp.arange(span)[None, :] < lengths[:, None])[:, None, :]
    self_q = rounded((matmul(flat, self_w[0]) + vector_rows[0]) * scale)
    self_k = rounded(matmul(flat, self_w[1]))
    self_v = rounded(matmul(flat, self_w[2]) + vector_rows[1])
    mixed = lax.map(jax.checkpoint(attend), (heads_of(self_q, count), heads_of(self_k, count), heads_of(self_v, count), self_allowed))
    mixed = rounded(mixed.reshape(count * seq_length, model_width))
    branch = low_back(matmul(mixed, self_w[3]) + vector_rows[2])
    first = layer_norm(flat + branch, vector_rows[3], vector_rows[4])
    first_low = low(first)
    cross_q = rounded((matmul(first_low, cross_w[0]) + vector_rows[5]) * scale)
    cross_k = rounded(matmul(mem_flat, cross_w[1]))
    cross_v = rounded(matmul(mem_flat, cross_w[2]) + vector_rows[6])
    cmixed = lax.map(jax.checkpoint(attend), (heads_of(cross_q, count), heads_of(cross_k, count), heads_of(cross_v, count), cross_allowed))
    cmixed = rounded(cmixed.reshape(count * seq_length, model_width))
    cbranch = low_back(matmul(cmixed, cross_w[3]) + vector_rows[7])
    second = layer_norm(first + cbranch, vector_rows[8], vector_rows[9])
    second_low = low(second)
    inner = low_back(matmul(second_low, feed_w[0]) + hidden_b[0])
    hidden = low(jax.nn.gelu(inner, approximate=False))
    fbranch = low_back(matmul(hidden, feed_w[1].T) + vector_rows[10])
    output = layer_norm(second + fbranch, vector_rows[11], vector_rows[12])
    return output.reshape(count, seq_length, model_width)

def reference(decoder_input, memory, decoder_mask, memory_length, self_weights, cross_weights, feed_weights, vectors, hidden_bias, cotangent):
    params = (self_weights.astype(jnp.float32), cross_weights.astype(jnp.float32), feed_weights.astype(jnp.float32), vectors, hidden_bias)
    groups = decoder_input.shape[0] // SEQ_DEV

    def split_groups(array):
        return array.reshape((groups, SEQ_DEV) + array.shape[1:])

    def step(totals, items):
        inputs, memories, masks, lengths, cotan = items

        def forward(inp, mem, self_w, cross_w, feed_w, vector_rows, hidden_b):
            return layer(inp, mem, self_w, cross_w, feed_w, vector_rows, hidden_b, masks, lengths)
        output, pull = jax.vjp(forward, inputs.astype(jnp.float32), memories.astype(jnp.float32), params[0], params[1], params[2], params[3], params[4])
        grads = pull(cotan.astype(jnp.float32))
        totals = tuple((total + grad for total, grad in zip(totals, grads[2:])))
        return (totals, (output.astype(jnp.bfloat16), grads[0], grads[1]))
    zeros = tuple((jnp.zeros(param.shape, jnp.float32) for param in params))
    items = (split_groups(decoder_input), split_groups(memory), split_groups(decoder_mask), split_groups(memory_length), split_groups(cotangent))
    totals, stacked = lax.scan(step, zeros, items)
    outputs, input_grads, memory_grads = stacked
    return (outputs.reshape(decoder_input.shape), input_grads.reshape(decoder_input.shape), memory_grads.reshape(memory.shape), totals[0], totals[1], totals[2], totals[3], totals[4])
```

```python
import functools
import math

import jax
import jax.numpy as jnp
from jax import lax
from jax.experimental import pallas as pl
from jax.experimental.pallas import tpu as pltpu
from jax.sharding import PartitionSpec as P

HEADS = 16
HEAD_DIM = 64


NEGATIVE = -1000000000.0
EPSILON = 1e-05


def layer_norm(hidden, gain, shift):
    centre = hidden - jnp.mean(hidden, axis=-1, keepdims=True)
    spread = jnp.mean(centre * centre, axis=-1, keepdims=True)
    return centre * lax.rsqrt(spread + EPSILON) * gain + shift


def gelu_exact(inner):
    return jax.nn.gelu(inner, approximate=False)


def linear(left, right):
    return jnp.dot(left, right, preferred_element_type=jnp.float32)


def linear_tr(left, right):
    return lax.dot_general(
        left, right, (((1,), (1,)), ((), ())), preferred_element_type=jnp.float32
    )


def outer_sum(left, right):
    return lax.dot_general(
        left, right, (((0,), (0,)), ((), ())), preferred_element_type=jnp.float32
    )


def column_sum(grad_low):
    return jnp.sum(grad_low.astype(jnp.float32), axis=0)


MESH_ID = pl.DeviceIdType.MESH


class Position:
    def __init__(self, wide, narrow):
        index = lax.axis_index("wide")
        self.core = index % 2
        self.pair = (index // 2) % 2
        self.line = index // 4
        self.column = lax.axis_index("narrow")
        self.sizes = {"line": wide // 4, "pair": 2, "core": 2, "column": narrow}

    def get(self, axis):
        return getattr(self, axis)

    def device(self, **moved):
        spot = {name: moved.get(name, self.get(name)) for name in self.sizes}
        return (spot["line"] * 4 + spot["pair"] * 2 + spot["core"], spot["column"])


class Channels:
    def __init__(self, sends, recvs):
        self.sends, self.recvs, self.used = sends, recvs, 0

    def take(self):
        self.used += 1
        return self.sends.at[self.used - 1], self.recvs.at[self.used - 1]


def remote(source, target, channel, device):
    return pltpu.make_async_remote_copy(
        src_ref=source,
        dst_ref=target,
        send_sem=channel[0],
        recv_sem=channel[1],
        device_id=device,
        device_id_type=MESH_ID,
    )


def greet(position, doubling=False):
    barrier = pltpu.get_barrier_semaphore()

    def signal(device):
        pl.semaphore_signal(barrier, inc=1, device_id=device, device_id_type=MESH_ID)

    expected = 2
    signal(position.device(core=1 - position.core))
    signal(position.device(pair=1 - position.pair))
    for axis in ("line", "column"):
        size, index = position.sizes[axis], position.get(axis)
        if size == 2:
            signal(position.device(**{axis: 1 - index}))
            expected = expected + 1
        elif size > 2:

            @pl.when(index > 0)
            def _():
                signal(position.device(**{axis: index - 1}))

            @pl.when(index < size - 1)
            def _():
                signal(position.device(**{axis: index + 1}))

            expected = expected + jnp.where(index > 0, 1, 0) + jnp.where(index < size - 1, 1, 0)
        if doubling and size > 2:
            bit = 1
            while bit < size:
                signal(position.device(**{axis: flip(index, bit)}))
                expected = expected + 1
                bit *= 2
    pl.semaphore_wait(barrier, expected)


def flip(index, bit):
    return index + bit - 2 * bit * ((index // bit) % 2)


def advance(generator):
    return next(generator, "done") != "done"


def run_rounds(flows, live=()):
    waiting, live = list(flows), list(live)
    while waiting or live:
        live = live + waiting[:2]
        waiting = waiting[2:]
        live = [flow for flow in live if advance(flow)]


def gather_axis(position, axis, channels, block, own, sent):
    size, index = position.sizes[axis], position.get(axis)
    if size == 2:
        channel = channels.take()
        other = position.device(**{axis: 1 - index})
        copy = remote(own, block(index), channel, other)
        copy.start()
        sent.append((None, copy))
        yield
        remote(own, block(1 - index), channel, other).wait_recv()
        return
    for step in range(1, size):
        for sign in (1, -1):
            channel = channels.take()
            held = index - sign * (step - 1)
            target = index + sign
            active = (held >= 0) & (held < size) & (target >= 0) & (target < size)
            device = position.device(**{axis: target})
            source = own if step == 1 else block(held)
            copy = remote(source, block(held), channel, device)

            @pl.when(active)
            def _():
                copy.start()

            sent.append((active, copy))
        pairs = channels.used
        yield
        for place, sign in ((pairs - 2, 1), (pairs - 1, -1)):
            came = index - sign * step
            channel = (channels.sends.at[place], channels.recvs.at[place])
            device = position.device(**{axis: index - sign})

            @pl.when((came >= 0) & (came < size))
            def _():
                remote(own, block(came), channel, device).wait_recv()


def finish_sends(sent):
    for active, copy in sent:
        if active is None:
            copy.wait_send()
        else:

            @pl.when(active)
            def _():
                copy.wait_send()


def gather_flow(position, channels, local_sem, own, region, order):
    sent = []
    spot = {axis: position.get(axis) for axis in position.sizes}
    local = pltpu.make_async_copy(own, region(**spot), local_sem)
    local.start()
    for place, axis in enumerate(order):

        def block(j, axis=axis):
            return region(**{**spot, axis: j})

        source = own if place == 0 else block(position.get(axis))
        yield from gather_axis(position, axis, channels, block, source, sent)
        if place == 0:
            local.wait()
        spot[axis] = None
    finish_sends(sent)


def whole(index):
    return slice(None) if index is None else index


def row_splits(rows, most):
    return max(1, min(most, rows // 16))


def gather_channels(wide, narrow):
    line = wide // 4
    count = 2
    count += 1 if line == 2 else 2 * (line - 1)
    count += 1 if narrow == 2 else 2 * (narrow - 1)
    return count


def gather_kernel(wide, narrow, groups, counts, *refs):
    blocks, (vector_ref, bias_ref) = refs[:counts], refs[counts : counts + 2]
    fulls = refs[counts + 2 : 2 * counts + 2]
    vector_out, bias_out, sends, recvs, local_sems = refs[2 * counts + 2 :]
    position = Position(wide, narrow)
    channels = Channels(sends, recvs)
    greet(position)
    flows = []

    def column_flow(block_ref, full_ref, sem):
        def region(column, **ignored):
            return full_ref.at[column]

        sent = []
        local = pltpu.make_async_copy(block_ref, region(position.column), sem)
        local.start()
        yield from gather_axis(position, "column", channels, region, block_ref, sent)
        local.wait()
        finish_sends(sent)

    flows.append(column_flow(vector_ref, vector_out, local_sems.at[0]))
    flows.append(column_flow(bias_ref, bias_out, local_sems.at[1]))
    for number, (array, matrix, part, parts, order) in enumerate(groups):
        block_ref, full_ref = blocks[array], fulls[array]
        rows = block_ref.shape[1] // parts
        width = block_ref.shape[2]

        def region(
            line, pair, core, column, full_ref=full_ref, matrix=matrix, part=part, rows=rows, width=width
        ):
            columns = (
                slice(None)
                if column is None
                else pl.ds(pl.multiple_of(column * width, 128), width)
            )
            return full_ref.at[
                matrix, whole(line), whole(pair), whole(core), pl.ds(part * rows, rows), columns
            ]

        own = block_ref.at[matrix, pl.ds(part * rows, rows)]
        flows.append(
            gather_flow(position, channels, local_sems.at[number + 2], own, region, order)
        )
    run_rounds(flows)


ORDER_A = ("line", "pair", "column", "core")
ORDER_B = ("line", "column", "pair", "core")


def gather_weights(wide, narrow, arrays, vectors, hidden_bias, collective_id):
    groups = []
    for number, array in enumerate(arrays):
        matrices, rows, width = array.shape
        parts = row_splits(rows, 4) if matrices == 2 else 1
        for part in range(parts):
            for matrix in range(matrices):
                groups.append(
                    (number, matrix, part, parts, ORDER_A if matrix % 2 == 0 else ORDER_B)
                )
    copies = gather_channels(wide, narrow) * (len(groups) + 2)
    outs = [
        jax.ShapeDtypeStruct(
            (array.shape[0], wide // 4, 2, 2, array.shape[1], array.shape[2] * narrow), array.dtype
        )
        for array in arrays
    ]
    outs.append(jax.ShapeDtypeStruct((narrow,) + vectors.shape, vectors.dtype))
    outs.append(jax.ShapeDtypeStruct((narrow,) + hidden_bias.shape, hidden_bias.dtype))
    results = pl.pallas_call(
        functools.partial(gather_kernel, wide, narrow, groups, len(arrays)),
        out_shape=outs,
        in_specs=[pl.BlockSpec(memory_space=pltpu.VMEM)] * (len(arrays) + 2),
        out_specs=[pl.BlockSpec(memory_space=pl.ANY)] * len(outs),
        scratch_shapes=[
            pltpu.SemaphoreType.DMA((copies,)),
            pltpu.SemaphoreType.DMA((copies,)),
            pltpu.SemaphoreType.DMA((len(groups) + 2,)),
        ],
        compiler_params=pltpu.CompilerParams(collective_id=collective_id, has_side_effects=True),
        name="gather_weights",
    )(*arrays, vectors, hidden_bias)
    fulls = [
        full.reshape(full.shape[0], -1, full.shape[-1]) for full in results[: len(arrays)]
    ]
    vector_all = jnp.moveaxis(results[-2], 0, 1).reshape(vectors.shape[0], -1)
    bias_all = jnp.moveaxis(results[-1], 0, 1).reshape(1, -1)
    return fulls, vector_all, bias_all


def add_rows(target, first, second):
    lead = target.shape[:-2]
    count = math.prod(lead)

    def place(k):
        where = []
        for extent in reversed(lead):
            where.insert(0, k % extent)
            k = k // extent
        return tuple(where)

    if count == 1:
        spot = (0,) * len(lead)
        target[spot] = (
            first[spot].astype(jnp.float32) + second[spot].astype(jnp.float32)
        ).astype(target.dtype)
        return

    @pl.loop(0, count)
    def _(k):
        spot = place(k)
        target[spot] = (
            first[spot].astype(jnp.float32) + second[spot].astype(jnp.float32)
        ).astype(target.dtype)


def reduce_axis(position, axis, channels, local, slots, result, sent):
    size, index = position.sizes[axis], position.get(axis)
    if size == 2:
        channel = channels.take()
        other = position.device(**{axis: 1 - index})
        copy = remote(local(1 - index), slots.at[0], channel, other)
        copy.start()
        sent.append((None, copy))
        yield
        copy.wait_recv()
        add_rows(result, slots.at[0], local(index))
        return
    taken = [(channels.take(), channels.take()) for _ in range(size - 1)]
    for step in range(size):
        for sign in (1, -1):
            chunk = size - 1 - step if sign == 1 else step
            slot = slots.at[chunk]
            behind, ahead = index - sign, index + sign
            comes = (behind >= 0) & (behind < size) & (sign * (chunk - index) >= 0)
            goes = sign * (chunk - index) > 0
            lane = 0 if sign == 1 else 1
            ordinal = step
            if (sign == 1 and chunk == 0) or (sign == -1 and chunk == size - 1):
                continue
            channel = taken[ordinal][lane]
            inbox = slots.at[chunk] if sign == 1 else slots.at[size + chunk]
            to = position.device(**{axis: ahead})
            relay = remote(inbox, inbox, channel, to)
            first = remote(local(chunk), inbox, channel, to)
            starts = goes & ((behind < 0) | (behind >= size))

            @pl.when(comes)
            def _():
                remote(inbox, inbox, channel, position.device(**{axis: behind})).wait_recv()

            @pl.when(comes & goes)
            def _():
                add_rows(inbox, inbox, local(chunk))
                relay.start()

            @pl.when(starts)
            def _():
                first.start()

            sent.append((comes & goes, relay))
            sent.append((starts, first))
        yield
    low, high = slots.at[index], slots.at[size + index]

    @pl.when((index > 0) & (index < size - 1))
    def _():
        add_rows(low, low, high)

    @pl.when(index > 0)
    def _():
        add_rows(result, low, local(index))

    @pl.when(index == 0)
    def _():
        add_rows(result, high, local(index))


def reduce_flow(position, channels, local_sem, grads, result, buffers, order):
    loc, first, mid, last, line_slots = buffers
    sent = []
    mine = position.core
    own = pltpu.make_async_copy(grads(mine), loc, local_sem)
    own.start()
    channel = channels.take()
    copy = remote(grads(1 - mine), first, channel, position.device(core=1 - mine))
    copy.start()
    sent.append((None, copy))
    yield
    own.wait()
    copy.wait_recv()
    add_rows(first, first, loc)
    width = result.shape[-1]

    def columns(j):
        return pl.ds(pl.multiple_of(j * width, 128), width)

    if order == "A":
        yield from reduce_axis(
            position, "column", channels, lambda j: first.at[:, :, :, columns(j)], mid, mid_result(mid), sent
        )
        held = mid_result(mid)
        yield from reduce_axis(
            position, "pair", channels, lambda j: held.at[:, j], last, mid_result(last), sent
        )
    else:
        yield from reduce_axis(
            position, "pair", channels, lambda j: first.at[:, j], mid, mid_result(mid), sent
        )
        held = mid_result(mid)
        yield from reduce_axis(
            position, "column", channels, lambda j: held.at[:, :, columns(j)], last, mid_result(last), sent
        )
    final = mid_result(last)
    yield from reduce_axis(
        position, "line", channels, lambda j: final.at[pl.ds(j, 1)], line_slots, result, sent
    )
    finish_sends(sent)


def mid_result(slots):
    return slots.at[slots.shape[0] - 1]


def stage_slots(size):
    return (1 if size == 2 else 2 * size) + 1


def double_flow(position, channels, terms_ref, total, inbox, result):
    total[0] = terms_ref[...]
    step = 0
    for axis in ("core", "pair", "line", "column"):
        size, index = position.sizes[axis], position.get(axis)
        bit = 1
        while bit < size:
            channel = channels.take()
            copy = remote(
                total.at[step], inbox.at[step], channel, position.device(**{axis: flip(index, bit)})
            )
            copy.start()
            yield
            copy.wait_recv()
            total[step + 1] = total[step] + inbox[step]
            copy.wait_send()
            bit *= 2
            step += 1
    result[...] = total[step]


def reduce_kernel(wide, narrow, groups, doubling, *refs):
    grads_ref = refs[0]
    if doubling:
        terms_ref, result_ref, terms_out = refs[1:4]
        sends, recvs, local_sems, total, inbox = refs[4:9]
        buffers = refs[9:]
    else:
        result_ref, sends, recvs, local_sems = refs[1:5]
        buffers = refs[5:]
    position = Position(wide, narrow)
    channels = Channels(sends, recvs)
    greet(position, doubling)
    flows = []
    for number, (matrix, part, rows, order) in enumerate(groups):

        def grads(core, matrix=matrix, part=part, rows=rows):
            return grads_ref.at[matrix, :, :, core, pl.ds(part * rows, rows)]

        result = result_ref.at[pl.ds(matrix, 1), pl.ds(part * rows, rows)]
        flows.append(
            reduce_flow(
                position,
                channels,
                local_sems.at[number],
                grads,
                result,
                buffers[number * 5 : number * 5 + 5],
                order,
            )
        )
    extra = [double_flow(position, channels, terms_ref, total, inbox, terms_out)] if doubling else []
    run_rounds(flows, extra)


def reduce_gradients(wide, narrow, grads, collective_id, terms=None):
    matrices, depth, span = grads.shape
    rows, width = depth // wide, span // narrow
    line = wide // 4
    parts = row_splits(rows, 4) if matrices == 2 else 1
    piece = rows // parts
    groups = [
        (matrix, part, piece, "A" if matrix % 2 == 0 else "B")
        for part in range(parts)
        for matrix in range(matrices)
    ]
    view = grads.reshape(matrices, line, 2, 2, rows, span)
    copies = gather_channels(wide, narrow) * len(groups) + 16
    low = jnp.bfloat16
    scratch = [
        pltpu.SemaphoreType.DMA((copies,)),
        pltpu.SemaphoreType.DMA((copies,)),
        pltpu.SemaphoreType.DMA((len(groups),)),
    ]
    outs = [jax.ShapeDtypeStruct((matrices, rows, width), jnp.float32)]
    operands = [view]
    in_specs = [pl.BlockSpec(memory_space=pl.ANY)]
    if terms is not None:
        steps = (wide * narrow).bit_length() - 1
        scratch.append(pltpu.VMEM((steps + 1,) + terms.shape, jnp.float32))
        scratch.append(pltpu.VMEM((steps,) + terms.shape, jnp.float32))
        outs.append(jax.ShapeDtypeStruct(terms.shape, jnp.float32))
        operands.append(terms)
        in_specs.append(pl.BlockSpec(memory_space=pltpu.VMEM))
    for matrix, part, piece, order in groups:
        scratch.append(pltpu.VMEM((line, 2, piece, span), low))
        scratch.append(pltpu.VMEM((line, 2, piece, span), low))
        if order == "A":
            scratch.append(pltpu.VMEM((stage_slots(narrow), line, 2, piece, width), low))
            scratch.append(pltpu.VMEM((stage_slots(2), line, piece, width), low))
        else:
            scratch.append(pltpu.VMEM((stage_slots(2), line, piece, span), low))
            scratch.append(pltpu.VMEM((stage_slots(narrow), line, piece, width), low))
        scratch.append(pltpu.VMEM((stage_slots(line), 1, piece, width), low))
    return pl.pallas_call(
        functools.partial(reduce_kernel, wide, narrow, groups, terms is not None),
        out_shape=outs,
        in_specs=in_specs,
        out_specs=[pl.BlockSpec(memory_space=pltpu.VMEM)] * len(outs),
        scratch_shapes=scratch,
        compiler_params=pltpu.CompilerParams(
            collective_id=collective_id, has_side_effects=True, vmem_limit_bytes=60000 * 1024
        ),
        name="reduce_gradients",
    )(*operands)


def stack_low(grads):
    return jnp.stack([grad.astype(jnp.bfloat16) for grad in grads])


def heads_of(rows, count):
    return rows.reshape(count, -1, HEADS, HEAD_DIM)


def score_block(query_rows, key_matrix_rows, allowed):
    score_matrix = jnp.einsum(
        "blhd,bmhd->bhlm", query_rows, key_matrix_rows, preferred_element_type=jnp.float32
    )
    return jnp.where(allowed[:, None], score_matrix, NEGATIVE)


def attend(query_rows, key_matrix_rows, value_matrix_rows, allowed):
    score_matrix = score_block(query_rows, key_matrix_rows, allowed)
    peak = jnp.max(score_matrix, axis=-1, keepdims=True)
    expo = jnp.exp(score_matrix - peak)
    totals = jnp.sum(expo, axis=-1, keepdims=True)
    weights_low = (expo / totals).astype(jnp.bfloat16)
    mixed = jnp.einsum(
        "bhlm,bmhd->blhd", weights_low, value_matrix_rows, preferred_element_type=jnp.float32
    )
    return (mixed.astype(jnp.bfloat16), peak + jnp.log(totals))


def attend_back(query_rows, key_matrix_rows, value_matrix_rows, allowed, log_total, grad_mixed):
    score_matrix = score_block(query_rows, key_matrix_rows, allowed)
    probs = jnp.exp(score_matrix - log_total)
    grad_probs = jnp.einsum(
        "blhd,bmhd->bhlm", grad_mixed, value_matrix_rows, preferred_element_type=jnp.float32
    )
    grad_scores = (
        probs * (grad_probs - jnp.sum(grad_probs * probs, axis=-1, keepdims=True))
    ).astype(jnp.bfloat16)
    grad_queries = jnp.einsum(
        "bhlm,bmhd->blhd", grad_scores, key_matrix_rows, preferred_element_type=jnp.float32
    )
    grad_keys = jnp.einsum(
        "bhlm,blhd->bmhd", grad_scores, query_rows, preferred_element_type=jnp.float32
    )
    grad_values = jnp.einsum(
        "bhlm,blhd->bmhd",
        probs.astype(jnp.bfloat16),
        grad_mixed,
        preferred_element_type=jnp.float32,
    )
    return (
        grad_queries.astype(jnp.bfloat16),
        grad_keys.astype(jnp.bfloat16),
        grad_values.astype(jnp.bfloat16),
    )


def per_sequence(function, operands):

    def single_entry(items):
        results = function(*[item[None] for item in items])
        return tuple((result[0] for result in results))

    return lax.map(single_entry, operands)


def per_device(
    wide,
    narrow,
    decoder_input,
    memory,
    decoder_mask,
    memory_length,
    self_weights,
    cross_weights,
    feed_weights,
    vectors,
    hidden_bias,
    cotangent,
):
    seq_count, seq_length, model_width = decoder_input.shape
    mem_span = memory.shape[1]
    token_rows = seq_count * seq_length
    scale = HEAD_DIM ** (-0.5)
    (self_full, cross_full, feed_full), vector_all, bias_all = gather_weights(
        wide, narrow, (self_weights, cross_weights, feed_weights), vectors, hidden_bias, 1
    )
    input_low = decoder_input.reshape(token_rows, model_width)
    input_full = input_low.astype(jnp.float32)
    memory_low = memory.reshape(seq_count * mem_span, model_width)
    positions = jnp.arange(seq_length)
    causal = positions[:, None] >= positions[None, :]
    self_allowed = causal[None] & (decoder_mask[:, None, :] == 1)
    cross_allowed = (jnp.arange(mem_span)[None, :] < memory_length[:, None])[:, None, :]
    self_query = heads_of(
        ((linear(input_low, self_full[0]) + vector_all[0]) * scale).astype(jnp.bfloat16), seq_count
    )
    self_keys = heads_of(linear(input_low, self_full[1]).astype(jnp.bfloat16), seq_count)
    self_values = heads_of(
        (linear(input_low, self_full[2]) + vector_all[1]).astype(jnp.bfloat16), seq_count
    )
    self_mixed, self_log = attend(self_query, self_keys, self_values, self_allowed)
    self_mixed = self_mixed.reshape(token_rows, model_width)
    first_sum = input_full + (linear(self_mixed, self_full[3]) + vector_all[2])
    first_out = layer_norm(first_sum, vector_all[3], vector_all[4])
    first_low = first_out.astype(jnp.bfloat16)
    cross_query = heads_of(
        ((linear(first_low, cross_full[0]) + vector_all[5]) * scale).astype(jnp.bfloat16), seq_count
    )
    cross_keys = heads_of(linear(memory_low, cross_full[1]).astype(jnp.bfloat16), seq_count)
    cross_values = heads_of(
        (linear(memory_low, cross_full[2]) + vector_all[6]).astype(jnp.bfloat16), seq_count
    )
    cross_mixed, cross_log = per_sequence(
        attend, (cross_query, cross_keys, cross_values, cross_allowed)
    )
    cross_mixed = cross_mixed.reshape(token_rows, model_width)
    second_sum = first_out + (linear(cross_mixed, cross_full[3]) + vector_all[7])
    second_out = layer_norm(second_sum, vector_all[8], vector_all[9])
    second_low = second_out.astype(jnp.bfloat16)
    inner = linear(second_low, feed_full[0]) + bias_all[0]
    hidden_low = gelu_exact(inner).astype(jnp.bfloat16)
    third_sum = second_out + (linear_tr(hidden_low, feed_full[1]) + vector_all[10])
    output = layer_norm(third_sum, vector_all[11], vector_all[12])
    layer_output = output.astype(jnp.bfloat16).reshape(seq_count, seq_length, model_width)
    grad_output = cotangent.reshape(token_rows, model_width).astype(jnp.float32)
    unused_three, pull_three = jax.vjp(layer_norm, third_sum, vector_all[11], vector_all[12])
    grad_third, gain_three, shift_three = pull_three(grad_output)
    feed_back = feed_full
    grad_branch = grad_third.astype(jnp.bfloat16)
    grad_hidden = linear(grad_branch, feed_back[1])
    unused_gelu, pull_gelu = jax.vjp(gelu_exact, inner)
    grad_inner = pull_gelu(grad_hidden)[0].astype(jnp.bfloat16)
    grad_second = grad_third + linear_tr(grad_inner, feed_back[0])
    (feed_grad,) = reduce_gradients(
        wide,
        narrow,
        stack_low([outer_sum(second_low, grad_inner), outer_sum(grad_branch, hidden_low)]),
        2,
    )
    unused_two, pull_two = jax.vjp(layer_norm, second_sum, vector_all[8], vector_all[9])
    grad_second, gain_two, shift_two = pull_two(grad_second)
    cross_back = cross_full
    grad_cross = grad_second.astype(jnp.bfloat16)
    grad_cmixed = heads_of(linear_tr(grad_cross, cross_back[3]).astype(jnp.bfloat16), seq_count)
    cross_gq, cross_gk, cross_gv = per_sequence(
        attend_back, (cross_query, cross_keys, cross_values, cross_allowed, cross_log, grad_cmixed)
    )
    cross_gq = cross_gq.reshape(token_rows, model_width)
    cross_gk = cross_gk.reshape(seq_count * mem_span, model_width)
    cross_gv = cross_gv.reshape(seq_count * mem_span, model_width)
    grad_first = grad_second + linear_tr(cross_gq, cross_back[0]) * scale
    memory_grad = linear_tr(cross_gk, cross_back[1]) + linear_tr(cross_gv, cross_back[2])
    (cross_grad,) = reduce_gradients(
        wide,
        narrow,
        stack_low(
            [
                outer_sum(first_low, cross_gq) * scale,
                outer_sum(memory_low, cross_gk),
                outer_sum(memory_low, cross_gv),
                outer_sum(cross_mixed, grad_cross),
            ]
        ),
        3,
    )
    unused_one, pull_one = jax.vjp(layer_norm, first_sum, vector_all[3], vector_all[4])
    grad_first, gain_one, shift_one = pull_one(grad_first)
    self_back = self_full
    grad_self = grad_first.astype(jnp.bfloat16)
    grad_smixed = heads_of(linear_tr(grad_self, self_back[3]).astype(jnp.bfloat16), seq_count)
    self_gq, self_gk, self_gv = attend_back(
        self_query, self_keys, self_values, self_allowed, self_log, grad_smixed
    )
    self_gq = self_gq.reshape(token_rows, model_width)
    self_gk = self_gk.reshape(token_rows, model_width)
    self_gv = self_gv.reshape(token_rows, model_width)
    input_grad = (
        grad_first
        + linear_tr(self_gq, self_back[0]) * scale
        + linear_tr(self_gk, self_back[1])
        + linear_tr(self_gv, self_back[2])
    )
    vector_terms = jnp.stack(
        [
            column_sum(self_gq) * scale,
            column_sum(self_gv),
            column_sum(grad_self),
            gain_one,
            shift_one,
            column_sum(cross_gq) * scale,
            column_sum(cross_gv),
            column_sum(grad_cross),
            gain_two,
            shift_two,
            column_sum(grad_branch),
            gain_three,
            shift_three,
        ]
    )
    bias_term = column_sum(grad_inner)[None]
    terms = jnp.concatenate([vector_terms, bias_term.reshape(-1, model_width)], axis=0)
    count = terms.shape[0]
    terms = jnp.pad(terms, ((0, -count % 8), (0, 0)))
    self_weight_gradient, totals = reduce_gradients(
        wide,
        narrow,
        stack_low(
            [
                outer_sum(input_low, self_gq) * scale,
                outer_sum(input_low, self_gk),
                outer_sum(input_low, self_gv),
                outer_sum(self_mixed, grad_self),
            ]
        ),
        4,
        terms,
    )
    vector_total = totals[: vectors.shape[0]]
    bias_total = totals[vectors.shape[0] : count].reshape(1, -1)
    vector_part = vectors.shape[1]
    bias_part = hidden_bias.shape[1]
    narrow_index = lax.axis_index("narrow")
    vectors_grad = lax.dynamic_slice_in_dim(
        vector_total, narrow_index * vector_part, vector_part, 1
    )
    hidden_bias_grad = lax.dynamic_slice_in_dim(bias_total, narrow_index * bias_part, bias_part, 1)
    return (
        layer_output,
        input_grad.reshape(seq_count, seq_length, model_width),
        memory_grad.reshape(seq_count, mem_span, model_width),
        self_weight_gradient,
        cross_grad,
        feed_grad,
        vectors_grad,
        hidden_bias_grad,
    )


def solution(mesh):
    placed = (
        P(("wide", "narrow"), None, None),
        P(("wide", "narrow"), None, None),
        P(("wide", "narrow"), None),
        P(("wide", "narrow")),
        P(None, "wide", "narrow"),
        P(None, "wide", "narrow"),
        P(None, "wide", "narrow"),
        P(None, "narrow"),
        P(None, "narrow"),
        P(("wide", "narrow"), None, None),
    )
    return jax.shard_map(
        functools.partial(per_device, mesh.shape["wide"], mesh.shape["narrow"]),
        mesh=mesh,
        in_specs=placed,
        out_specs=(
            P(("wide", "narrow"), None, None),
            P(("wide", "narrow"), None, None),
            P(("wide", "narrow"), None, None),
            P(None, "wide", "narrow"),
            P(None, "wide", "narrow"),
            P(None, "wide", "narrow"),
            P(None, "narrow"),
            P(None, "narrow"),
        ),
        check_vma=False,
    )
```

```python
import functools
import math

import jax
import jax.numpy as jnp
from jax import lax
from jax.experimental import pallas as pl
from jax.experimental.pallas import tpu as pltpu
from jax.sharding import PartitionSpec as P

HEADS = 16
HEAD_DIM = 64


MESH_ID = pl.DeviceIdType.MESH


class Position:
    def __init__(self, wide, narrow):
        index = lax.axis_index("wide")
        self.core = index % 2
        self.pair = (index // 2) % 2
        self.line = index // 4
        self.column = lax.axis_index("narrow")
        self.sizes = {"line": wide // 4, "pair": 2, "core": 2, "column": narrow}

    def get(self, axis):
        return getattr(self, axis)

    def device(self, **moved):
        spot = {name: moved.get(name, self.get(name)) for name in self.sizes}
        return (spot["line"] * 4 + spot["pair"] * 2 + spot["core"], spot["column"])


class Channels:
    def __init__(self, sends, recvs):
        self.sends, self.recvs, self.used = sends, recvs, 0

    def take(self):
        self.used += 1
        return self.sends.at[self.used - 1], self.recvs.at[self.used - 1]


def remote(source, target, channel, device):
    return pltpu.make_async_remote_copy(
        src_ref=source,
        dst_ref=target,
        send_sem=channel[0],
        recv_sem=channel[1],
        device_id=device,
        device_id_type=MESH_ID,
    )


def greet(position, doubling=False):
    barrier = pltpu.get_barrier_semaphore()

    def signal(device):
        pl.semaphore_signal(barrier, inc=1, device_id=device, device_id_type=MESH_ID)

    expected = 2
    signal(position.device(core=1 - position.core))
    signal(position.device(pair=1 - position.pair))
    for axis in ("line", "column"):
        size, index = position.sizes[axis], position.get(axis)
        if size == 2:
            signal(position.device(**{axis: 1 - index}))
            expected = expected + 1
        elif size > 2:

            @pl.when(index > 0)
            def _():
                signal(position.device(**{axis: index - 1}))

            @pl.when(index < size - 1)
            def _():
                signal(position.device(**{axis: index + 1}))

            expected = expected + jnp.where(index > 0, 1, 0) + jnp.where(index < size - 1, 1, 0)
        if doubling and size > 2:
            bit = 1
            while bit < size:
                signal(position.device(**{axis: flip(index, bit)}))
                expected = expected + 1
                bit *= 2
    pl.semaphore_wait(barrier, expected)


def flip(index, bit):
    return index + bit - 2 * bit * ((index // bit) % 2)


def advance(generator):
    return next(generator, "done") != "done"


def run_rounds(flows, live=()):
    waiting, live = list(flows), list(live)
    while waiting or live:
        live = live + waiting[:2]
        waiting = waiting[2:]
        live = [flow for flow in live if advance(flow)]


def gather_axis(position, axis, channels, block, own, sent):
    size, index = position.sizes[axis], position.get(axis)
    if size == 2:
        channel = channels.take()
        other = position.device(**{axis: 1 - index})
        copy = remote(own, block(index), channel, other)
        copy.start()
        sent.append((None, copy))
        yield
        remote(own, block(1 - index), channel, other).wait_recv()
        return
    for step in range(1, size):
        for sign in (1, -1):
            channel = channels.take()
            held = index - sign * (step - 1)
            target = index + sign
            active = (held >= 0) & (held < size) & (target >= 0) & (target < size)
            device = position.device(**{axis: target})
            source = own if step == 1 else block(held)
            copy = remote(source, block(held), channel, device)

            @pl.when(active)
            def _():
                copy.start()

            sent.append((active, copy))
        pairs = channels.used
        yield
        for place, sign in ((pairs - 2, 1), (pairs - 1, -1)):
            came = index - sign * step
            channel = (channels.sends.at[place], channels.recvs.at[place])
            device = position.device(**{axis: index - sign})

            @pl.when((came >= 0) & (came < size))
            def _():
                remote(own, block(came), channel, device).wait_recv()


def finish_sends(sent):
    for active, copy in sent:
        if active is None:
            copy.wait_send()
        else:

            @pl.when(active)
            def _():
                copy.wait_send()


def gather_flow(position, channels, local_sem, own, region, order):
    sent = []
    spot = {axis: position.get(axis) for axis in position.sizes}
    local = pltpu.make_async_copy(own, region(**spot), local_sem)
    local.start()
    for place, axis in enumerate(order):

        def block(j, axis=axis):
            return region(**{**spot, axis: j})

        source = own if place == 0 else block(position.get(axis))
        yield from gather_axis(position, axis, channels, block, source, sent)
        if place == 0:
            local.wait()
        spot[axis] = None
    finish_sends(sent)


def whole(index):
    return slice(None) if index is None else index


def row_splits(rows, most):
    return max(1, min(most, rows // 16))


def gather_channels(wide, narrow):
    line = wide // 4
    count = 2
    count += 1 if line == 2 else 2 * (line - 1)
    count += 1 if narrow == 2 else 2 * (narrow - 1)
    return count


def gather_kernel(wide, narrow, groups, counts, *refs):
    blocks, (vector_ref, bias_ref) = refs[:counts], refs[counts : counts + 2]
    fulls = refs[counts + 2 : 2 * counts + 2]
    vector_out, bias_out, sends, recvs, local_sems = refs[2 * counts + 2 :]
    position = Position(wide, narrow)
    channels = Channels(sends, recvs)
    greet(position)
    flows = []

    def column_flow(block_ref, full_ref, sem):
        def region(column, **ignored):
            return full_ref.at[column]

        sent = []
        local = pltpu.make_async_copy(block_ref, region(position.column), sem)
        local.start()
        yield from gather_axis(position, "column", channels, region, block_ref, sent)
        local.wait()
        finish_sends(sent)

    flows.append(column_flow(vector_ref, vector_out, local_sems.at[0]))
    flows.append(column_flow(bias_ref, bias_out, local_sems.at[1]))
    for number, (array, matrix, part, parts, order) in enumerate(groups):
        block_ref, full_ref = blocks[array], fulls[array]
        rows = block_ref.shape[1] // parts
        width = block_ref.shape[2]

        def region(
            line, pair, core, column, full_ref=full_ref, matrix=matrix, part=part, rows=rows, width=width
        ):
            columns = (
                slice(None)
                if column is None
                else pl.ds(pl.multiple_of(column * width, 128), width)
            )
            return full_ref.at[
                matrix, whole(line), whole(pair), whole(core), pl.ds(part * rows, rows), columns
            ]

        own = block_ref.at[matrix, pl.ds(part * rows, rows)]
        flows.append(
            gather_flow(position, channels, local_sems.at[number + 2], own, region, order)
        )
    run_rounds(flows)


ORDER_A = ("line", "pair", "column", "core")
ORDER_B = ("line", "column", "pair", "core")


def gather_weights(wide, narrow, arrays, vectors, hidden_bias, collective_id):
    groups = []
    for number, array in enumerate(arrays):
        matrices, rows, width = array.shape
        parts = row_splits(rows, 4) if matrices == 2 else 1
        for part in range(parts):
            for matrix in range(matrices):
                groups.append(
                    (number, matrix, part, parts, ORDER_A if matrix % 2 == 0 else ORDER_B)
                )
    copies = gather_channels(wide, narrow) * (len(groups) + 2)
    outs = [
        jax.ShapeDtypeStruct(
            (array.shape[0], wide // 4, 2, 2, array.shape[1], array.shape[2] * narrow), array.dtype
        )
        for array in arrays
    ]
    outs.append(jax.ShapeDtypeStruct((narrow,) + vectors.shape, vectors.dtype))
    outs.append(jax.ShapeDtypeStruct((narrow,) + hidden_bias.shape, hidden_bias.dtype))
    results = pl.pallas_call(
        functools.partial(gather_kernel, wide, narrow, groups, len(arrays)),
        out_shape=outs,
        in_specs=[pl.BlockSpec(memory_space=pltpu.VMEM)] * (len(arrays) + 2),
        out_specs=[pl.BlockSpec(memory_space=pl.ANY)] * len(outs),
        scratch_shapes=[
            pltpu.SemaphoreType.DMA((copies,)),
            pltpu.SemaphoreType.DMA((copies,)),
            pltpu.SemaphoreType.DMA((len(groups) + 2,)),
        ],
        compiler_params=pltpu.CompilerParams(collective_id=collective_id, has_side_effects=True),
        name="gather_weights",
    )(*arrays, vectors, hidden_bias)
    fulls = [
        full.reshape(full.shape[0], -1, full.shape[-1]) for full in results[: len(arrays)]
    ]
    vector_all = jnp.moveaxis(results[-2], 0, 1).reshape(vectors.shape[0], -1)
    bias_all = jnp.moveaxis(results[-1], 0, 1).reshape(1, -1)
    return fulls, vector_all, bias_all


def add_rows(target, first, second):
    lead = target.shape[:-2]
    count = math.prod(lead)

    def place(k):
        where = []
        for extent in reversed(lead):
            where.insert(0, k % extent)
            k = k // extent
        return tuple(where)

    if count == 1:
        spot = (0,) * len(lead)
        target[spot] = (
            first[spot].astype(jnp.float32) + second[spot].astype(jnp.float32)
        ).astype(target.dtype)
        return

    @pl.loop(0, count)
    def _(k):
        spot = place(k)
        target[spot] = (
            first[spot].astype(jnp.float32) + second[spot].astype(jnp.float32)
        ).astype(target.dtype)


def reduce_axis(position, axis, channels, local, slots, result, sent):
    size, index = position.sizes[axis], position.get(axis)
    if size == 2:
        channel = channels.take()
        other = position.device(**{axis: 1 - index})
        copy = remote(local(1 - index), slots.at[0], channel, other)
        copy.start()
        sent.append((None, copy))
        yield
        copy.wait_recv()
        add_rows(result, slots.at[0], local(index))
        return
    moves = []
    for step in range(size - 1):
        for sign in (1, -1):
            chunk = size - 1 - step if sign == 1 else step
            inbox = slots.at[chunk] if sign == 1 else slots.at[size + chunk]
            behind, to = index - sign, position.device(**{axis: index + sign})
            comes = (behind >= 0) & (behind < size) & (sign * (chunk - index) >= 0)
            goes = sign * (chunk - index) > 0
            starts = goes & ((behind < 0) | (behind >= size))
            channel = channels.take()
            first = remote(local(chunk), inbox, channel, to)

            @pl.when(starts)
            def _():
                first.start()

            moves.append((chunk, inbox, channel, to, comes, goes))
            sent.append((starts, first))
    yield
    for number, (chunk, inbox, channel, to, comes, goes) in enumerate(moves):
        relay = remote(inbox, inbox, channel, to)

        @pl.when(comes & goes)
        def _():
            relay.wait_recv()
            add_rows(inbox, inbox, local(chunk))
            relay.start()

        sent.append((comes & goes, relay))
        if number % 2:
            yield
    for chunk, inbox, channel, to, comes, goes in moves:

        @pl.when(comes & jnp.logical_not(goes))
        def _():
            remote(inbox, inbox, channel, to).wait_recv()

    low, high = slots.at[index], slots.at[size + index]

    @pl.when((index > 0) & (index < size - 1))
    def _():
        add_rows(low, low, high)

    @pl.when(index > 0)
    def _():
        add_rows(result, low, local(index))

    @pl.when(index == 0)
    def _():
        add_rows(result, high, local(index))


def reduce_flow(position, channels, local_sem, grads, result, buffers, order):
    loc, first, mid, last, line_slots = buffers
    sent = []
    mine = position.core
    own = pltpu.make_async_copy(grads(mine), loc, local_sem)
    own.start()
    channel = channels.take()
    copy = remote(grads(1 - mine), first, channel, position.device(core=1 - mine))
    copy.start()
    sent.append((None, copy))
    yield
    own.wait()
    copy.wait_recv()
    add_rows(first, first, loc)
    width = result.shape[-1]

    def columns(j):
        return pl.ds(pl.multiple_of(j * width, 128), width)

    if order == "A":
        yield from reduce_axis(
            position, "column", channels, lambda j: first.at[:, :, :, columns(j)], mid, mid_result(mid), sent
        )
        held = mid_result(mid)
        yield from reduce_axis(
            position, "pair", channels, lambda j: held.at[:, j], last, mid_result(last), sent
        )
    else:
        yield from reduce_axis(
            position, "pair", channels, lambda j: first.at[:, j], mid, mid_result(mid), sent
        )
        held = mid_result(mid)
        yield from reduce_axis(
            position, "column", channels, lambda j: held.at[:, :, columns(j)], last, mid_result(last), sent
        )
    final = mid_result(last)
    yield from reduce_axis(
        position, "line", channels, lambda j: final.at[pl.ds(j, 1)], line_slots, result, sent
    )
    finish_sends(sent)


def mid_result(slots):
    return slots.at[slots.shape[0] - 1]


def stage_slots(size):
    return (1 if size == 2 else 2 * size) + 1


def double_flow(position, channels, terms_ref, total, inbox, result):
    total[0] = terms_ref[...]
    step = 0
    for axis in ("core", "pair", "line", "column"):
        size, index = position.sizes[axis], position.get(axis)
        bit = 1
        while bit < size:
            channel = channels.take()
            copy = remote(
                total.at[step], inbox.at[step], channel, position.device(**{axis: flip(index, bit)})
            )
            copy.start()
            yield
            copy.wait_recv()
            total[step + 1] = total[step] + inbox[step]
            copy.wait_send()
            bit *= 2
            step += 1
    result[...] = total[step]


def reduce_kernel(wide, narrow, groups, counts, doubling, *refs):
    sources, refs = refs[:counts], refs[counts - 1 :]
    if doubling:
        terms_ref, result_ref, terms_out = refs[1:4]
        sends, recvs, local_sems, total, inbox = refs[4:9]
        buffers = refs[9:]
    else:
        result_ref, sends, recvs, local_sems = refs[1:5]
        buffers = refs[5:]
    position = Position(wide, narrow)
    channels = Channels(sends, recvs)
    greet(position, doubling)
    flows = []
    for number, (matrix, source, inner, part, rows, order) in enumerate(groups):

        def grads(core, source=source, inner=inner, part=part, rows=rows):
            return sources[source].at[inner, :, :, core, pl.ds(part * rows, rows)]

        result = result_ref.at[pl.ds(matrix, 1), pl.ds(part * rows, rows)]
        flows.append(
            reduce_flow(
                position,
                channels,
                local_sems.at[number],
                grads,
                result,
                buffers[number * 5 : number * 5 + 5],
                order,
            )
        )
    extra = [double_flow(position, channels, terms_ref, total, inbox, terms_out)] if doubling else []
    run_rounds(flows, extra)


def reduce_gradients(wide, narrow, grads, collective_id, terms=None):
    matrices = sum(grad.shape[0] for grad in grads)
    depth, span = grads[0].shape[1:]
    where = [(source, inner) for source, grad in enumerate(grads) for inner in range(grad.shape[0])]
    rows, width = depth // wide, span // narrow
    line = wide // 4
    parts = row_splits(rows, 4) if matrices == 2 else 1
    piece = rows // parts
    groups = [
        (matrix,) + where[matrix] + (part, piece, "A" if matrix % 2 == 0 else "B")
        for part in range(parts)
        for matrix in range(matrices)
    ]
    views = [grad.reshape(grad.shape[0], line, 2, 2, rows, span) for grad in grads]
    copies = gather_channels(wide, narrow) * len(groups) + 16
    low = jnp.bfloat16
    scratch = [
        pltpu.SemaphoreType.DMA((copies,)),
        pltpu.SemaphoreType.DMA((copies,)),
        pltpu.SemaphoreType.DMA((len(groups),)),
    ]
    outs = [jax.ShapeDtypeStruct((matrices, rows, width), jnp.float32)]
    operands = views
    in_specs = [pl.BlockSpec(memory_space=pl.ANY)] * len(views)
    if terms is not None:
        steps = (wide * narrow).bit_length() - 1
        scratch.append(pltpu.VMEM((steps + 1,) + terms.shape, jnp.float32))
        scratch.append(pltpu.VMEM((steps,) + terms.shape, jnp.float32))
        outs.append(jax.ShapeDtypeStruct(terms.shape, jnp.float32))
        operands.append(terms)
        in_specs.append(pl.BlockSpec(memory_space=pltpu.VMEM))
    for *_, order in groups:
        scratch.append(pltpu.VMEM((line, 2, piece, span), low))
        scratch.append(pltpu.VMEM((line, 2, piece, span), low))
        if order == "A":
            scratch.append(pltpu.VMEM((stage_slots(narrow), line, 2, piece, width), low))
            scratch.append(pltpu.VMEM((stage_slots(2), line, piece, width), low))
        else:
            scratch.append(pltpu.VMEM((stage_slots(2), line, piece, span), low))
            scratch.append(pltpu.VMEM((stage_slots(narrow), line, piece, width), low))
        scratch.append(pltpu.VMEM((stage_slots(line), 1, piece, width), low))
    return pl.pallas_call(
        functools.partial(reduce_kernel, wide, narrow, groups, len(grads), terms is not None),
        out_shape=outs,
        in_specs=in_specs,
        out_specs=[pl.BlockSpec(memory_space=pltpu.VMEM)] * len(outs),
        scratch_shapes=scratch,
        compiler_params=pltpu.CompilerParams(
            collective_id=collective_id, has_side_effects=True, vmem_limit_bytes=60000 * 1024
        ),
        name="reduce_gradients",
    )(*operands)


LOW = jnp.bfloat16
NEGATIVE = -1000000000.0
EPSILON = 1e-05
PAIR = 2 * HEAD_DIM
SCALE = HEAD_DIM ** (-0.5)
BUDGET = 60000 * 1024


def dot_nn(left, right):
    return jnp.dot(left, right, preferred_element_type=jnp.float32)


def dot_nt(left, right):
    return lax.dot_general(
        left, right, (((1,), (1,)), ((), ())), preferred_element_type=jnp.float32
    )


def dot_tn(left, right):
    return lax.dot_general(
        left, right, (((0,), (0,)), ((), ())), preferred_element_type=jnp.float32
    )


def padded(length):
    return -(-length // 16) * 16


def column_sum(rows):
    return jnp.sum(rows.astype(jnp.float32), axis=0, keepdims=True)


def standardise(hidden):
    centre = hidden - jnp.mean(hidden, axis=-1, keepdims=True)
    spread = jnp.mean(centre * centre, axis=-1, keepdims=True)
    inverse = lax.rsqrt(spread + EPSILON)
    return centre * inverse, inverse


def norm_back(grad, unit, inverse, gain):
    scaled = grad * gain
    first = jnp.mean(scaled, axis=-1, keepdims=True)
    second = jnp.mean(scaled * unit, axis=-1, keepdims=True)
    return inverse * (scaled - first - unit * second)


def fill_tokens(target, source):
    count, length, span = source.shape
    rows = padded(length)
    for s in range(count):
        if rows > length:
            base = s * rows + length // 16 * 16
            target[base : (s + 1) * rows] = jnp.zeros(((s + 1) * rows - base, span), target.dtype)
        target[s * rows : s * rows + length] = source[s].astype(target.dtype)


def store_tokens(target, values):
    count, length, span = target.shape
    rows = padded(length)
    for s in range(count):
        target[s] = values[s * rows : s * rows + length].astype(target.dtype)


def head_lanes(rows, which):
    lane = lax.broadcasted_iota(jnp.int32, rows.shape, 1)
    return (lane >= HEAD_DIM) == (which == 1)


def one_head(rows, which):
    return jnp.where(head_lanes(rows, which), rows, jnp.zeros_like(rows))


def pick_column(table, number):
    lane = lax.broadcasted_iota(jnp.int32, table.shape, 1)
    return jnp.sum(jnp.where(lane == number, table, 0.0), axis=1, keepdims=True)


def attend_pair(query, keys, values, allowed):
    mixed, logs = [], []
    for which in range(2):
        scores = dot_nt(one_head(query, which), keys)
        scores = jnp.where(allowed, scores, NEGATIVE)
        peak = jnp.max(scores, axis=-1, keepdims=True)
        expo = jnp.exp(scores - peak)
        total = jnp.sum(expo, axis=-1, keepdims=True)
        weights = (expo * (1.0 / total)).astype(LOW)
        mixed.append(dot_nn(weights, values))
        logs.append(peak + jnp.log(total))
    both = jnp.where(head_lanes(mixed[0], 0), mixed[0], mixed[1])
    return both.astype(LOW), logs


def attend_pair_back(query, keys, values, allowed, logs, grad):
    grad_query, grad_keys, grad_values = [], None, None
    for which in range(2):
        query_one, grad_one = one_head(query, which), one_head(grad, which)
        scores = jnp.where(allowed, dot_nt(query_one, keys), NEGATIVE)
        probs = jnp.exp(scores - logs[which])
        grad_probs = dot_nt(grad_one, values)
        slope = jnp.sum(grad_probs * probs, axis=-1, keepdims=True)
        grad_scores = (probs * (grad_probs - slope)).astype(LOW)
        grad_query.append(dot_nn(grad_scores, keys))
        part_keys = dot_tn(grad_scores, query_one)
        part_values = dot_tn(probs.astype(LOW), grad_one)
        grad_keys = part_keys if which == 0 else grad_keys + part_keys
        grad_values = part_values if which == 0 else grad_values + part_values
    both = jnp.where(head_lanes(grad_query[0], 0), grad_query[0], grad_query[1])
    return both.astype(LOW), grad_keys.astype(LOW), grad_values.astype(LOW)


def causal_allowed(rows, mask_row):
    valid = jnp.sum(mask_row, axis=-1, keepdims=True)
    query_at = lax.broadcasted_iota(jnp.int32, (rows, rows), 0)
    key_at = lax.broadcasted_iota(jnp.int32, (rows, rows), 1)
    return (query_at >= key_at) & (key_at < valid)


def for_head_groups(count, rows, span, function):
    lanes = min(span, 4 * PAIR)
    groups = span // lanes
    for s in range(count):

        @pl.loop(0, groups)
        def _(g, s=s):
            for p in range(lanes // PAIR):
                lane = pl.multiple_of(g * lanes + p * PAIR, PAIR)
                function(s, s * rows, lane, 2 * (g * (lanes // PAIR) + p))


def self_forward_kernel(
    tokens, mask, vectors, weight, query_weight, qkv, mixed, logs, unit, inverse, query, low
):
    step = pl.program_id(0)
    count, length, span = tokens.shape
    rows = padded(length)

    @pl.when(step == 0)
    def _():
        fill_tokens(low, tokens)

    @pl.when(step < 3)
    def _():
        product = dot_nn(low[...], weight[0])
        shift = jnp.where(
            step == 0, vectors[0:1], jnp.where(step == 2, vectors[1:2], jnp.zeros_like(vectors[0:1]))
        )
        product = (product + shift) * jnp.where(step == 0, SCALE, 1.0)
        qkv[step] = product.astype(LOW)

    @pl.when(step == 3)
    def _():
        logs[...] = jnp.zeros_like(logs)

        def pair(s, row, lane, head):
            allowed = causal_allowed(rows, mask[s : s + 1])
            where = (pl.ds(row, rows), pl.ds(lane, PAIR))
            both, sums = attend_pair(qkv[(0,) + where], qkv[(1,) + where], qkv[(2,) + where], allowed)
            mixed[where] = both
            table = logs[row : row + rows]
            spot = lax.broadcasted_iota(jnp.int32, table.shape, 1)
            for which in range(2):
                table = jnp.where(spot == head + which, sums[which], table)
            logs[row : row + rows] = table

        for_head_groups(count, rows, span, pair)
        hidden = low[...].astype(jnp.float32) + (dot_nn(mixed[...], weight[0]) + vectors[2:3])
        unit[...], inverse[...] = standardise(hidden)

    @pl.when(step == 4)
    def _():
        first_low = (unit[...] * vectors[3:4] + vectors[4:5]).astype(LOW)
        product = dot_nn(first_low, query_weight[0])
        query[...] = ((product + vectors[5:6]) * SCALE).astype(LOW)


def whole_spec(shape):
    return pl.BlockSpec(shape, lambda *at: (0,) * len(shape))


def params(**more):
    return pltpu.CompilerParams(vmem_limit_bytes=BUDGET, **more)


def self_forward(tokens, mask, vectors, self_full, cross_full):
    count, length, span = tokens.shape
    total = count * padded(length)
    outs = [
        jax.ShapeDtypeStruct((3, total, span), LOW),
        jax.ShapeDtypeStruct((total, span), LOW),
        jax.ShapeDtypeStruct((total, 128), jnp.float32),
        jax.ShapeDtypeStruct((total, span), jnp.float32),
        jax.ShapeDtypeStruct((total, 1), jnp.float32),
        jax.ShapeDtypeStruct((total, span), LOW),
    ]
    return pl.pallas_call(
        self_forward_kernel,
        grid=(5,),
        in_specs=[
            whole_spec(tokens.shape),
            whole_spec(mask.shape),
            whole_spec(vectors.shape),
            pl.BlockSpec((1, span, span), lambda i: (jnp.minimum(i, 3), 0, 0)),
            pl.BlockSpec((1, span, span), lambda i: (0, 0, 0)),
        ],
        out_specs=[whole_spec(out.shape) for out in outs],
        out_shape=outs,
        scratch_shapes=[pltpu.VMEM((total, span), LOW)],
        compiler_params=params(),
        name="self_forward",
    )(tokens, mask, vectors, self_full, cross_full)


def memory_forward(memory, cross_full, vectors):
    rows, span = memory.shape
    tile = min(rows, 512)

    def kernel(memory, key_weight, value_weight, vectors, keys, values):
        keys[...] = dot_nn(memory[...], key_weight[0]).astype(LOW)
        values[...] = (dot_nn(memory[...], value_weight[0]) + vectors[6:7]).astype(LOW)

    block = pl.BlockSpec((tile, span), lambda i: (i, 0))
    out = jax.ShapeDtypeStruct((rows, span), LOW)
    return pl.pallas_call(
        kernel,
        grid=(rows // tile,),
        in_specs=[
            block,
            pl.BlockSpec((1, span, span), lambda i: (1, 0, 0)),
            pl.BlockSpec((1, span, span), lambda i: (2, 0, 0)),
            whole_spec(vectors.shape),
        ],
        out_specs=[block, block],
        out_shape=[out, out],
        compiler_params=params(),
        name="memory_forward",
    )(memory, cross_full, cross_full, vectors)


CROSS_LANES = 2 * PAIR


def cross_forward(query, keys, values, lengths):
    count = lengths.shape[0]
    rows, slots, span = query.shape[0] // count, keys.shape[0] // count, query.shape[1]
    groups = span // CROSS_LANES

    def kernel(lengths, query, keys, values, mixed, logs):
        slot = lax.broadcasted_iota(jnp.int32, (1, slots), 1)
        allowed = slot < lengths[pl.program_id(0)]
        table = jnp.zeros(logs.shape[1:], jnp.float32)
        spot = lax.broadcasted_iota(jnp.int32, table.shape, 1)
        for p in range(CROSS_LANES // PAIR):
            where = pl.ds(p * PAIR, PAIR)
            both, sums = attend_pair(query[:, where], keys[:, where], values[:, where], allowed)
            mixed[:, where] = both
            for which in range(2):
                table = jnp.where(spot == 2 * p + which, sums[which], table)
        logs[0] = table

    token = pl.BlockSpec((rows, CROSS_LANES), lambda s, g: (s, g))
    stored = pl.BlockSpec((slots, CROSS_LANES), lambda s, g: (s, g))
    return pl.pallas_call(
        kernel,
        grid=(count, groups),
        in_specs=[pl.BlockSpec(memory_space=pltpu.SMEM), token, stored, stored],
        out_specs=[token, pl.BlockSpec((1, rows, 128), lambda s, g: (s * groups + g, 0, 0))],
        out_shape=[
            jax.ShapeDtypeStruct(query.shape, LOW),
            jax.ShapeDtypeStruct((count * groups, rows, 128), jnp.float32),
        ],
        compiler_params=params(),
        name="cross_forward",
    )(lengths, query, keys, values)


def feed_forward_kernel(
    tiles,
    mixed,
    out_weight,
    unit_one,
    vectors,
    bias,
    up,
    down,
    cotangent,
    hidden,
    slope,
    output,
    unit_two,
    inverse_two,
    grad_three,
    sums,
    second,
    low,
    total,
):
    step = pl.program_id(0)

    @pl.when(step == 0)
    def _():
        first = unit_one[...] * vectors[3:4] + vectors[4:5]
        unit, inverse_two[...] = standardise(
            first + (dot_nn(mixed[...], out_weight[0]) + vectors[7:8])
        )
        unit_two[...] = unit
        second[...] = unit * vectors[8:9] + vectors[9:10]
        low[...] = second[...].astype(LOW)
        total[...] = jnp.zeros_like(total)

    inner = dot_nn(low[...], up[0]) + bias[...]
    half = 0.5 + 0.5 * lax.erf(inner * (0.5**0.5))
    bell = jnp.exp(-0.5 * inner * inner) * ((0.5 / math.pi) ** 0.5)
    active = (inner * half).astype(LOW)
    hidden[...] = active
    slope[...] = (half + inner * bell).astype(LOW)
    total[...] += dot_nt(active, down[0])

    @pl.when(step == tiles - 1)
    def _():
        unit, inverse = standardise(second[...] + (total[...] + vectors[10:11]))
        store_tokens(output, unit * vectors[11:12] + vectors[12:13])
        fill_tokens(total, cotangent)
        grad = total[...]
        down_grad = norm_back(grad, unit, inverse, vectors[11:12])
        grad_three[...] = down_grad
        sums[...] = jnp.zeros_like(sums)
        sums[0:1] = column_sum(down_grad.astype(LOW))
        sums[1:2] = column_sum(grad * unit)
        sums[2:3] = column_sum(grad)


FEED_TILE = 512


def feed_forward(mixed, cross_full, unit_one, vectors, bias, feed_full, cotangent):
    total, span = mixed.shape
    width = feed_full.shape[2]
    tiles = width // FEED_TILE
    tile = pl.BlockSpec((total, FEED_TILE), lambda j: (0, j))
    outs = [
        jax.ShapeDtypeStruct((total, width), LOW),
        jax.ShapeDtypeStruct((total, width), LOW),
        jax.ShapeDtypeStruct(cotangent.shape, LOW),
        jax.ShapeDtypeStruct((total, span), jnp.float32),
        jax.ShapeDtypeStruct((total, 1), jnp.float32),
        jax.ShapeDtypeStruct((total, span), jnp.float32),
        jax.ShapeDtypeStruct((8, span), jnp.float32),
    ]
    return pl.pallas_call(
        functools.partial(feed_forward_kernel, tiles),
        grid=(tiles,),
        in_specs=[
            whole_spec(mixed.shape),
            pl.BlockSpec((1, span, span), lambda j: (3, 0, 0)),
            whole_spec(unit_one.shape),
            whole_spec(vectors.shape),
            pl.BlockSpec((1, FEED_TILE), lambda j: (0, j)),
            pl.BlockSpec((1, span, FEED_TILE), lambda j: (0, 0, j)),
            pl.BlockSpec((1, span, FEED_TILE), lambda j: (1, 0, j)),
            whole_spec(cotangent.shape),
        ],
        out_specs=[tile, tile] + [whole_spec(out.shape) for out in outs[2:]],
        out_shape=outs,
        scratch_shapes=[
            pltpu.VMEM((total, span), jnp.float32),
            pltpu.VMEM((total, span), LOW),
            pltpu.VMEM((total, span), jnp.float32),
        ],
        compiler_params=params(),
        name="feed_forward",
    )(mixed, cross_full, unit_one, vectors, bias, feed_full, feed_full, cotangent)


def feed_backward_kernel(
    tiles,
    grad_three,
    unit_two,
    inverse_two,
    vectors,
    hidden,
    slope,
    up,
    down,
    out_weight,
    mixed,
    feed_grad,
    bias_grad,
    grad_two,
    grad_mixed,
    out_grad,
    sums,
    low,
    branch,
    total,
):
    step = pl.program_id(0)

    @pl.when(step == 0)
    def _():
        low[...] = (unit_two[...] * vectors[8:9] + vectors[9:10]).astype(LOW)
        branch[...] = grad_three[...].astype(LOW)
        total[...] = grad_three[...]

    grad_inner = (slope[...].astype(jnp.float32) * dot_nn(branch[...], down[0])).astype(LOW)
    feed_grad[0] = dot_tn(low[...], grad_inner).astype(LOW)
    feed_grad[1] = dot_tn(branch[...], hidden[...]).astype(LOW)
    bias_grad[...] = column_sum(grad_inner)
    total[...] += dot_nt(grad_inner, up[0])

    @pl.when(step == tiles - 1)
    def _():
        grad = total[...]
        unit = unit_two[...]
        down_grad = norm_back(grad, unit, inverse_two[...], vectors[8:9])
        grad_two[...] = down_grad
        grad_low = down_grad.astype(LOW)
        sums[...] = jnp.zeros_like(sums)
        sums[0:1] = column_sum(grad_low)
        sums[1:2] = column_sum(grad * unit)
        sums[2:3] = column_sum(grad)
        grad_mixed[...] = dot_nt(grad_low, out_weight[0]).astype(LOW)
        out_grad[...] = dot_tn(mixed[...], grad_low).astype(LOW)


def feed_backward(grad_three, unit_two, inverse_two, vectors, hidden, slope, feed_full, cross_full, mixed):
    total, span = mixed.shape
    width = feed_full.shape[2]
    tiles = width // FEED_TILE
    tile = pl.BlockSpec((total, FEED_TILE), lambda j: (0, j))
    outs = [
        jax.ShapeDtypeStruct((2, span, width), LOW),
        jax.ShapeDtypeStruct((1, width), jnp.float32),
        jax.ShapeDtypeStruct((total, span), jnp.float32),
        jax.ShapeDtypeStruct((total, span), LOW),
        jax.ShapeDtypeStruct((span, span), LOW),
        jax.ShapeDtypeStruct((8, span), jnp.float32),
    ]
    return pl.pallas_call(
        functools.partial(feed_backward_kernel, tiles),
        grid=(tiles,),
        in_specs=[
            whole_spec(grad_three.shape),
            whole_spec(unit_two.shape),
            whole_spec(inverse_two.shape),
            whole_spec(vectors.shape),
            tile,
            tile,
            pl.BlockSpec((1, span, FEED_TILE), lambda j: (0, 0, j)),
            pl.BlockSpec((1, span, FEED_TILE), lambda j: (1, 0, j)),
            pl.BlockSpec((1, span, span), lambda j: (3, 0, 0)),
            whole_spec(mixed.shape),
        ],
        out_specs=[
            pl.BlockSpec((2, span, FEED_TILE), lambda j: (0, 0, j)),
            pl.BlockSpec((1, FEED_TILE), lambda j: (0, j)),
        ]
        + [whole_spec(out.shape) for out in outs[2:]],
        out_shape=outs,
        scratch_shapes=[
            pltpu.VMEM((total, span), LOW),
            pltpu.VMEM((total, span), LOW),
            pltpu.VMEM((total, span), jnp.float32),
        ],
        compiler_params=params(),
        name="feed_backward",
    )(grad_three, unit_two, inverse_two, vectors, hidden, slope, feed_full, feed_full, cross_full, mixed)


def cross_backward(query, keys, values, lengths, logs, grad_mixed):
    count = lengths.shape[0]
    rows, slots, span = query.shape[0] // count, keys.shape[0] // count, query.shape[1]
    groups = span // CROSS_LANES

    def kernel(lengths, query, keys, values, logs, grad, grad_query, grad_keys, grad_values, sums):
        slot = lax.broadcasted_iota(jnp.int32, (1, slots), 1)
        allowed = slot < lengths[pl.program_id(0)]
        sums[...] = jnp.zeros_like(sums)
        for p in range(CROSS_LANES // PAIR):
            where = pl.ds(p * PAIR, PAIR)
            columns = [pick_column(logs[0], 2 * p + which) for which in range(2)]
            results = attend_pair_back(
                query[:, where], keys[:, where], values[:, where], allowed, columns, grad[:, where]
            )
            grad_query[:, where], grad_keys[:, where], grad_values[:, where] = results
            sums[0, 0:1, where] = column_sum(results[0])
            sums[0, 1:2, where] = column_sum(results[2])

    token = pl.BlockSpec((rows, CROSS_LANES), lambda s, g: (s, g))
    stored = pl.BlockSpec((slots, CROSS_LANES), lambda s, g: (s, g))
    return pl.pallas_call(
        kernel,
        grid=(count, groups),
        in_specs=[
            pl.BlockSpec(memory_space=pltpu.SMEM),
            token,
            stored,
            stored,
            pl.BlockSpec((1, rows, 128), lambda s, g: (s * groups + g, 0, 0)),
            token,
        ],
        out_specs=[
            token,
            stored,
            stored,
            pl.BlockSpec((1, 8, CROSS_LANES), lambda s, g: (s, 0, g)),
        ],
        out_shape=[
            jax.ShapeDtypeStruct(query.shape, LOW),
            jax.ShapeDtypeStruct(keys.shape, LOW),
            jax.ShapeDtypeStruct(keys.shape, LOW),
            jax.ShapeDtypeStruct((count, 8, span), jnp.float32),
        ],
        compiler_params=params(),
        name="cross_backward",
    )(lengths, query, keys, values, logs, grad_mixed)


def memory_backward(memory, grad_keys, grad_values, cross_full):
    rows, span = memory.shape
    tile = min(rows, 512)
    tiles = rows // tile

    def kernel(memory, grad_keys, grad_values, key_weight, value_weight, grad, weight_grad, sums):
        step = pl.program_id(0)
        grad[...] = dot_nt(grad_keys[...], key_weight[0]) + dot_nt(grad_values[...], value_weight[0])
        for number, part in ((0, grad_keys), (1, grad_values)):
            product = dot_tn(memory[...], part[...])

            @pl.when(step == 0)
            def _():
                sums[number] = product

            @pl.when(step > 0)
            def _():
                sums[number] += product

        @pl.when(step == tiles - 1)
        def _():
            weight_grad[...] = sums[...].astype(LOW)

    block = pl.BlockSpec((tile, span), lambda i: (i, 0))
    return pl.pallas_call(
        kernel,
        grid=(tiles,),
        in_specs=[
            block,
            block,
            block,
            pl.BlockSpec((1, span, span), lambda i: (1, 0, 0)),
            pl.BlockSpec((1, span, span), lambda i: (2, 0, 0)),
        ],
        out_specs=[block, whole_spec((2, span, span))],
        out_shape=[
            jax.ShapeDtypeStruct((rows, span), jnp.float32),
            jax.ShapeDtypeStruct((2, span, span), LOW),
        ],
        scratch_shapes=[pltpu.VMEM((2, span, span), jnp.float32)],
        compiler_params=params(),
        name="memory_backward",
    )(memory, grad_keys, grad_values, cross_full, cross_full)


def self_backward_kernel(
    tokens,
    mask,
    vectors,
    weight,
    query_weight,
    qkv,
    mixed,
    logs,
    unit,
    inverse,
    cross_query_grad,
    grad_two,
    cross_sums,
    feed_sums,
    out_sums,
    bias_grad,
    query_grad,
    weight_grads,
    input_grad,
    terms,
    low,
    grads,
    total,
):
    step = pl.program_id(0)
    count, length, span = tokens.shape
    rows = padded(length)

    @pl.when(step == 0)
    def _():
        fill_tokens(low, tokens)
        terms[...] = jnp.zeros_like(terms)
        first_low = (unit[...] * vectors[3:4] + vectors[4:5]).astype(LOW)
        query_grad[...] = (dot_tn(first_low, cross_query_grad[...]) * SCALE).astype(LOW)
        grad = grad_two[...] + dot_nt(cross_query_grad[...], query_weight[0]) * SCALE
        down_grad = norm_back(grad, unit[...], inverse[...], vectors[3:4])
        total[...] = down_grad
        terms[2:3] = column_sum(down_grad.astype(LOW))
        terms[3:4] = column_sum(grad * unit[...])
        terms[4:5] = column_sum(grad)
        spread = jnp.sum(cross_sums[...], axis=0)
        terms[5:6] = spread[0:1] * SCALE
        terms[6:7] = spread[1:2]
        terms[7:10] = out_sums[0:3]
        terms[10:13] = feed_sums[0:3]
        for k in range(bias_grad.shape[1] // span):
            terms[13 + k : 14 + k] = bias_grad[:, k * span : (k + 1) * span]

    @pl.when(step == 1)
    def _():
        grad_low = total[...].astype(LOW)
        weight_grads[0] = dot_tn(mixed[...], grad_low).astype(LOW)
        grads[0] = dot_nt(grad_low, weight[0]).astype(LOW)

        def pair(s, row, lane, head):
            allowed = causal_allowed(rows, mask[s : s + 1])
            where = (pl.ds(row, rows), pl.ds(lane, PAIR))
            table = logs[row : row + rows]
            columns = [pick_column(table, head + which) for which in range(2)]
            results = attend_pair_back(
                qkv[(0,) + where],
                qkv[(1,) + where],
                qkv[(2,) + where],
                allowed,
                columns,
                grads[(0,) + where],
            )
            for number in range(3):
                grads[(1 + number,) + where] = results[number]

        for_head_groups(count, rows, span, pair)
        terms[0:1] = column_sum(grads[1]) * SCALE
        terms[1:2] = column_sum(grads[3])

    @pl.when(step > 1)
    def _():
        factor = jnp.where(step == 2, SCALE, 1.0)
        part = grads[step - 1]
        weight_grads[0] = (dot_tn(low[...], part) * factor).astype(LOW)
        total[...] += dot_nt(part, weight[0]) * factor

    @pl.when(step == 4)
    def _():
        store_tokens(input_grad, total[...])


def self_backward(
    tokens, mask, vectors, self_full, cross_full, saved, cross_query_grad, grad_two, cross_sums, feed_sums, out_sums, bias_grad
):
    count, length, span = tokens.shape
    qkv, mixed, logs, unit, inverse = saved
    total = mixed.shape[0]
    count_terms = 13 + bias_grad.shape[1] // span
    count_terms += -count_terms % 8
    outs = [
        jax.ShapeDtypeStruct((span, span), LOW),
        jax.ShapeDtypeStruct((4, span, span), LOW),
        jax.ShapeDtypeStruct(tokens.shape, jnp.float32),
        jax.ShapeDtypeStruct((count_terms, span), jnp.float32),
    ]

    def which(i):
        return jnp.where(i <= 1, 3, i - 2)

    operands = (
        tokens, mask, vectors, self_full, cross_full, qkv, mixed, logs, unit, inverse,
        cross_query_grad, grad_two, cross_sums, feed_sums, out_sums, bias_grad,
    )
    specs = [whole_spec(operand.shape) for operand in operands]
    specs[3] = pl.BlockSpec((1, span, span), lambda i: (which(i), 0, 0))
    specs[4] = pl.BlockSpec((1, span, span), lambda i: (0, 0, 0))
    return pl.pallas_call(
        self_backward_kernel,
        grid=(5,),
        in_specs=specs,
        out_specs=[
            whole_spec((span, span)),
            pl.BlockSpec((1, span, span), lambda i: (which(i), 0, 0)),
            whole_spec(tokens.shape),
            whole_spec((count_terms, span)),
        ],
        out_shape=outs,
        scratch_shapes=[
            pltpu.VMEM((total, span), LOW),
            pltpu.VMEM((4, total, span), LOW),
            pltpu.VMEM((total, span), jnp.float32),
        ],
        compiler_params=params(),
        name="self_backward",
    )(*operands)


def per_device(
    wide,
    narrow,
    decoder_input,
    memory,
    decoder_mask,
    memory_length,
    self_weights,
    cross_weights,
    feed_weights,
    vectors,
    hidden_bias,
    cotangent,
):
    seq_count, seq_length, model_width = decoder_input.shape
    mem_span = memory.shape[1]
    memory_low = memory.reshape(seq_count * mem_span, model_width)
    (self_full, cross_full, feed_full), vector_all, bias_all = gather_weights(
        wide, narrow, (self_weights, cross_weights, feed_weights), vectors, hidden_bias, 1
    )
    qkv, self_mixed, self_logs, unit_one, inverse_one, cross_query = self_forward(
        decoder_input, decoder_mask, vector_all, self_full, cross_full
    )
    cross_keys, cross_values = memory_forward(memory_low, cross_full, vector_all)
    cross_mixed, cross_logs = cross_forward(cross_query, cross_keys, cross_values, memory_length)
    hidden, slope, layer_output, unit_two, inverse_two, grad_three, feed_sums = feed_forward(
        cross_mixed, cross_full, unit_one, vector_all, bias_all, feed_full, cotangent
    )
    feed_part, bias_part, grad_two, grad_cmixed, cross_out_grad, out_sums = feed_backward(
        grad_three, unit_two, inverse_two, vector_all, hidden, slope, feed_full, cross_full, cross_mixed
    )
    (feed_grad,) = reduce_gradients(wide, narrow, [feed_part], 2)
    cross_gq, cross_gk, cross_gv, cross_sums = cross_backward(
        cross_query, cross_keys, cross_values, memory_length, cross_logs, grad_cmixed
    )
    memory_grad, memory_parts = memory_backward(memory_low, cross_gk, cross_gv, cross_full)
    cross_query_part, self_parts, input_grad, terms = self_backward(
        decoder_input,
        decoder_mask,
        vector_all,
        self_full,
        cross_full,
        (qkv, self_mixed, self_logs, unit_one, inverse_one),
        cross_gq,
        grad_two,
        cross_sums,
        feed_sums,
        out_sums,
        bias_part,
    )
    (cross_grad,) = reduce_gradients(
        wide, narrow, [cross_query_part[None], memory_parts, cross_out_grad[None]], 3
    )
    self_weight_gradient, totals = reduce_gradients(wide, narrow, [self_parts], 4, terms)
    vector_total = totals[: vectors.shape[0]]
    bias_rows = bias_all.shape[1] // model_width
    bias_total = totals[vectors.shape[0] : vectors.shape[0] + bias_rows].reshape(1, -1)
    narrow_index = lax.axis_index("narrow")
    vectors_grad = lax.dynamic_slice_in_dim(
        vector_total, narrow_index * vectors.shape[1], vectors.shape[1], 1
    )
    hidden_bias_grad = lax.dynamic_slice_in_dim(
        bias_total, narrow_index * hidden_bias.shape[1], hidden_bias.shape[1], 1
    )
    return (
        layer_output,
        input_grad,
        memory_grad.reshape(seq_count, mem_span, model_width),
        self_weight_gradient,
        cross_grad,
        feed_grad,
        vectors_grad,
        hidden_bias_grad,
    )


def solution(mesh):
    placed = (
        P(("wide", "narrow"), None, None),
        P(("wide", "narrow"), None, None),
        P(("wide", "narrow"), None),
        P(("wide", "narrow")),
        P(None, "wide", "narrow"),
        P(None, "wide", "narrow"),
        P(None, "wide", "narrow"),
        P(None, "narrow"),
        P(None, "narrow"),
        P(("wide", "narrow"), None, None),
    )
    return jax.shard_map(
        functools.partial(per_device, mesh.shape["wide"], mesh.shape["narrow"]),
        mesh=mesh,
        in_specs=placed,
        out_specs=(
            P(("wide", "narrow"), None, None),
            P(("wide", "narrow"), None, None),
            P(("wide", "narrow"), None, None),
            P(None, "wide", "narrow"),
            P(None, "wide", "narrow"),
            P(None, "wide", "narrow"),
            P(None, "narrow"),
            P(None, "narrow"),
        ),
        check_vma=False,
    )
```

```python
import functools
import math

import jax
import jax.numpy as jnp
from jax import lax
from jax.experimental import pallas as pl
from jax.experimental.pallas import tpu as pltpu
from jax.sharding import PartitionSpec as P

HEADS = 16
HEAD_DIM = 64


MESH_ID = pl.DeviceIdType.MESH


class Position:
    def __init__(self, wide, narrow):
        self.sizes = {"line": wide // 4, "pair": 2, "core": 2, "column": narrow}

    def get(self, axis):
        if axis == "column":
            return lax.axis_index("narrow")
        index = lax.axis_index("wide")
        if axis == "core":
            return index % 2
        return (index // 2) % 2 if axis == "pair" else index // 4

    def device(self, **moved):
        spot = {name: moved.get(name, self.get(name)) for name in self.sizes}
        return (spot["line"] * 4 + spot["pair"] * 2 + spot["core"], spot["column"])


class Channels:
    def __init__(self, sends, recvs):
        self.sends, self.recvs, self.used = sends, recvs, 0

    def take(self):
        self.used += 1
        number = self.used - 1
        return lambda: (self.sends.at[number], self.recvs.at[number])


def remote(source, target, channel, device):
    return pltpu.make_async_remote_copy(
        src_ref=source,
        dst_ref=target,
        send_sem=channel()[0],
        recv_sem=channel()[1],
        device_id=device,
        device_id_type=MESH_ID,
    )


def flip(index, bit):
    return index + bit - 2 * bit * ((index // bit) % 2)


def peers(position, axis, distance):
    at = (position.get(axis) + distance) % position.sizes[axis]
    return at, position.device(**{axis: at})


def greet(position):
    barrier = pltpu.get_barrier_semaphore()
    expected = 0
    for axis, size in position.sizes.items():
        for distance in range(1, size):
            pl.semaphore_signal(
                barrier,
                inc=1,
                device_id=peers(position, axis, distance)[1],
                device_id_type=MESH_ID,
            )
            expected += 1
    pl.semaphore_wait(barrier, expected)


def advance(generator):
    return next(generator, "done") != "done"


class Rounds:
    def __init__(self, flows, live=(), together=2):
        self.waiting, self.live, self.together = list(flows), list(live), together

    def run(self, count=None):
        while (self.waiting or self.live) and (count is None or count > 0):
            self.live = self.live + self.waiting[: self.together]
            self.waiting = self.waiting[self.together :]
            self.live = [flow for flow in self.live if advance(flow)]
            count = None if count is None else count - 1


def finish_sends(sent):
    for describe in sent:
        describe().wait_send()


def gather_axis(position, axis, channels, block, own, sent):
    arrivals = []
    for distance in range(1, position.sizes[axis]):
        channel = channels.take()

        def send(distance=distance, channel=channel):
            device = peers(position, axis, distance)[1]
            return remote(own(), block(position.get(axis)), channel, device)

        def arrival(distance=distance, channel=channel):
            came, device = peers(position, axis, -distance)
            return remote(block(came), block(came), channel, device)

        send().start()
        sent.append(send)
        arrivals.append(arrival)
    yield
    for arrival in arrivals:
        arrival().wait_recv()


def gather_flow(position, channels, local_sem, own, region, order):
    sent = []

    def place(done, axis=None, at=None):
        spot = {name: None if name in done else position.get(name) for name in position.sizes}
        if axis is not None:
            spot[axis] = at
        return region(**spot)

    def local():
        return pltpu.make_async_copy(own(), place(()), local_sem())

    local().start()
    for number, axis in enumerate(order):
        done = order[:number]

        def block(j, axis=axis, done=done):
            return place(done, axis, j)

        def source(block=block, axis=axis, first=number == 0):
            return own() if first else block(position.get(axis))

        yield from gather_axis(position, axis, channels, block, source, sent)
        if number == 0:
            local().wait()
    finish_sends(sent)


def whole(index):
    return slice(None) if index is None else index


def row_splits(rows, most):
    return max(1, min(most, rows // 16))


def flow_channels(wide, narrow):
    return 2 + (wide // 4 - 1) + (narrow - 1)


ORDER_A = ("line", "pair", "column", "core")
ORDER_B = ("line", "column", "pair", "core")


def gather_pieces(arrays):
    pieces = []
    for number, array in enumerate(arrays):
        matrices, rows, width = array.shape
        parts = row_splits(rows, 4) if matrices == 2 else 1
        for part in range(parts):
            for matrix in range(matrices):
                pieces.append((number, matrix, part, parts))
    return pieces


def gather_flows(position, channels, local_sems, pieces, blocks, fulls):
    flows = []
    for number, (array, matrix, part, parts) in enumerate(pieces):
        block_ref, full_ref = blocks[array], fulls[array]
        rows = block_ref.shape[1] // parts
        width = block_ref.shape[2]

        def region(
            line, pair, core, column, full_ref=full_ref, matrix=matrix, part=part, rows=rows, width=width
        ):
            columns = (
                slice(None)
                if column is None
                else pl.ds(pl.multiple_of(column * width, 128), width)
            )
            return full_ref.at[
                matrix, whole(line), whole(pair), whole(core), pl.ds(part * rows, rows), columns
            ]

        def own(block_ref=block_ref, matrix=matrix, part=part, rows=rows):
            return block_ref.at[matrix, pl.ds(part * rows, rows)]

        order = ORDER_A if number % 2 == 0 else ORDER_B
        flows.append(gather_flow(
                position, channels, lambda number=number: local_sems.at[number], own, region, order
            ))
    return flows


def column_flow(position, channels, sem, block_ref, full_ref):
    def region(column):
        return full_ref.at[column]

    def local():
        return pltpu.make_async_copy(block_ref, region(position.get("column")), sem)

    sent = []
    local().start()
    yield from gather_axis(position, "column", channels, region, lambda: block_ref, sent)
    local().wait()
    finish_sends(sent)


def full_shape(wide, narrow, array):
    matrices, rows, width = array.shape
    return jax.ShapeDtypeStruct((matrices, wide // 4, 2, 2, rows, width * narrow), array.dtype)


def gather_kernel(wide, narrow, pieces, count, *refs):
    blocks, (vector_ref, bias_ref) = refs[:count], refs[count : count + 2]
    fulls = refs[count + 2 : 2 * count + 2]
    vector_out, bias_out, sends, recvs, local_sems = refs[2 * count + 2 :]
    position = Position(wide, narrow)
    channels = Channels(sends, recvs)
    greet(position)
    flows = [
        column_flow(position, channels, local_sems.at[len(pieces)], vector_ref, vector_out),
        column_flow(position, channels, local_sems.at[len(pieces) + 1], bias_ref, bias_out),
    ]
    rounds = Rounds(gather_flows(position, channels, local_sems, pieces, blocks, fulls), flows)
    rounds.run()


def gather_weights(wide, narrow, arrays, vectors, hidden_bias, collective_id):
    pieces = gather_pieces(arrays)
    copies = flow_channels(wide, narrow) * (len(pieces) + 2)
    outs = [full_shape(wide, narrow, array) for array in arrays]
    outs.append(jax.ShapeDtypeStruct((narrow,) + vectors.shape, vectors.dtype))
    outs.append(jax.ShapeDtypeStruct((narrow,) + hidden_bias.shape, hidden_bias.dtype))
    results = pl.pallas_call(
        functools.partial(gather_kernel, wide, narrow, pieces, len(arrays)),
        out_shape=outs,
        in_specs=[pl.BlockSpec(memory_space=pltpu.VMEM)] * (len(arrays) + 2),
        out_specs=[pl.BlockSpec(memory_space=pl.ANY)] * len(outs),
        scratch_shapes=[
            pltpu.SemaphoreType.DMA((copies,)),
            pltpu.SemaphoreType.DMA((copies,)),
            pltpu.SemaphoreType.DMA((len(pieces) + 2,)),
        ],
        compiler_params=pltpu.CompilerParams(collective_id=collective_id, has_side_effects=True),
        name="gather_weights",
    )(*arrays, vectors, hidden_bias)
    fulls = [
        full.reshape(full.shape[0], -1, full.shape[-1]) for full in results[: len(arrays)]
    ]
    vector_all = jnp.moveaxis(results[-2], 0, 1).reshape(vectors.shape[0], -1)
    bias_all = jnp.moveaxis(results[-1], 0, 1).reshape(1, -1)
    return fulls, vector_all, bias_all


def add_rows(target, parts):
    lead = target.shape[:-2]
    count = math.prod(lead)

    def add(spot):
        total = parts[0][spot].astype(jnp.float32)
        for part in parts[1:]:
            total = total + part[spot].astype(jnp.float32)
        target[spot] = total.astype(target.dtype)

    if count == 1:
        add((0,) * len(lead))
        return

    @pl.loop(0, count)
    def _(k):
        where = []
        for extent in reversed(lead):
            where.insert(0, k % extent)
            k = k // extent
        add(tuple(where))


def reduce_axis(position, axis, channels, local, slots, result, sent):
    size = position.sizes[axis]
    for distance in range(1, size):
        channel = channels.take()

        def send(distance=distance, channel=channel):
            at, device = peers(position, axis, distance)
            return remote(local(at), slots.at[distance - 1], channel, device)

        send().start()
        sent.append(send)
    yield
    for send in sent[1 - size :]:
        send().wait_recv()
    add_rows(
        result(), [local(position.get(axis))] + [slots.at[k] for k in range(size - 1)]
    )


def reduce_flow(position, channels, local_sem, loc, grads, result, buffers, order):
    first, mid, last, line_slots = buffers
    sent = []

    def own():
        return pltpu.make_async_copy(grads(position.get("core")), loc(), local_sem())

    channel = channels.take()

    def swap():
        mine = position.get("core")
        return remote(grads(1 - mine), first, channel, position.device(core=1 - mine))

    own().start()
    swap().start()
    sent.append(swap)
    yield
    own().wait()
    swap().wait_recv()
    add_rows(first, [first, loc()])
    width = result().shape[-1]

    def columns(j):
        return pl.ds(pl.multiple_of(j * width, 128), width)

    def held():
        return mid.at[0]

    def final():
        return last.at[0]

    if order == "A":
        yield from reduce_axis(
            position, "column", channels, lambda j: first.at[:, :, :, columns(j)], mid, held, sent
        )
        yield from reduce_axis(position, "pair", channels, lambda j: held().at[:, j], last, final, sent)
    else:
        yield from reduce_axis(position, "pair", channels, lambda j: first.at[:, j], mid, held, sent)
        yield from reduce_axis(
            position, "column", channels, lambda j: held().at[:, :, columns(j)], last, final, sent
        )
    yield from reduce_axis(
        position, "line", channels, lambda j: final().at[pl.ds(j, 1)], line_slots, result, sent
    )
    finish_sends(sent)


def double_flow(position, channels, terms_ref, total, inbox, result):
    total[0] = terms_ref[...]
    step = 0
    for axis in ("core", "pair", "line", "column"):
        bit = 1
        while bit < position.sizes[axis]:
            channel = channels.take()

            def describe():
                to = position.device(**{axis: flip(position.get(axis), bit)})
                return remote(total.at[step], inbox.at[step], channel, to)

            describe().start()
            yield
            describe().wait_recv()
            total[step + 1] = total[step] + inbox[step]
            describe().wait_send()
            bit *= 2
            step += 1
    result[...] = total[step]


class Reduction:
    RING = 4

    def __init__(self, wide, narrow, grads, parts, terms=None):
        self.wide, self.narrow, self.terms = wide, narrow, terms
        depth, span = grads[0].shape[1:]
        rows = depth // wide
        self.parts = row_splits(rows, parts)
        self.piece = rows // self.parts
        self.line, self.span, self.width = wide // 4, span, span // narrow
        matrices = [(s, m) for s, grad in enumerate(grads) for m in range(grad.shape[0])]
        self.pieces = [
            (number, source, inner, part)
            for number, (source, inner) in enumerate(matrices)
            for part in range(self.parts)
        ]
        self.views = [grad.reshape(grad.shape[0], self.line, 2, 2, rows, span) for grad in grads]
        self.out = jax.ShapeDtypeStruct((len(matrices), rows, self.width), jnp.float32)

    def order(self, number):
        return "A" if number % 2 == 0 else "B"

    def operands(self):
        return self.views + ([] if self.terms is None else [self.terms])

    def in_specs(self):
        specs = [pl.BlockSpec(memory_space=pl.ANY)] * len(self.views)
        return specs + ([] if self.terms is None else [pl.BlockSpec(memory_space=pltpu.VMEM)])

    def outs(self):
        if self.terms is None:
            return [self.out]
        return [self.out, jax.ShapeDtypeStruct(self.terms.shape, jnp.float32)]

    def out_specs(self):
        return [pl.BlockSpec(memory_space=pltpu.VMEM)] * len(self.outs())

    def scratch(self):
        low, line, piece = jnp.bfloat16, self.line, self.piece
        copies = flow_channels(self.wide, self.narrow) * len(self.pieces) + 16
        shapes = [
            pltpu.SemaphoreType.DMA((copies,)),
            pltpu.SemaphoreType.DMA((copies,)),
            pltpu.SemaphoreType.DMA((len(self.pieces),)),
            pltpu.VMEM((self.RING, line, 2, piece, self.span), low),
        ]
        if self.terms is not None:
            steps = (self.wide * self.narrow).bit_length() - 1
            shapes.append(pltpu.VMEM((steps + 1,) + self.terms.shape, jnp.float32))
            shapes.append(pltpu.VMEM((steps,) + self.terms.shape, jnp.float32))
        for number in range(len(self.pieces)):
            shapes.append(pltpu.VMEM((line, 2, piece, self.span), low))
            if self.order(number) == "A":
                shapes.append(pltpu.VMEM((self.narrow - 1, line, 2, piece, self.width), low))
                shapes.append(pltpu.VMEM((1, line, piece, self.width), low))
            else:
                shapes.append(pltpu.VMEM((1, line, piece, self.span), low))
                shapes.append(pltpu.VMEM((self.narrow - 1, line, piece, self.width), low))
            shapes.append(pltpu.VMEM((line - 1, 1, piece, self.width), low))
        return shapes

    def rounds(self, operands, outs, scratch):
        position = Position(self.wide, self.narrow)
        channels = Channels(scratch[0], scratch[1])
        local_sems, ring, buffers = scratch[2], scratch[3], scratch[4:]
        live = []
        if self.terms is not None:
            live.append(double_flow(position, channels, operands[-1], buffers[0], buffers[1], outs[1]))
            buffers = buffers[2:]
        flows = []
        for number, (matrix, source, inner, part) in enumerate(self.pieces):
            at = pl.ds(part * self.piece, self.piece)

            def grads(core, source=source, inner=inner, at=at):
                return operands[source].at[inner, :, :, core, at]

            flows.append(
                reduce_flow(
                    position,
                    channels,
                    lambda number=number: local_sems.at[number],
                    lambda number=number: ring.at[number % self.RING],
                    grads,
                    lambda matrix=matrix, at=at: outs[0].at[pl.ds(matrix, 1), at],
                    buffers[4 * number : 4 * number + 4],
                    self.order(number),
                )
            )
        return Rounds(flows, live)

    def greet(self):
        greet(Position(self.wide, self.narrow))


def reduce_gradients(reduction, collective_id):
    operands = reduction.operands()
    count, total = len(operands), len(operands) + len(reduction.outs())

    def kernel(*refs):
        reduction.greet()
        reduction.rounds(refs[:count], refs[count:total], refs[total:]).run()

    return pl.pallas_call(
        kernel,
        out_shape=reduction.outs(),
        in_specs=reduction.in_specs(),
        out_specs=reduction.out_specs(),
        scratch_shapes=reduction.scratch(),
        compiler_params=pltpu.CompilerParams(
            collective_id=collective_id, has_side_effects=True, vmem_limit_bytes=BUDGET
        ),
        name="reduce_gradients",
    )(*operands)


LOW = jnp.bfloat16
NEGATIVE = -1000000000.0
EPSILON = 1e-05
PAIR = 2 * HEAD_DIM
SCALE = HEAD_DIM ** (-0.5)
BUDGET = 65000 * 1024


def dot_nn(left, right):
    return jnp.dot(left, right, preferred_element_type=jnp.float32)


def dot_nt(left, right):
    return lax.dot_general(
        left, right, (((1,), (1,)), ((), ())), preferred_element_type=jnp.float32
    )


def dot_tn(left, right):
    return lax.dot_general(
        left, right, (((0,), (0,)), ((), ())), preferred_element_type=jnp.float32
    )


def padded(length):
    return -(-length // 16) * 16


def column_sum(rows):
    return jnp.sum(rows.astype(jnp.float32), axis=0, keepdims=True)


def standardise(hidden):
    centre = hidden - jnp.mean(hidden, axis=-1, keepdims=True)
    spread = jnp.mean(centre * centre, axis=-1, keepdims=True)
    inverse = lax.rsqrt(spread + EPSILON)
    return centre * inverse, inverse


def norm_back(grad, unit, inverse, gain):
    scaled = grad * gain
    first = jnp.mean(scaled, axis=-1, keepdims=True)
    second = jnp.mean(scaled * unit, axis=-1, keepdims=True)
    return inverse * (scaled - first - unit * second)


def fill_tokens(target, source):
    count, length, span = source.shape
    rows = padded(length)
    for s in range(count):
        if rows > length:
            base = s * rows + length // 16 * 16
            target[base : (s + 1) * rows] = jnp.zeros(((s + 1) * rows - base, span), target.dtype)
        target[s * rows : s * rows + length] = source[s].astype(target.dtype)


def store_tokens(target, values):
    count, length, span = target.shape
    rows = padded(length)
    for s in range(count):
        target[s] = values[s * rows : s * rows + length].astype(target.dtype)


def head_lanes(rows, which):
    lane = lax.broadcasted_iota(jnp.int32, rows.shape, 1)
    return (lane >= HEAD_DIM) == (which == 1)


def one_head(rows, which):
    return jnp.where(head_lanes(rows, which), rows, jnp.zeros_like(rows))


def pick_column(table, number):
    lane = lax.broadcasted_iota(jnp.int32, table.shape, 1)
    return jnp.sum(jnp.where(lane == number, table, 0.0), axis=1, keepdims=True)


def attend_pair(query, keys, values, allowed):
    mixed, logs = [], []
    for which in range(2):
        scores = dot_nt(one_head(query, which), keys)
        scores = jnp.where(allowed, scores, NEGATIVE)
        peak = jnp.max(scores, axis=-1, keepdims=True)
        expo = jnp.exp(scores - peak)
        total = jnp.sum(expo, axis=-1, keepdims=True)
        weights = (expo * (1.0 / total)).astype(LOW)
        mixed.append(dot_nn(weights, values))
        logs.append(peak + jnp.log(total))
    both = jnp.where(head_lanes(mixed[0], 0), mixed[0], mixed[1])
    return both.astype(LOW), logs


def attend_pair_back(query, keys, values, allowed, logs, grad):
    grad_query, grad_keys, grad_values = [], None, None
    for which in range(2):
        query_one, grad_one = one_head(query, which), one_head(grad, which)
        scores = jnp.where(allowed, dot_nt(query_one, keys), NEGATIVE)
        probs = jnp.exp(scores - logs[which])
        grad_probs = dot_nt(grad_one, values)
        slope = jnp.sum(grad_probs * probs, axis=-1, keepdims=True)
        grad_scores = (probs * (grad_probs - slope)).astype(LOW)
        grad_query.append(dot_nn(grad_scores, keys))
        part_keys = dot_tn(grad_scores, query_one)
        part_values = dot_tn(probs.astype(LOW), grad_one)
        grad_keys = part_keys if which == 0 else grad_keys + part_keys
        grad_values = part_values if which == 0 else grad_values + part_values
    both = jnp.where(head_lanes(grad_query[0], 0), grad_query[0], grad_query[1])
    return both.astype(LOW), grad_keys.astype(LOW), grad_values.astype(LOW)


def causal_allowed(rows, mask_row):
    valid = jnp.sum(mask_row, axis=-1, keepdims=True)
    query_at = lax.broadcasted_iota(jnp.int32, (rows, rows), 0)
    key_at = lax.broadcasted_iota(jnp.int32, (rows, rows), 1)
    return (query_at >= key_at) & (key_at < valid)


def for_head_groups(count, rows, span, function):
    lanes = min(span, 4 * PAIR)
    groups = span // lanes
    for s in range(count):

        @pl.loop(0, groups)
        def _(g, s=s):
            for p in range(lanes // PAIR):
                lane = pl.multiple_of(g * lanes + p * PAIR, PAIR)
                function(s, s * rows, lane, 2 * (g * (lanes // PAIR) + p))


def self_forward_kernel(
    tokens, mask, vectors, weight, query_weight, qkv, mixed, logs, unit, inverse, query, low
):
    step = pl.program_id(0)
    count, length, span = tokens.shape
    rows = padded(length)

    @pl.when(step == 0)
    def _():
        fill_tokens(low, tokens)

    @pl.when(step < 3)
    def _():
        product = dot_nn(low[...], weight[0])
        shift = jnp.where(
            step == 0, vectors[0:1], jnp.where(step == 2, vectors[1:2], jnp.zeros_like(vectors[0:1]))
        )
        product = (product + shift) * jnp.where(step == 0, SCALE, 1.0)
        qkv[step] = product.astype(LOW)

    @pl.when(step == 3)
    def _():
        logs[...] = jnp.zeros_like(logs)

        def pair(s, row, lane, head):
            allowed = causal_allowed(rows, mask[s : s + 1])
            where = (pl.ds(row, rows), pl.ds(lane, PAIR))
            both, sums = attend_pair(qkv[(0,) + where], qkv[(1,) + where], qkv[(2,) + where], allowed)
            mixed[where] = both
            table = logs[row : row + rows]
            spot = lax.broadcasted_iota(jnp.int32, table.shape, 1)
            for which in range(2):
                table = jnp.where(spot == head + which, sums[which], table)
            logs[row : row + rows] = table

        for_head_groups(count, rows, span, pair)
        hidden = low[...].astype(jnp.float32) + (dot_nn(mixed[...], weight[0]) + vectors[2:3])
        unit[...], inverse[...] = standardise(hidden)

    @pl.when(step == 4)
    def _():
        first_low = (unit[...] * vectors[3:4] + vectors[4:5]).astype(LOW)
        product = dot_nn(first_low, query_weight[0])
        query[...] = ((product + vectors[5:6]) * SCALE).astype(LOW)


def whole_spec(shape):
    return pl.BlockSpec(shape, lambda *at: (0,) * len(shape))


def params(**more):
    return pltpu.CompilerParams(vmem_limit_bytes=BUDGET, **more)


def self_forward(tokens, mask, vectors, self_full, cross_full):
    count, length, span = tokens.shape
    total = count * padded(length)
    outs = [
        jax.ShapeDtypeStruct((3, total, span), LOW),
        jax.ShapeDtypeStruct((total, span), LOW),
        jax.ShapeDtypeStruct((total, 128), jnp.float32),
        jax.ShapeDtypeStruct((total, span), jnp.float32),
        jax.ShapeDtypeStruct((total, 1), jnp.float32),
        jax.ShapeDtypeStruct((total, span), LOW),
    ]
    return pl.pallas_call(
        self_forward_kernel,
        grid=(5,),
        in_specs=[
            whole_spec(tokens.shape),
            whole_spec(mask.shape),
            whole_spec(vectors.shape),
            pl.BlockSpec((1, span, span), lambda i: (jnp.minimum(i, 3), 0, 0)),
            pl.BlockSpec((1, span, span), lambda i: (0, 0, 0)),
        ],
        out_specs=[whole_spec(out.shape) for out in outs],
        out_shape=outs,
        scratch_shapes=[pltpu.VMEM((total, span), LOW)],
        compiler_params=params(),
        name="self_forward",
    )(tokens, mask, vectors, self_full, cross_full)


def memory_forward(memory, cross_full, vectors):
    rows, span = memory.shape
    tile = min(rows, 512)

    def kernel(memory, key_weight, value_weight, vectors, keys, values):
        keys[...] = dot_nn(memory[...], key_weight[0]).astype(LOW)
        values[...] = (dot_nn(memory[...], value_weight[0]) + vectors[6:7]).astype(LOW)

    block = pl.BlockSpec((tile, span), lambda i: (i, 0))
    out = jax.ShapeDtypeStruct((rows, span), LOW)
    return pl.pallas_call(
        kernel,
        grid=(rows // tile,),
        in_specs=[
            block,
            pl.BlockSpec((1, span, span), lambda i: (1, 0, 0)),
            pl.BlockSpec((1, span, span), lambda i: (2, 0, 0)),
            whole_spec(vectors.shape),
        ],
        out_specs=[block, block],
        out_shape=[out, out],
        compiler_params=params(),
        name="memory_forward",
    )(memory, cross_full, cross_full, vectors)


CROSS_LANES = 2 * PAIR


def cross_forward(query, keys, values, lengths):
    count = lengths.shape[0]
    rows, slots, span = query.shape[0] // count, keys.shape[0] // count, query.shape[1]
    groups = span // CROSS_LANES

    def kernel(lengths, query, keys, values, mixed, logs):
        slot = lax.broadcasted_iota(jnp.int32, (1, slots), 1)
        allowed = slot < lengths[pl.program_id(0)]
        table = jnp.zeros(logs.shape[1:], jnp.float32)
        spot = lax.broadcasted_iota(jnp.int32, table.shape, 1)
        for p in range(CROSS_LANES // PAIR):
            where = pl.ds(p * PAIR, PAIR)
            both, sums = attend_pair(query[:, where], keys[:, where], values[:, where], allowed)
            mixed[:, where] = both
            for which in range(2):
                table = jnp.where(spot == 2 * p + which, sums[which], table)
        logs[0] = table

    token = pl.BlockSpec((rows, CROSS_LANES), lambda s, g: (s, g))
    stored = pl.BlockSpec((slots, CROSS_LANES), lambda s, g: (s, g))
    return pl.pallas_call(
        kernel,
        grid=(count, groups),
        in_specs=[pl.BlockSpec(memory_space=pltpu.SMEM), token, stored, stored],
        out_specs=[token, pl.BlockSpec((1, rows, 128), lambda s, g: (s * groups + g, 0, 0))],
        out_shape=[
            jax.ShapeDtypeStruct(query.shape, LOW),
            jax.ShapeDtypeStruct((count * groups, rows, 128), jnp.float32),
        ],
        compiler_params=params(),
        name="cross_forward",
    )(lengths, query, keys, values)


def feed_forward_kernel(
    tiles,
    mixed,
    out_weight,
    unit_one,
    vectors,
    bias,
    up,
    down,
    cotangent,
    hidden,
    slope,
    output,
    unit_two,
    inverse_two,
    grad_three,
    sums,
    second,
    low,
    total,
):
    step = pl.program_id(0)

    @pl.when(step == 0)
    def _():
        first = unit_one[...] * vectors[3:4] + vectors[4:5]
        unit, inverse_two[...] = standardise(
            first + (dot_nn(mixed[...], out_weight[0]) + vectors[7:8])
        )
        unit_two[...] = unit
        second[...] = unit * vectors[8:9] + vectors[9:10]
        low[...] = second[...].astype(LOW)
        total[...] = jnp.zeros_like(total)

    inner = dot_nn(low[...], up[0]) + bias[...]
    half = 0.5 + 0.5 * lax.erf(inner * (0.5**0.5))
    bell = jnp.exp(-0.5 * inner * inner) * ((0.5 / math.pi) ** 0.5)
    active = (inner * half).astype(LOW)
    hidden[...] = active
    slope[...] = (half + inner * bell).astype(LOW)
    total[...] += dot_nt(active, down[0])

    @pl.when(step == tiles - 1)
    def _():
        unit, inverse = standardise(second[...] + (total[...] + vectors[10:11]))
        store_tokens(output, unit * vectors[11:12] + vectors[12:13])
        fill_tokens(total, cotangent)
        grad = total[...]
        down_grad = norm_back(grad, unit, inverse, vectors[11:12])
        grad_three[...] = down_grad
        sums[...] = jnp.zeros_like(sums)
        sums[0:1] = column_sum(down_grad.astype(LOW))
        sums[1:2] = column_sum(grad * unit)
        sums[2:3] = column_sum(grad)


FEED_TILE = 512


def feed_forward(mixed, cross_full, unit_one, vectors, bias, feed_full, cotangent):
    total, span = mixed.shape
    width = feed_full.shape[2]
    tiles = width // FEED_TILE
    tile = pl.BlockSpec((total, FEED_TILE), lambda j: (0, j))
    outs = [
        jax.ShapeDtypeStruct((total, width), LOW),
        jax.ShapeDtypeStruct((total, width), LOW),
        jax.ShapeDtypeStruct(cotangent.shape, LOW),
        jax.ShapeDtypeStruct((total, span), jnp.float32),
        jax.ShapeDtypeStruct((total, 1), jnp.float32),
        jax.ShapeDtypeStruct((total, span), jnp.float32),
        jax.ShapeDtypeStruct((8, span), jnp.float32),
    ]
    return pl.pallas_call(
        functools.partial(feed_forward_kernel, tiles),
        grid=(tiles,),
        in_specs=[
            whole_spec(mixed.shape),
            pl.BlockSpec((1, span, span), lambda j: (3, 0, 0)),
            whole_spec(unit_one.shape),
            whole_spec(vectors.shape),
            pl.BlockSpec((1, FEED_TILE), lambda j: (0, j)),
            pl.BlockSpec((1, span, FEED_TILE), lambda j: (0, 0, j)),
            pl.BlockSpec((1, span, FEED_TILE), lambda j: (1, 0, j)),
            whole_spec(cotangent.shape),
        ],
        out_specs=[tile, tile] + [whole_spec(out.shape) for out in outs[2:]],
        out_shape=outs,
        scratch_shapes=[
            pltpu.VMEM((total, span), jnp.float32),
            pltpu.VMEM((total, span), LOW),
            pltpu.VMEM((total, span), jnp.float32),
        ],
        compiler_params=params(),
        name="feed_forward",
    )(mixed, cross_full, unit_one, vectors, bias, feed_full, feed_full, cotangent)


def feed_backward_kernel(
    tiles,
    grad_three,
    unit_two,
    inverse_two,
    vectors,
    hidden,
    slope,
    up,
    down,
    out_weight,
    mixed,
    feed_grad,
    bias_grad,
    grad_two,
    grad_mixed,
    out_grad,
    sums,
    low,
    branch,
    total,
):
    step = pl.program_id(0)

    @pl.when(step == 0)
    def _():
        low[...] = (unit_two[...] * vectors[8:9] + vectors[9:10]).astype(LOW)
        branch[...] = grad_three[...].astype(LOW)
        total[...] = grad_three[...]

    grad_inner = (slope[...].astype(jnp.float32) * dot_nn(branch[...], down[0])).astype(LOW)
    feed_grad[0] = dot_tn(low[...], grad_inner).astype(LOW)
    feed_grad[1] = dot_tn(branch[...], hidden[...]).astype(LOW)
    bias_grad[...] = column_sum(grad_inner)
    total[...] += dot_nt(grad_inner, up[0])

    @pl.when(step == tiles - 1)
    def _():
        grad = total[...]
        unit = unit_two[...]
        down_grad = norm_back(grad, unit, inverse_two[...], vectors[8:9])
        grad_two[...] = down_grad
        grad_low = down_grad.astype(LOW)
        sums[...] = jnp.zeros_like(sums)
        sums[0:1] = column_sum(grad_low)
        sums[1:2] = column_sum(grad * unit)
        sums[2:3] = column_sum(grad)
        grad_mixed[...] = dot_nt(grad_low, out_weight[0]).astype(LOW)
        out_grad[...] = dot_tn(mixed[...], grad_low).astype(LOW)


def feed_backward(grad_three, unit_two, inverse_two, vectors, hidden, slope, feed_full, cross_full, mixed):
    total, span = mixed.shape
    width = feed_full.shape[2]
    tiles = width // FEED_TILE
    tile = pl.BlockSpec((total, FEED_TILE), lambda j: (0, j))
    outs = [
        jax.ShapeDtypeStruct((2, span, width), LOW),
        jax.ShapeDtypeStruct((1, width), jnp.float32),
        jax.ShapeDtypeStruct((total, span), jnp.float32),
        jax.ShapeDtypeStruct((total, span), LOW),
        jax.ShapeDtypeStruct((span, span), LOW),
        jax.ShapeDtypeStruct((8, span), jnp.float32),
    ]
    return pl.pallas_call(
        functools.partial(feed_backward_kernel, tiles),
        grid=(tiles,),
        in_specs=[
            whole_spec(grad_three.shape),
            whole_spec(unit_two.shape),
            whole_spec(inverse_two.shape),
            whole_spec(vectors.shape),
            tile,
            tile,
            pl.BlockSpec((1, span, FEED_TILE), lambda j: (0, 0, j)),
            pl.BlockSpec((1, span, FEED_TILE), lambda j: (1, 0, j)),
            pl.BlockSpec((1, span, span), lambda j: (3, 0, 0)),
            whole_spec(mixed.shape),
        ],
        out_specs=[
            pl.BlockSpec((2, span, FEED_TILE), lambda j: (0, 0, j)),
            pl.BlockSpec((1, FEED_TILE), lambda j: (0, j)),
        ]
        + [whole_spec(out.shape) for out in outs[2:]],
        out_shape=outs,
        scratch_shapes=[
            pltpu.VMEM((total, span), LOW),
            pltpu.VMEM((total, span), LOW),
            pltpu.VMEM((total, span), jnp.float32),
        ],
        compiler_params=params(),
        name="feed_backward",
    )(grad_three, unit_two, inverse_two, vectors, hidden, slope, feed_full, feed_full, cross_full, mixed)


def cross_backward(
    reduction, query, keys, values, lengths, logs, grad_mixed, memory, cross_full, collective_id
):
    count = lengths.shape[0]
    rows, slots, span = query.shape[0] // count, keys.shape[0] // count, query.shape[1]
    groups = span // CROSS_LANES
    heads_steps = count * groups
    tiles = 4
    tile_rows, tile_lanes = keys.shape[0] // tiles, span // tiles
    last = heads_steps + tiles - 1
    carried, produced = len(reduction.operands()), len(reduction.outs())

    def kernel(*refs):
        lengths, query, keys, values, logs, grad, memory, key_weight, value_weight = refs[:9]
        operands, refs = refs[9 : 9 + carried], refs[9 + carried :]
        grad_query, sums, memory_grad, weight_grad = refs[:4]
        results, refs = refs[4 : 4 + produced], refs[4 + produced :]
        stored, scratch = refs[0], refs[1:]
        step = pl.program_id(0)
        rounds = reduction.rounds(operands, results, scratch)
        starts = list(range(0, heads_steps, 2)) + list(range(heads_steps, last + 1))
        for number, start in enumerate(starts):

            @pl.when(step == start)
            def _():
                if number == 0:
                    reduction.greet()
                rounds.run(1)

        @pl.when(step < heads_steps)
        def _():
            s, g = step // groups, step % groups
            slot = lax.broadcasted_iota(jnp.int32, (1, slots), 1)
            allowed = slot < lengths[s]
            sums[...] = jnp.zeros_like(sums)
            at = pl.ds(pl.multiple_of(s * slots, 16), slots)
            for p in range(CROSS_LANES // PAIR):
                where = pl.ds(p * PAIR, PAIR)
                columns = [pick_column(logs[0], 2 * p + which) for which in range(2)]
                found = attend_pair_back(
                    query[:, where], keys[:, where], values[:, where], allowed, columns, grad[:, where]
                )
                lanes = pl.ds(pl.multiple_of(g * CROSS_LANES + p * PAIR, PAIR), PAIR)
                grad_query[:, where] = found[0]
                stored[0, at, lanes], stored[1, at, lanes] = found[1:]
                sums[0, 0:1, where] = column_sum(found[0])
                sums[0, 1:2, where] = column_sum(found[2])

        @pl.when(step >= heads_steps)
        def _():
            t = step - heads_steps
            at = pl.ds(pl.multiple_of(t * tile_rows, 16), tile_rows)
            lanes = pl.ds(pl.multiple_of(t * tile_lanes, 128), tile_lanes)
            memory_grad[...] = dot_nt(stored[0, at], key_weight[0]) + dot_nt(
                stored[1, at], value_weight[0]
            )
            for number in range(2):
                weight_grad[number] = dot_tn(memory[...], stored[number, :, lanes]).astype(LOW)

        @pl.when(step == last)
        def _():
            rounds.run()

    def head(i):
        return jnp.minimum(i, heads_steps - 1)

    def later(i):
        return jnp.maximum(i - heads_steps, 0)

    once = pl.Buffered(1)
    token = pl.BlockSpec((rows, CROSS_LANES), lambda i: (head(i) // groups, head(i) % groups))
    held = pl.BlockSpec((slots, CROSS_LANES), lambda i: (head(i) // groups, head(i) % groups))
    return pl.pallas_call(
        kernel,
        grid=(last + 1,),
        in_specs=[
            pl.BlockSpec(memory_space=pltpu.SMEM),
            token,
            held,
            held,
            pl.BlockSpec((1, rows, 128), lambda i: (head(i), 0, 0)),
            token,
            pl.BlockSpec(memory.shape, lambda i: (0, 0), pipeline_mode=once),
            pl.BlockSpec((1, span, span), lambda i: (1, 0, 0), pipeline_mode=once),
            pl.BlockSpec((1, span, span), lambda i: (2, 0, 0), pipeline_mode=once),
        ]
        + reduction.in_specs(),
        out_specs=[
            token,
            pl.BlockSpec((1, 8, CROSS_LANES), lambda i: (head(i) // groups, 0, head(i) % groups)),
            pl.BlockSpec((tile_rows, span), lambda i: (later(i), 0)),
            pl.BlockSpec((2, span, tile_lanes), lambda i: (0, 0, later(i))),
        ]
        + reduction.out_specs(),
        out_shape=[
            jax.ShapeDtypeStruct(query.shape, LOW),
            jax.ShapeDtypeStruct((count, 8, span), jnp.float32),
            jax.ShapeDtypeStruct(memory.shape, jnp.float32),
            jax.ShapeDtypeStruct((2, span, span), LOW),
        ]
        + reduction.outs(),
        scratch_shapes=[pltpu.VMEM((2,) + keys.shape, LOW)] + reduction.scratch(),
        compiler_params=params(collective_id=collective_id, has_side_effects=True),
        name="cross_backward",
    )(
        lengths, query, keys, values, logs, grad_mixed, memory, cross_full, cross_full,
        *reduction.operands(),
    )


def self_backward_kernel(
    reduction,
    tokens,
    mask,
    vectors,
    weight,
    query_weight,
    qkv,
    mixed,
    logs,
    unit,
    inverse,
    cross_query_grad,
    grad_two,
    cross_sums,
    feed_sums,
    out_sums,
    bias_grad,
    *refs,
):
    carried, produced = len(reduction.operands()), len(reduction.outs())
    operands, refs = refs[:carried], refs[carried:]
    query_grad, weight_grads, input_grad, terms = refs[:4]
    results, refs = refs[4 : 4 + produced], refs[4 + produced :]
    (low, grads, total), scratch = refs[:3], refs[3:]
    step = pl.program_id(0)
    count, length, span = tokens.shape
    rows = padded(length)
    rounds = reduction.rounds(operands, results, scratch)
    for number, many in enumerate((2, 1, 1, 2, 1)):

        @pl.when(step == number)
        def _():
            if number == 0:
                reduction.greet()
            rounds.run(many)

    @pl.when(step == 0)
    def _():
        fill_tokens(low, tokens)
        terms[...] = jnp.zeros_like(terms)
        first_low = (unit[...] * vectors[3:4] + vectors[4:5]).astype(LOW)
        query_grad[...] = (dot_tn(first_low, cross_query_grad[...]) * SCALE).astype(LOW)
        grad = grad_two[...] + dot_nt(cross_query_grad[...], query_weight[0]) * SCALE
        down_grad = norm_back(grad, unit[...], inverse[...], vectors[3:4])
        total[...] = down_grad
        terms[2:3] = column_sum(down_grad.astype(LOW))
        terms[3:4] = column_sum(grad * unit[...])
        terms[4:5] = column_sum(grad)
        spread = jnp.sum(cross_sums[...], axis=0)
        terms[5:6] = spread[0:1] * SCALE
        terms[6:7] = spread[1:2]
        terms[7:10] = out_sums[0:3]
        terms[10:13] = feed_sums[0:3]
        for k in range(bias_grad.shape[1] // span):
            terms[13 + k : 14 + k] = bias_grad[:, k * span : (k + 1) * span]

    @pl.when(step == 1)
    def _():
        grad_low = total[...].astype(LOW)
        weight_grads[0] = dot_tn(mixed[...], grad_low).astype(LOW)
        grads[0] = dot_nt(grad_low, weight[0]).astype(LOW)

        def pair(s, row, lane, head):
            allowed = causal_allowed(rows, mask[s : s + 1])
            where = (pl.ds(row, rows), pl.ds(lane, PAIR))
            table = logs[row : row + rows]
            columns = [pick_column(table, head + which) for which in range(2)]
            results = attend_pair_back(
                qkv[(0,) + where],
                qkv[(1,) + where],
                qkv[(2,) + where],
                allowed,
                columns,
                grads[(0,) + where],
            )
            for number in range(3):
                grads[(1 + number,) + where] = results[number]

        for_head_groups(count, rows, span, pair)
        terms[0:1] = column_sum(grads[1]) * SCALE
        terms[1:2] = column_sum(grads[3])

    @pl.when(step > 1)
    def _():
        factor = jnp.where(step == 2, SCALE, 1.0)
        part = grads[step - 1]
        weight_grads[0] = (dot_tn(low[...], part) * factor).astype(LOW)
        total[...] += dot_nt(part, weight[0]) * factor

    @pl.when(step == 4)
    def _():
        store_tokens(input_grad, total[...])
        rounds.run()


def self_backward(
    reduction, collective_id, tokens, mask, vectors, self_full, cross_full, saved, cross_query_grad, grad_two, cross_sums, feed_sums, out_sums, bias_grad
):
    count, length, span = tokens.shape
    qkv, mixed, logs, unit, inverse = saved
    total = mixed.shape[0]
    count_terms = 13 + bias_grad.shape[1] // span
    count_terms += -count_terms % 8
    outs = [
        jax.ShapeDtypeStruct((span, span), LOW),
        jax.ShapeDtypeStruct((4, span, span), LOW),
        jax.ShapeDtypeStruct(tokens.shape, jnp.float32),
        jax.ShapeDtypeStruct((count_terms, span), jnp.float32),
    ]

    def which(i):
        return jnp.where(i <= 1, 3, i - 2)

    operands = (
        tokens, mask, vectors, self_full, cross_full, qkv, mixed, logs, unit, inverse,
        cross_query_grad, grad_two, cross_sums, feed_sums, out_sums, bias_grad,
    )
    specs = [
        pl.BlockSpec(operand.shape, lambda i, n=operand.ndim: (0,) * n, pipeline_mode=pl.Buffered(1))
        for operand in operands
    ]
    specs[3] = pl.BlockSpec((1, span, span), lambda i: (which(i), 0, 0))
    specs[4] = pl.BlockSpec((1, span, span), lambda i: (0, 0, 0), pipeline_mode=pl.Buffered(1))
    return pl.pallas_call(
        functools.partial(self_backward_kernel, reduction),
        grid=(5,),
        in_specs=specs + reduction.in_specs(),
        out_specs=[
            whole_spec((span, span)),
            pl.BlockSpec((1, span, span), lambda i: (which(i), 0, 0)),
            whole_spec(tokens.shape),
            whole_spec((count_terms, span)),
        ]
        + reduction.out_specs(),
        out_shape=outs + reduction.outs(),
        scratch_shapes=[
            pltpu.VMEM((total, span), LOW),
            pltpu.VMEM((4, total, span), LOW),
            pltpu.VMEM((total, span), jnp.float32),
        ]
        + reduction.scratch(),
        compiler_params=params(collective_id=collective_id, has_side_effects=True),
        name="self_backward",
    )(*operands, *reduction.operands())


def per_device(
    wide,
    narrow,
    decoder_input,
    memory,
    decoder_mask,
    memory_length,
    self_weights,
    cross_weights,
    feed_weights,
    vectors,
    hidden_bias,
    cotangent,
):
    seq_count, seq_length, model_width = decoder_input.shape
    mem_span = memory.shape[1]
    memory_low = memory.reshape(seq_count * mem_span, model_width)
    (self_full, cross_full, feed_full), vector_all, bias_all = gather_weights(
        wide, narrow, (self_weights, cross_weights, feed_weights), vectors, hidden_bias, 1
    )
    qkv, self_mixed, self_logs, unit_one, inverse_one, cross_query = self_forward(
        decoder_input, decoder_mask, vector_all, self_full, cross_full
    )
    cross_keys, cross_values = memory_forward(memory_low, cross_full, vector_all)
    cross_mixed, cross_logs = cross_forward(cross_query, cross_keys, cross_values, memory_length)
    hidden, slope, layer_output, unit_two, inverse_two, grad_three, feed_sums = feed_forward(
        cross_mixed, cross_full, unit_one, vector_all, bias_all, feed_full, cotangent
    )
    feed_part, bias_part, grad_two, grad_cmixed, cross_out_grad, out_sums = feed_backward(
        grad_three, unit_two, inverse_two, vector_all, hidden, slope, feed_full, cross_full, cross_mixed
    )
    cross_gq, cross_sums, memory_grad, memory_parts, feed_grad = cross_backward(
        Reduction(wide, narrow, [feed_part], 4),
        cross_query,
        cross_keys,
        cross_values,
        memory_length,
        cross_logs,
        grad_cmixed,
        memory_low,
        cross_full,
        2,
    )
    cross_query_part, self_parts, input_grad, terms, most_cross = self_backward(
        Reduction(wide, narrow, [memory_parts, cross_out_grad[None]], 2),
        3,
        decoder_input,
        decoder_mask,
        vector_all,
        self_full,
        cross_full,
        (qkv, self_mixed, self_logs, unit_one, inverse_one),
        cross_gq,
        grad_two,
        cross_sums,
        feed_sums,
        out_sums,
        bias_part,
    )
    rest, totals = reduce_gradients(
        Reduction(wide, narrow, [self_parts, cross_query_part[None]], 2, terms), 4
    )
    self_weight_gradient = rest[:4]
    cross_grad = jnp.concatenate([rest[4:], most_cross])
    vector_total = totals[: vectors.shape[0]]
    bias_rows = bias_all.shape[1] // model_width
    bias_total = totals[vectors.shape[0] : vectors.shape[0] + bias_rows].reshape(1, -1)
    narrow_index = lax.axis_index("narrow")
    vectors_grad = lax.dynamic_slice_in_dim(
        vector_total, narrow_index * vectors.shape[1], vectors.shape[1], 1
    )
    hidden_bias_grad = lax.dynamic_slice_in_dim(
        bias_total, narrow_index * hidden_bias.shape[1], hidden_bias.shape[1], 1
    )
    return (
        layer_output,
        input_grad,
        memory_grad.reshape(seq_count, mem_span, model_width),
        self_weight_gradient,
        cross_grad,
        feed_grad,
        vectors_grad,
        hidden_bias_grad,
    )


def solution(mesh):
    placed = (
        P(("wide", "narrow"), None, None),
        P(("wide", "narrow"), None, None),
        P(("wide", "narrow"), None),
        P(("wide", "narrow")),
        P(None, "wide", "narrow"),
        P(None, "wide", "narrow"),
        P(None, "wide", "narrow"),
        P(None, "narrow"),
        P(None, "narrow"),
        P(("wide", "narrow"), None, None),
    )
    return jax.shard_map(
        functools.partial(per_device, mesh.shape["wide"], mesh.shape["narrow"]),
        mesh=mesh,
        in_specs=placed,
        out_specs=(
            P(("wide", "narrow"), None, None),
            P(("wide", "narrow"), None, None),
            P(("wide", "narrow"), None, None),
            P(None, "wide", "narrow"),
            P(None, "wide", "narrow"),
            P(None, "wide", "narrow"),
            P(None, "narrow"),
            P(None, "narrow"),
        ),
        check_vma=False,
    )
```

```python
import functools
import math

import jax
import jax.numpy as jnp
from jax import lax
from jax.experimental import pallas as pl
from jax.experimental.pallas import tpu as pltpu
from jax.sharding import PartitionSpec as P

HEADS = 16
HEAD_DIM = 64


MESH_ID = pl.DeviceIdType.MESH


class Position:
    def __init__(self, wide, narrow):
        self.sizes = {"line": wide // 4, "pair": 2, "core": 2, "column": narrow}

    def get(self, axis):
        if axis == "column":
            return lax.axis_index("narrow")
        index = lax.axis_index("wide")
        if axis == "core":
            return index % 2
        return (index // 2) % 2 if axis == "pair" else index // 4

    def device(self, **moved):
        spot = {name: moved.get(name, self.get(name)) for name in self.sizes}
        return (spot["line"] * 4 + spot["pair"] * 2 + spot["core"], spot["column"])


class Channels:
    def __init__(self, sends, recvs):
        self.sends, self.recvs, self.used = sends, recvs, 0

    def take(self):
        self.used += 1
        number = self.used - 1
        return lambda: (self.sends.at[number], self.recvs.at[number])


def remote(source, target, channel, device):
    return pltpu.make_async_remote_copy(
        src_ref=source,
        dst_ref=target,
        send_sem=channel()[0],
        recv_sem=channel()[1],
        device_id=device,
        device_id_type=MESH_ID,
    )


def flip(index, bit):
    return index + bit - 2 * bit * ((index // bit) % 2)


def peers(position, axis, distance):
    at = (position.get(axis) + distance) % position.sizes[axis]
    return at, position.device(**{axis: at})


def greet(position):
    barrier = pltpu.get_barrier_semaphore()
    expected = 0
    for axis, size in position.sizes.items():
        for distance in range(1, size):
            pl.semaphore_signal(
                barrier,
                inc=1,
                device_id=peers(position, axis, distance)[1],
                device_id_type=MESH_ID,
            )
            expected += 1
    pl.semaphore_wait(barrier, expected)


def advance(generator):
    return next(generator, "done") != "done"


class Rounds:
    def __init__(self, flows, live=()):
        self.waiting, self.live = list(flows), list(live)

    def run(self, start=0):
        self.live = self.live + self.waiting[:start]
        self.waiting = self.waiting[start:]
        self.live = [flow for flow in self.live if advance(flow)]

    def finish(self, together=2):
        while self.waiting or self.live:
            self.run(together)


def finish_sends(sent):
    for describe in sent:
        describe().wait_send()


def gather_axis(position, axis, channels, block, own, sent):
    arrivals = []
    for distance in range(1, position.sizes[axis]):
        channel = channels.take()

        def send(distance=distance, channel=channel):
            device = peers(position, axis, distance)[1]
            return remote(own(), block(position.get(axis)), channel, device)

        def arrival(distance=distance, channel=channel):
            came, device = peers(position, axis, -distance)
            return remote(block(came), block(came), channel, device)

        send().start()
        sent.append(send)
        arrivals.append(arrival)
    yield
    for arrival in arrivals:
        arrival().wait_recv()


def gather_flow(position, channels, local_sem, own, region, order):
    sent = []

    def place(done, axis=None, at=None):
        spot = {name: None if name in done else position.get(name) for name in position.sizes}
        if axis is not None:
            spot[axis] = at
        return region(**spot)

    def local():
        return pltpu.make_async_copy(own(), place(()), local_sem())

    local().start()
    for number, axis in enumerate(order):
        done = order[:number]

        def block(j, axis=axis, done=done):
            return place(done, axis, j)

        def source(block=block, axis=axis, first=number == 0):
            return own() if first else block(position.get(axis))

        yield from gather_axis(position, axis, channels, block, source, sent)
        if number == 0:
            local().wait()
    finish_sends(sent)


def whole(index):
    return slice(None) if index is None else index


def row_splits(rows, most):
    return max(1, min(most, rows // 16))


def flow_channels(wide, narrow):
    return 2 + (wide // 4 - 1) + (narrow - 1)


ORDER_A = ("line", "pair", "column", "core")
ORDER_B = ("line", "column", "pair", "core")


def gather_pieces(arrays):
    pieces = []
    for number, array in enumerate(arrays):
        matrices, rows, width = array.shape
        parts = row_splits(rows, 4) if matrices == 2 else 1
        for part in range(parts):
            for matrix in range(matrices):
                pieces.append((number, matrix, part, parts))
    return pieces


def gather_flows(position, channels, local_sems, pieces, blocks, fulls):
    flows = []
    for number, (array, matrix, part, parts) in enumerate(pieces):
        block_ref, full_ref = blocks[array], fulls[array]
        rows = block_ref.shape[1] // parts
        width = block_ref.shape[2]

        def region(
            line, pair, core, column, full_ref=full_ref, matrix=matrix, part=part, rows=rows, width=width
        ):
            columns = (
                slice(None)
                if column is None
                else pl.ds(pl.multiple_of(column * width, 128), width)
            )
            return full_ref.at[
                matrix, whole(line), whole(pair), whole(core), pl.ds(part * rows, rows), columns
            ]

        def own(block_ref=block_ref, matrix=matrix, part=part, rows=rows):
            return block_ref.at[matrix, pl.ds(part * rows, rows)]

        order = ORDER_A if number % 2 == 0 else ORDER_B
        flows.append(gather_flow(
                position, channels, lambda number=number: local_sems.at[number], own, region, order
            ))
    return flows


def column_flow(position, channels, sem, block_ref, full_ref):
    width = block_ref.shape[1]

    def region(column):
        return full_ref.at[:, pl.ds(pl.multiple_of(column * width, 128), width)]

    def local():
        return pltpu.make_async_copy(block_ref, region(position.get("column")), sem())

    sent = []
    local().start()
    yield from gather_axis(position, "column", channels, region, lambda: block_ref, sent)
    local().wait()
    finish_sends(sent)


def full_shape(wide, narrow, array):
    matrices, rows, width = array.shape
    return jax.ShapeDtypeStruct((matrices, wide // 4, 2, 2, rows, width * narrow), array.dtype)


class Gather:
    def __init__(self, wide, narrow, arrays, vectors=()):
        self.wide, self.narrow = wide, narrow
        self.arrays, self.vectors = list(arrays), list(vectors)
        self.pieces = gather_pieces(arrays)

    def operands(self):
        return self.arrays + self.vectors

    def in_specs(self):
        return [pl.BlockSpec(memory_space=pltpu.VMEM)] * len(self.operands())

    def wholes(self):
        return [(vector.shape[0], vector.shape[1] * self.narrow) for vector in self.vectors]

    def outs(self):
        outs = [full_shape(self.wide, self.narrow, array) for array in self.arrays]
        return outs + [jax.ShapeDtypeStruct(shape, jnp.float32) for shape in self.wholes()]

    def out_specs(self):
        specs = [pl.BlockSpec(memory_space=pl.ANY)] * len(self.arrays)
        return specs + [pl.BlockSpec(memory_space=pltpu.VMEM)] * len(self.vectors)

    def scratch(self):
        flows = len(self.pieces) + len(self.vectors)
        copies = flow_channels(self.wide, self.narrow) * flows
        return [
            pltpu.SemaphoreType.DMA((copies,)),
            pltpu.SemaphoreType.DMA((copies,)),
            pltpu.SemaphoreType.DMA((flows,)),
        ] + [pltpu.VMEM(shape, jnp.float32) for shape in self.wholes()]

    def rounds(self, operands, outs, scratch):
        position = Position(self.wide, self.narrow)
        channels = Channels(scratch[0], scratch[1])
        count, local_sems, wholes = len(self.arrays), scratch[2], scratch[3:]
        live = [
            column_flow(
                position,
                channels,
                lambda k=k: local_sems.at[len(self.pieces) + k],
                operands[count + k],
                wholes[k],
            )
            for k in range(len(self.vectors))
        ]
        flows = gather_flows(
            position, channels, local_sems, self.pieces, operands[:count], outs[:count]
        )
        return Rounds(flows, live), wholes

    def greet(self):
        greet(Position(self.wide, self.narrow))

    def join(self, results):
        count = len(self.arrays)
        fulls = [full.reshape(full.shape[0], -1, full.shape[-1]) for full in results[:count]]
        return fulls + list(results[count:])


def add_rows(target, parts):
    lead = target.shape[:-2]
    count = math.prod(lead)

    def add(spot):
        total = parts[0][spot].astype(jnp.float32)
        for part in parts[1:]:
            total = total + part[spot].astype(jnp.float32)
        target[spot] = total.astype(target.dtype)

    if count == 1:
        add((0,) * len(lead))
        return

    @pl.loop(0, count)
    def _(k):
        where = []
        for extent in reversed(lead):
            where.insert(0, k % extent)
            k = k // extent
        add(tuple(where))


def reduce_axis(position, axis, channels, local, slots, result, sent):
    size = position.sizes[axis]
    for distance in range(1, size):
        channel = channels.take()

        def send(distance=distance, channel=channel):
            at, device = peers(position, axis, distance)
            return remote(local(at), slots.at[distance - 1], channel, device)

        send().start()
        sent.append(send)
    yield
    for send in sent[1 - size :]:
        send().wait_recv()
    add_rows(
        result(), [local(position.get(axis))] + [slots.at[k] for k in range(size - 1)]
    )


def reduce_flow(position, channels, local_sem, loc, grads, result, buffers, order):
    first, mid, last, line_slots = buffers
    sent = []

    def own():
        return pltpu.make_async_copy(grads(position.get("core")), loc(), local_sem())

    def mine():
        return grads(position.get("core")) if loc is None else loc()

    channel = channels.take()

    def swap():
        core = position.get("core")
        return remote(grads(1 - core), first, channel, position.device(core=1 - core))

    if loc is not None:
        own().start()
    swap().start()
    sent.append(swap)
    yield
    if loc is not None:
        own().wait()
    swap().wait_recv()
    add_rows(first, [first, mine()])
    width = result().shape[-1]

    def columns(j):
        return pl.ds(pl.multiple_of(j * width, 128), width)

    def held():
        return mid.at[0]

    def final():
        return last.at[0]

    if order == "A":
        yield from reduce_axis(
            position, "column", channels, lambda j: first.at[:, :, :, columns(j)], mid, held, sent
        )
        yield from reduce_axis(position, "pair", channels, lambda j: held().at[:, j], last, final, sent)
    else:
        yield from reduce_axis(position, "pair", channels, lambda j: first.at[:, j], mid, held, sent)
        yield from reduce_axis(
            position, "column", channels, lambda j: held().at[:, :, columns(j)], last, final, sent
        )
    yield from reduce_axis(
        position, "line", channels, lambda j: final().at[pl.ds(j, 1)], line_slots, result, sent
    )
    finish_sends(sent)


def double_flow(position, channels, terms, total, inbox, vectors_out, bias_out):
    total[0] = terms[...]
    step = 0
    for axis in ("core", "pair", "line", "column"):
        bit = 1
        while bit < position.sizes[axis]:
            channel = channels.take()

            def describe():
                to = position.device(**{axis: flip(position.get(axis), bit)})
                return remote(total.at[step], inbox.at[step], channel, to)

            describe().start()
            yield
            describe().wait_recv()
            total[step + 1] = total[step] + inbox[step]
            describe().wait_send()
            bit *= 2
            step += 1
    column, span = position.get("column"), terms.shape[1]
    count, width = vectors_out.shape
    vectors_out[...] = total[step, 0:count, pl.ds(pl.multiple_of(column * width, 128), width)]
    width = bias_out.shape[1]
    part = min(width, span)
    for k in range(width // part):
        offset = column * width + k * part
        lanes = pl.ds(pl.multiple_of(offset % span, 128), part)
        bias_out[:, k * part : (k + 1) * part] = total[step, pl.ds(count + offset // span, 1), lanes]


class Reduction:
    RING = 4

    def __init__(self, wide, narrow, arrays, parts, held=0, places=None, shapes=()):
        self.wide, self.narrow, self.held, self.shapes = wide, narrow, held, list(shapes)
        depth, span = arrays[0].shape[1:]
        self.rows = rows = depth // wide
        self.parts = row_splits(rows, parts)
        self.piece = rows // self.parts
        self.line, self.span, self.width = wide // 4, span, span // narrow
        matrices = [(s, m) for s, array in enumerate(arrays) for m in range(array.shape[0])]
        matrices += [(None, m) for m in range(held)]
        self.places = places or [(0, m) for m in range(len(matrices))]
        self.pieces = [
            matrix + (part,) + place
            for matrix, place in zip(matrices, self.places)
            for part in range(self.parts)
        ]
        self.views = [array.reshape(array.shape[0], self.line, 2, 2, rows, span) for array in arrays]
        self.loaded = sum(array.shape[0] for array in arrays) * self.parts

    def order(self, number):
        return "A" if number % 2 == 0 else "B"

    def operands(self):
        return self.views

    def in_specs(self):
        return [pl.BlockSpec(memory_space=pl.ANY)] * len(self.views)

    def outs(self):
        outs = []
        for out in range(1 + max(out for out, _ in self.places)):
            count = sum(1 for place in self.places if place[0] == out)
            outs.append(jax.ShapeDtypeStruct((count, self.rows, self.width), jnp.float32))
        return outs + [jax.ShapeDtypeStruct(shape, jnp.float32) for shape in self.shapes]

    def out_specs(self):
        return [pl.BlockSpec(memory_space=pltpu.VMEM)] * len(self.outs())

    def steps(self):
        return (self.wide * self.narrow).bit_length() - 1

    def terms_shape(self):
        count = self.shapes[0][0] + self.shapes[1][1] * self.narrow // self.span
        return (count + -count % 8, self.span)

    def scratch(self):
        low, line, piece = jnp.bfloat16, self.line, self.piece
        copies = flow_channels(self.wide, self.narrow) * len(self.pieces) + 16
        shapes = [
            pltpu.SemaphoreType.DMA((copies,)),
            pltpu.SemaphoreType.DMA((copies,)),
            pltpu.SemaphoreType.DMA((len(self.pieces),)),
            pltpu.VMEM((self.RING, line, 2, piece, self.span), low),
        ]
        if self.held:
            shapes.append(pltpu.VMEM((self.held, line, 2, 2, self.rows, self.span), low))
        if self.shapes:
            shapes.append(pltpu.VMEM(self.terms_shape(), jnp.float32))
            shapes.append(pltpu.VMEM((self.steps() + 1,) + self.terms_shape(), jnp.float32))
            shapes.append(pltpu.VMEM((self.steps(),) + self.terms_shape(), jnp.float32))
        for number in range(len(self.pieces)):
            shapes.append(pltpu.VMEM((line, 2, piece, self.span), low))
            if self.order(number) == "A":
                shapes.append(pltpu.VMEM((self.narrow - 1, line, 2, piece, self.width), low))
                shapes.append(pltpu.VMEM((1, line, piece, self.width), low))
            else:
                shapes.append(pltpu.VMEM((1, line, piece, self.span), low))
                shapes.append(pltpu.VMEM((self.narrow - 1, line, piece, self.width), low))
            shapes.append(pltpu.VMEM((line - 1, 1, piece, self.width), low))
        return shapes

    def rounds(self, operands, outs, scratch):
        position = Position(self.wide, self.narrow)
        channels = Channels(scratch[0], scratch[1])
        local_sems, ring, buffers = scratch[2], scratch[3], list(scratch[4:])
        made = buffers.pop(0) if self.held else None
        terms, vector_flow = None, None
        if self.shapes:
            terms, total, inbox = buffers[:3]
            buffers = buffers[3:]
            vector_flow = double_flow(position, channels, terms, total, inbox, *outs[-2:])
        flows = []
        for number, (source, inner, part, out, matrix) in enumerate(self.pieces):
            at = pl.ds(part * self.piece, self.piece)

            def grads(core, source=source, inner=inner, at=at):
                array = made if source is None else operands[source]
                return array.at[inner, :, :, core, at]

            flows.append(
                reduce_flow(
                    position,
                    channels,
                    lambda number=number: local_sems.at[number],
                    None if source is None else lambda number=number: ring.at[number % self.RING],
                    grads,
                    lambda out=out, matrix=matrix, at=at: outs[out].at[pl.ds(matrix, 1), at],
                    buffers[4 * number : 4 * number + 4],
                    self.order(number),
                )
            )
        return Rounds(flows), made, terms, vector_flow

    def greet(self):
        greet(Position(self.wide, self.narrow))


LOW = jnp.bfloat16
NEGATIVE = -1000000000.0
EPSILON = 1e-05
PAIR = 2 * HEAD_DIM
SCALE = HEAD_DIM ** (-0.5)
BUDGET = 65000 * 1024


def dot_nn(left, right):
    return jnp.dot(left, right, preferred_element_type=jnp.float32)


def dot_nt(left, right):
    return lax.dot_general(
        left, right, (((1,), (1,)), ((), ())), preferred_element_type=jnp.float32
    )


def dot_tn(left, right):
    return lax.dot_general(
        left, right, (((0,), (0,)), ((), ())), preferred_element_type=jnp.float32
    )


def padded(length):
    return -(-length // 16) * 16


def column_sum(rows):
    return jnp.sum(rows.astype(jnp.float32), axis=0, keepdims=True)


def standardise(hidden):
    centre = hidden - jnp.mean(hidden, axis=-1, keepdims=True)
    spread = jnp.mean(centre * centre, axis=-1, keepdims=True)
    inverse = lax.rsqrt(spread + EPSILON)
    return centre * inverse, inverse


def norm_back(grad, unit, inverse, gain):
    scaled = grad * gain
    first = jnp.mean(scaled, axis=-1, keepdims=True)
    second = jnp.mean(scaled * unit, axis=-1, keepdims=True)
    return inverse * (scaled - first - unit * second)


def fill_tokens(target, source):
    count, length, span = source.shape
    rows = padded(length)
    for s in range(count):
        if rows > length:
            base = s * rows + length // 16 * 16
            target[base : (s + 1) * rows] = jnp.zeros(((s + 1) * rows - base, span), target.dtype)
        target[s * rows : s * rows + length] = source[s].astype(target.dtype)


def store_tokens(target, values):
    count, length, span = target.shape
    rows = padded(length)
    for s in range(count):
        target[s] = values[s * rows : s * rows + length].astype(target.dtype)


def head_lanes(rows, which):
    lane = lax.broadcasted_iota(jnp.int32, rows.shape, 1)
    return (lane >= HEAD_DIM) == (which == 1)


def one_head(rows, which):
    return jnp.where(head_lanes(rows, which), rows, jnp.zeros_like(rows))


def pick_column(table, number):
    lane = lax.broadcasted_iota(jnp.int32, table.shape, 1)
    return jnp.sum(jnp.where(lane == number, table, 0.0), axis=1, keepdims=True)


def attend_pair(query, keys, values, allowed):
    mixed, logs = [], []
    for which in range(2):
        scores = dot_nt(one_head(query, which), keys)
        scores = jnp.where(allowed, scores, NEGATIVE)
        peak = jnp.max(scores, axis=-1, keepdims=True)
        expo = jnp.exp(scores - peak)
        total = jnp.sum(expo, axis=-1, keepdims=True)
        weights = (expo * (1.0 / total)).astype(LOW)
        mixed.append(dot_nn(weights, values))
        logs.append(peak + jnp.log(total))
    both = jnp.where(head_lanes(mixed[0], 0), mixed[0], mixed[1])
    return both.astype(LOW), logs


def attend_pair_back(query, keys, values, allowed, logs, grad):
    grad_query, grad_keys, grad_values = [], None, None
    for which in range(2):
        query_one, grad_one = one_head(query, which), one_head(grad, which)
        scores = jnp.where(allowed, dot_nt(query_one, keys), NEGATIVE)
        probs = jnp.exp(scores - logs[which])
        grad_probs = dot_nt(grad_one, values)
        slope = jnp.sum(grad_probs * probs, axis=-1, keepdims=True)
        grad_scores = (probs * (grad_probs - slope)).astype(LOW)
        grad_query.append(dot_nn(grad_scores, keys))
        part_keys = dot_tn(grad_scores, query_one)
        part_values = dot_tn(probs.astype(LOW), grad_one)
        grad_keys = part_keys if which == 0 else grad_keys + part_keys
        grad_values = part_values if which == 0 else grad_values + part_values
    both = jnp.where(head_lanes(grad_query[0], 0), grad_query[0], grad_query[1])
    return both.astype(LOW), grad_keys.astype(LOW), grad_values.astype(LOW)


def causal_allowed(rows, mask_row):
    valid = jnp.sum(mask_row, axis=-1, keepdims=True)
    query_at = lax.broadcasted_iota(jnp.int32, (rows, rows), 0)
    key_at = lax.broadcasted_iota(jnp.int32, (rows, rows), 1)
    return (query_at >= key_at) & (key_at < valid)


def for_head_groups(span, function):
    lanes = min(span, 4 * PAIR)

    @pl.loop(0, span // lanes)
    def _(g):
        for p in range(lanes // PAIR):
            function(pl.multiple_of(g * lanes + p * PAIR, PAIR), 2 * (g * (lanes // PAIR) + p))


def whole_spec(shape):
    return pl.BlockSpec(shape, lambda *at: (0,) * len(shape))


def params(**more):
    return pltpu.CompilerParams(vmem_limit_bytes=BUDGET, **more)


CROSS_LANES = 2 * PAIR


def once_spec(shape):
    return pl.BlockSpec(shape, lambda *at: (0,) * len(shape), pipeline_mode=pl.Buffered(1))


def front(load, tokens, mask, lengths, memory, collective_id):
    count, length, span = tokens.shape
    rows = padded(length)
    total, slots = count * rows, memory.shape[0] // count
    tiles = 4
    tile = memory.shape[0] // tiles
    groups = span // CROSS_LANES
    attend, join, ask = 3, 3 + count, 4 + count
    recall = ask + 1
    look = recall + tiles
    last = look + count * groups - 1
    carried = len(load.operands())
    plan = {
        0: (2, 2, 2, 2, 2),
        2: (2,),
        ask: (2,),
        recall: (2,),
        look: (0,),
        look + count * groups // 2: (0,),
    }

    def kernel(*refs):
        tokens, mask, lengths, memory = refs[:4]
        operands, refs = refs[4 : 4 + carried], refs[4 + carried :]
        (qkv, mixed, logs, unit, inverse, query, keys, values, cross_mixed, cross_logs) = refs[:10]
        results, refs = refs[10 : 10 + carried], refs[10 + carried :]
        low, weights, weight_sem, scratch = refs[0], refs[1], refs[2], refs[3:]
        step = pl.program_id(0)
        rounds, (vectors, bias) = load.rounds(operands, results, scratch)
        for start, begins in plan.items():

            @pl.when(step == start)
            def _():
                if start == 0:
                    load.greet()
                for begin in begins:
                    rounds.run(begin)

        def fetch(array, matrix, slot):
            copy = pltpu.make_async_copy(results[array].at[matrix], weights.at[slot], weight_sem)
            copy.start()
            copy.wait()

        def weight(slot):
            return weights[slot].reshape(span, span)

        @pl.when(step == 0)
        def _():
            fill_tokens(low, tokens)

        @pl.when(step < attend)
        def _():
            fetch(0, step, 0)
            product = dot_nn(low[...], weight(0))
            none = jnp.zeros_like(vectors[0:1])
            shift = jnp.where(step == 0, vectors[0:1], jnp.where(step == 2, vectors[1:2], none))
            product = (product + shift) * jnp.where(step == 0, SCALE, 1.0)
            qkv[step] = product.astype(LOW)

        for s in range(count):

            @pl.when(step == attend + s)
            def _():
                allowed = causal_allowed(rows, mask[s : s + 1])
                table_at = slice(s * rows, (s + 1) * rows)
                logs[table_at] = jnp.zeros((rows, 128), jnp.float32)

                def pair(lane, head):
                    where = (table_at, pl.ds(lane, PAIR))
                    both, sums = attend_pair(
                        qkv[(0,) + where], qkv[(1,) + where], qkv[(2,) + where], allowed
                    )
                    mixed[where] = both
                    table = logs[table_at]
                    spot = lax.broadcasted_iota(jnp.int32, table.shape, 1)
                    for which in range(2):
                        table = jnp.where(spot == head + which, sums[which], table)
                    logs[table_at] = table

                for_head_groups(span, pair)

        @pl.when(step == join)
        def _():
            fetch(0, 3, 0)
            hidden = low[...].astype(jnp.float32) + (dot_nn(mixed[...], weight(0)) + vectors[2:3])
            unit[...], inverse[...] = standardise(hidden)

        @pl.when(step == ask)
        def _():
            first_low = (unit[...] * vectors[3:4] + vectors[4:5]).astype(LOW)
            fetch(1, 0, 0)
            product = dot_nn(first_low, weight(0))
            query[...] = ((product + vectors[5:6]) * SCALE).astype(LOW)

        @pl.when(step == recall)
        def _():
            fetch(1, 1, 0)
            fetch(1, 2, 1)

        @pl.when((step >= recall) & (step < look))
        def _():
            at = pl.ds(pl.multiple_of((step - recall) * tile, 16), tile)
            keys[at] = dot_nn(memory[...], weight(0)).astype(LOW)
            values[at] = (dot_nn(memory[...], weight(1)) + vectors[6:7]).astype(LOW)

        @pl.when(step >= look)
        def _():
            s, g = (step - look) // groups, (step - look) % groups
            slot = lax.broadcasted_iota(jnp.int32, (1, slots), 1)
            allowed = slot < lengths[s]
            token_at = pl.ds(pl.multiple_of(s * rows, 16), rows)
            slot_at = pl.ds(pl.multiple_of(s * slots, 16), slots)
            table = jnp.zeros(cross_logs.shape[1:], jnp.float32)
            spot = lax.broadcasted_iota(jnp.int32, table.shape, 1)
            for p in range(CROSS_LANES // PAIR):
                lanes = pl.ds(pl.multiple_of(g * CROSS_LANES + p * PAIR, PAIR), PAIR)
                both, sums = attend_pair(
                    query[token_at, lanes], keys[slot_at, lanes], values[slot_at, lanes], allowed
                )
                cross_mixed[token_at, lanes] = both
                for which in range(2):
                    table = jnp.where(spot == 2 * p + which, sums[which], table)
            cross_logs[0] = table

        @pl.when(step == last)
        def _():
            rounds.finish()
            results[-2][...] = vectors[...]
            results[-1][...] = bias[...]

    outs = [
        jax.ShapeDtypeStruct((3, total, span), LOW),
        jax.ShapeDtypeStruct((total, span), LOW),
        jax.ShapeDtypeStruct((total, 128), jnp.float32),
        jax.ShapeDtypeStruct((total, span), jnp.float32),
        jax.ShapeDtypeStruct((total, 1), jnp.float32),
        jax.ShapeDtypeStruct((total, span), LOW),
        jax.ShapeDtypeStruct(memory.shape, LOW),
        jax.ShapeDtypeStruct(memory.shape, LOW),
        jax.ShapeDtypeStruct((total, span), LOW),
        jax.ShapeDtypeStruct((count * groups, rows, 128), jnp.float32),
    ]

    results = pl.pallas_call(
        kernel,
        grid=(last + 1,),
        in_specs=[
            once_spec(tokens.shape),
            once_spec(mask.shape),
            pl.BlockSpec(memory_space=pltpu.SMEM),
            pl.BlockSpec((tile, span), lambda i: (jnp.clip(i - recall, 0, tiles - 1), 0)),
        ]
        + load.in_specs(),
        out_specs=[once_spec(out.shape) for out in outs[:-1]]
        + [pl.BlockSpec((1, rows, 128), lambda i: (jnp.maximum(i - look, 0), 0, 0))]
        + load.out_specs(),
        out_shape=outs + load.outs(),
        scratch_shapes=[
            pltpu.VMEM((total, span), LOW),
            pltpu.VMEM((2,) + load.outs()[0].shape[1:], LOW),
            pltpu.SemaphoreType.DMA,
        ]
        + load.scratch(),
        compiler_params=params(collective_id=collective_id, has_side_effects=True),
        name="front",
    )(tokens, mask, lengths, memory, *load.operands())
    return results[: len(outs)], load.join(results[len(outs) :])


def feed_forward_kernel(
    tiles,
    mixed,
    out_weight,
    unit_one,
    vectors,
    bias,
    up,
    down,
    cotangent,
    hidden,
    slope,
    output,
    unit_two,
    inverse_two,
    grad_three,
    sums,
    second,
    low,
    total,
):
    step = pl.program_id(0)

    @pl.when(step == 0)
    def _():
        first = unit_one[...] * vectors[3:4] + vectors[4:5]
        unit, inverse_two[...] = standardise(
            first + (dot_nn(mixed[...], out_weight[0]) + vectors[7:8])
        )
        unit_two[...] = unit
        second[...] = unit * vectors[8:9] + vectors[9:10]
        low[...] = second[...].astype(LOW)
        total[...] = jnp.zeros_like(total)

    inner = dot_nn(low[...], up[0]) + bias[...]
    half = 0.5 + 0.5 * lax.erf(inner * (0.5**0.5))
    bell = jnp.exp(-0.5 * inner * inner) * ((0.5 / math.pi) ** 0.5)
    active = (inner * half).astype(LOW)
    hidden[...] = active
    slope[...] = (half + inner * bell).astype(LOW)
    total[...] += dot_nt(active, down[0])

    @pl.when(step == tiles - 1)
    def _():
        unit, inverse = standardise(second[...] + (total[...] + vectors[10:11]))
        store_tokens(output, unit * vectors[11:12] + vectors[12:13])
        fill_tokens(total, cotangent)
        grad = total[...]
        down_grad = norm_back(grad, unit, inverse, vectors[11:12])
        grad_three[...] = down_grad
        sums[...] = jnp.zeros_like(sums)
        sums[0:1] = column_sum(down_grad.astype(LOW))
        sums[1:2] = column_sum(grad * unit)
        sums[2:3] = column_sum(grad)


FEED_TILE = 512


def feed_forward(mixed, cross_full, unit_one, vectors, bias, feed_full, cotangent):
    total, span = mixed.shape
    width = feed_full.shape[2]
    tiles = width // FEED_TILE
    tile = pl.BlockSpec((total, FEED_TILE), lambda j: (0, j))
    outs = [
        jax.ShapeDtypeStruct((total, width), LOW),
        jax.ShapeDtypeStruct((total, width), LOW),
        jax.ShapeDtypeStruct(cotangent.shape, LOW),
        jax.ShapeDtypeStruct((total, span), jnp.float32),
        jax.ShapeDtypeStruct((total, 1), jnp.float32),
        jax.ShapeDtypeStruct((total, span), jnp.float32),
        jax.ShapeDtypeStruct((8, span), jnp.float32),
    ]
    return pl.pallas_call(
        functools.partial(feed_forward_kernel, tiles),
        grid=(tiles,),
        in_specs=[
            whole_spec(mixed.shape),
            pl.BlockSpec((1, span, span), lambda j: (3, 0, 0)),
            whole_spec(unit_one.shape),
            whole_spec(vectors.shape),
            pl.BlockSpec((1, FEED_TILE), lambda j: (0, j)),
            pl.BlockSpec((1, span, FEED_TILE), lambda j: (0, 0, j)),
            pl.BlockSpec((1, span, FEED_TILE), lambda j: (1, 0, j)),
            whole_spec(cotangent.shape),
        ],
        out_specs=[tile, tile] + [whole_spec(out.shape) for out in outs[2:]],
        out_shape=outs,
        scratch_shapes=[
            pltpu.VMEM((total, span), jnp.float32),
            pltpu.VMEM((total, span), LOW),
            pltpu.VMEM((total, span), jnp.float32),
        ],
        compiler_params=params(),
        name="feed_forward",
    )(mixed, cross_full, unit_one, vectors, bias, feed_full, feed_full, cotangent)


def feed_backward_kernel(
    tiles,
    grad_three,
    unit_two,
    inverse_two,
    vectors,
    hidden,
    slope,
    up,
    down,
    out_weight,
    mixed,
    feed_grad,
    bias_grad,
    grad_two,
    grad_mixed,
    out_grad,
    sums,
    low,
    branch,
    total,
):
    step = pl.program_id(0)

    @pl.when(step == 0)
    def _():
        low[...] = (unit_two[...] * vectors[8:9] + vectors[9:10]).astype(LOW)
        branch[...] = grad_three[...].astype(LOW)
        total[...] = grad_three[...]

    grad_inner = (slope[...].astype(jnp.float32) * dot_nn(branch[...], down[0])).astype(LOW)
    feed_grad[0] = dot_tn(low[...], grad_inner).astype(LOW)
    feed_grad[1] = dot_tn(branch[...], hidden[...]).astype(LOW)
    bias_grad[...] = column_sum(grad_inner)
    total[...] += dot_nt(grad_inner, up[0])

    @pl.when(step == tiles - 1)
    def _():
        grad = total[...]
        unit = unit_two[...]
        down_grad = norm_back(grad, unit, inverse_two[...], vectors[8:9])
        grad_two[...] = down_grad
        grad_low = down_grad.astype(LOW)
        sums[...] = jnp.zeros_like(sums)
        sums[0:1] = column_sum(grad_low)
        sums[1:2] = column_sum(grad * unit)
        sums[2:3] = column_sum(grad)
        grad_mixed[...] = dot_nt(grad_low, out_weight[0]).astype(LOW)
        out_grad[...] = dot_tn(mixed[...], grad_low).astype(LOW)


def feed_backward(grad_three, unit_two, inverse_two, vectors, hidden, slope, feed_full, cross_full, mixed):
    total, span = mixed.shape
    width = feed_full.shape[2]
    tiles = width // FEED_TILE
    tile = pl.BlockSpec((total, FEED_TILE), lambda j: (0, j))
    outs = [
        jax.ShapeDtypeStruct((2, span, width), LOW),
        jax.ShapeDtypeStruct((1, width), jnp.float32),
        jax.ShapeDtypeStruct((total, span), jnp.float32),
        jax.ShapeDtypeStruct((total, span), LOW),
        jax.ShapeDtypeStruct((span, span), LOW),
        jax.ShapeDtypeStruct((8, span), jnp.float32),
    ]
    return pl.pallas_call(
        functools.partial(feed_backward_kernel, tiles),
        grid=(tiles,),
        in_specs=[
            whole_spec(grad_three.shape),
            whole_spec(unit_two.shape),
            whole_spec(inverse_two.shape),
            whole_spec(vectors.shape),
            tile,
            tile,
            pl.BlockSpec((1, span, FEED_TILE), lambda j: (0, 0, j)),
            pl.BlockSpec((1, span, FEED_TILE), lambda j: (1, 0, j)),
            pl.BlockSpec((1, span, span), lambda j: (3, 0, 0)),
            whole_spec(mixed.shape),
        ],
        out_specs=[
            pl.BlockSpec((2, span, FEED_TILE), lambda j: (0, 0, j)),
            pl.BlockSpec((1, FEED_TILE), lambda j: (0, j)),
        ]
        + [whole_spec(out.shape) for out in outs[2:]],
        out_shape=outs,
        scratch_shapes=[
            pltpu.VMEM((total, span), LOW),
            pltpu.VMEM((total, span), LOW),
            pltpu.VMEM((total, span), jnp.float32),
        ],
        compiler_params=params(),
        name="feed_backward",
    )(grad_three, unit_two, inverse_two, vectors, hidden, slope, feed_full, feed_full, cross_full, mixed)


def cross_backward(
    reduction, query, keys, values, lengths, logs, grad_mixed, memory, cross_full, collective_id
):
    count = lengths.shape[0]
    rows, slots, span = query.shape[0] // count, keys.shape[0] // count, query.shape[1]
    groups = span // CROSS_LANES
    heads_steps = count * groups
    tiles = 4
    tile_rows, tile_lanes = keys.shape[0] // tiles, span // tiles
    last = heads_steps + tiles - 1
    carried, produced = len(reduction.operands()), len(reduction.outs())

    def kernel(*refs):
        lengths, query, keys, values, logs, grad, memory, key_weight, value_weight = refs[:9]
        operands, refs = refs[9 : 9 + carried], refs[9 + carried :]
        grad_query, sums, memory_grad, weight_grad = refs[:4]
        results, refs = refs[4 : 4 + produced], refs[4 + produced :]
        stored, scratch = refs[0], refs[1:]
        step = pl.program_id(0)
        rounds = reduction.rounds(operands, results, scratch)[0]
        plan = {0: (2,), 1: (2,), 4: (2,), 7: (2,), 9: (0,), 10: (0,), 11: (0,)}
        for start, begins in plan.items():

            @pl.when(step == start)
            def _():
                if start == 0:
                    reduction.greet()
                for begin in begins:
                    rounds.run(begin)

        @pl.when(step < heads_steps)
        def _():
            s, g = step // groups, step % groups
            slot = lax.broadcasted_iota(jnp.int32, (1, slots), 1)
            allowed = slot < lengths[s]
            sums[...] = jnp.zeros_like(sums)
            at = pl.ds(pl.multiple_of(s * slots, 16), slots)
            for p in range(CROSS_LANES // PAIR):
                where = pl.ds(p * PAIR, PAIR)
                columns = [pick_column(logs[0], 2 * p + which) for which in range(2)]
                found = attend_pair_back(
                    query[:, where], keys[:, where], values[:, where], allowed, columns, grad[:, where]
                )
                lanes = pl.ds(pl.multiple_of(g * CROSS_LANES + p * PAIR, PAIR), PAIR)
                grad_query[:, where] = found[0]
                stored[0, at, lanes], stored[1, at, lanes] = found[1:]
                sums[0, 0:1, where] = column_sum(found[0])
                sums[0, 1:2, where] = column_sum(found[2])

        @pl.when(step >= heads_steps)
        def _():
            t = step - heads_steps
            at = pl.ds(pl.multiple_of(t * tile_rows, 16), tile_rows)
            lanes = pl.ds(pl.multiple_of(t * tile_lanes, 128), tile_lanes)
            memory_grad[...] = dot_nt(stored[0, at], key_weight[0]) + dot_nt(
                stored[1, at], value_weight[0]
            )
            for number in range(2):
                weight_grad[number] = dot_tn(memory[...], stored[number, :, lanes]).astype(LOW)

        @pl.when(step == last)
        def _():
            rounds.finish()

    def head(i):
        return jnp.minimum(i, heads_steps - 1)

    def later(i):
        return jnp.maximum(i - heads_steps, 0)

    once = pl.Buffered(1)
    token = pl.BlockSpec((rows, CROSS_LANES), lambda i: (head(i) // groups, head(i) % groups))
    held = pl.BlockSpec((slots, CROSS_LANES), lambda i: (head(i) // groups, head(i) % groups))
    return pl.pallas_call(
        kernel,
        grid=(last + 1,),
        in_specs=[
            pl.BlockSpec(memory_space=pltpu.SMEM),
            token,
            held,
            held,
            pl.BlockSpec((1, rows, 128), lambda i: (head(i), 0, 0)),
            token,
            pl.BlockSpec(memory.shape, lambda i: (0, 0), pipeline_mode=once),
            pl.BlockSpec((1, span, span), lambda i: (1, 0, 0), pipeline_mode=once),
            pl.BlockSpec((1, span, span), lambda i: (2, 0, 0), pipeline_mode=once),
        ]
        + reduction.in_specs(),
        out_specs=[
            token,
            pl.BlockSpec((1, 8, CROSS_LANES), lambda i: (head(i) // groups, 0, head(i) % groups)),
            pl.BlockSpec((tile_rows, span), lambda i: (later(i), 0)),
            pl.BlockSpec((2, span, tile_lanes), lambda i: (0, 0, later(i))),
        ]
        + reduction.out_specs(),
        out_shape=[
            jax.ShapeDtypeStruct(query.shape, LOW),
            jax.ShapeDtypeStruct((count, 8, span), jnp.float32),
            jax.ShapeDtypeStruct(memory.shape, jnp.float32),
            jax.ShapeDtypeStruct((2, span, span), LOW),
        ]
        + reduction.outs(),
        scratch_shapes=[pltpu.VMEM((2,) + keys.shape, LOW)] + reduction.scratch(),
        compiler_params=params(collective_id=collective_id, has_side_effects=True),
        name="cross_backward",
    )(
        lengths, query, keys, values, logs, grad_mixed, memory, cross_full, cross_full,
        *reduction.operands(),
    )


def self_backward(
    reduction, collective_id, tokens, mask, vectors, self_full, cross_full, saved, cross_query_grad,
    grad_two, cross_sums, feed_sums, out_sums, bias_grad
):
    count, length, span = tokens.shape
    qkv, mixed, logs, unit, inverse = saved
    rows, total_rows = padded(length), mixed.shape[0]
    attend = 2
    project = attend + count
    last = project + 2
    carried, produced = len(reduction.operands()), len(reduction.outs())
    pair = reduction.parts
    plan = {0: (pair,), 1: (pair,), 3: (pair,), 4: (pair,), 5: (2 * pair,), 6: (pair,)}

    def kernel(*refs):
        tokens, mask, vectors, weight, query_weight, qkv, mixed, logs, unit, inverse = refs[:10]
        cross_query_grad, grad_two, cross_sums, feed_sums, out_sums, bias_grad = refs[10:16]
        operands, refs = refs[16 : 16 + carried], refs[16 + carried :]
        input_grad, results, refs = refs[0], refs[1 : 1 + produced], refs[1 + produced :]
        (low, grads, total), scratch = refs[:3], refs[3:]
        step = pl.program_id(0)
        rounds, made, terms, vector_flow = reduction.rounds(operands, results, scratch)
        for start, begins in plan.items():

            @pl.when(step == start)
            def _():
                if start == 0:
                    reduction.greet()
                if start == project:
                    rounds.live.append(vector_flow)
                for begin in begins:
                    rounds.run(begin)

        def keep(number, product):
            made[number] = product.astype(LOW).reshape(made.shape[1:])

        @pl.when(step == 0)
        def _():
            fill_tokens(low, tokens)
            terms[...] = jnp.zeros_like(terms)
            first_low = (unit[...] * vectors[3:4] + vectors[4:5]).astype(LOW)
            keep(0, dot_tn(first_low, cross_query_grad[...]) * SCALE)
            grad = grad_two[...] + dot_nt(cross_query_grad[...], query_weight[0]) * SCALE
            down_grad = norm_back(grad, unit[...], inverse[...], vectors[3:4])
            total[...] = down_grad
            terms[2:3] = column_sum(down_grad.astype(LOW))
            terms[3:4] = column_sum(grad * unit[...])
            terms[4:5] = column_sum(grad)
            spread = jnp.sum(cross_sums[...], axis=0)
            terms[5:6] = spread[0:1] * SCALE
            terms[6:7] = spread[1:2]
            terms[7:10] = out_sums[0:3]
            terms[10:13] = feed_sums[0:3]
            for k in range(bias_grad.shape[1] // span):
                terms[13 + k : 14 + k] = bias_grad[:, k * span : (k + 1) * span]

        @pl.when(step == 1)
        def _():
            grad_low = total[...].astype(LOW)
            keep(1, dot_tn(mixed[...], grad_low))
            grads[0] = dot_nt(grad_low, weight[0]).astype(LOW)

        for s in range(count):

            @pl.when(step == attend + s)
            def _():
                allowed = causal_allowed(rows, mask[s : s + 1])
                table_at = slice(s * rows, (s + 1) * rows)

                def pair(lane, head):
                    where = (table_at, pl.ds(lane, PAIR))
                    table = logs[table_at]
                    columns = [pick_column(table, head + which) for which in range(2)]
                    found = attend_pair_back(
                        qkv[(0,) + where],
                        qkv[(1,) + where],
                        qkv[(2,) + where],
                        allowed,
                        columns,
                        grads[(0,) + where],
                    )
                    for number in range(3):
                        grads[(1 + number,) + where] = found[number]

                for_head_groups(span, pair)
                if s == count - 1:
                    terms[0:1] = column_sum(grads[1]) * SCALE
                    terms[1:2] = column_sum(grads[3])

        @pl.when(step >= project)
        def _():
            factor = jnp.where(step == project, SCALE, 1.0)
            part = grads[step - project + 1]
            keep(step - project + 2, dot_tn(low[...], part) * factor)
            total[...] += dot_nt(part, weight[0]) * factor

        @pl.when(step == last)
        def _():
            store_tokens(input_grad, total[...])
            rounds.finish(pair)

    operands = (
        tokens, mask, vectors, self_full, cross_full, qkv, mixed, logs, unit, inverse,
        cross_query_grad, grad_two, cross_sums, feed_sums, out_sums, bias_grad,
    )
    specs = [once_spec(operand.shape) for operand in operands]
    specs[3] = pl.BlockSpec(
        (1, span, span), lambda i: (jnp.where(i < project, 3, i - project), 0, 0)
    )
    specs[4] = once_spec((1, span, span))
    return pl.pallas_call(
        kernel,
        grid=(last + 1,),
        in_specs=specs + reduction.in_specs(),
        out_specs=[once_spec(tokens.shape)] + reduction.out_specs(),
        out_shape=[jax.ShapeDtypeStruct(tokens.shape, jnp.float32)] + reduction.outs(),
        scratch_shapes=[
            pltpu.VMEM((total_rows, span), LOW),
            pltpu.VMEM((4, total_rows, span), LOW),
            pltpu.VMEM((total_rows, span), jnp.float32),
        ]
        + reduction.scratch(),
        compiler_params=params(collective_id=collective_id, has_side_effects=True),
        name="self_backward",
    )(*operands, *reduction.operands())


def per_device(
    wide,
    narrow,
    decoder_input,
    memory,
    decoder_mask,
    memory_length,
    self_weights,
    cross_weights,
    feed_weights,
    vectors,
    hidden_bias,
    cotangent,
):
    seq_count, seq_length, model_width = decoder_input.shape
    mem_span = memory.shape[1]
    memory_low = memory.reshape(seq_count * mem_span, model_width)
    saved, (self_full, cross_full, feed_full, vector_all, bias_all) = front(
        Gather(
            wide, narrow, [self_weights, cross_weights, feed_weights], [vectors, hidden_bias]
        ),
        decoder_input,
        decoder_mask,
        memory_length,
        memory_low,
        1,
    )
    qkv, self_mixed, self_logs, unit_one, inverse_one = saved[:5]
    cross_query, cross_keys, cross_values, cross_mixed, cross_logs = saved[5:]
    hidden, slope, layer_output, unit_two, inverse_two, grad_three, feed_sums = feed_forward(
        cross_mixed, cross_full, unit_one, vector_all, bias_all, feed_full, cotangent
    )
    feed_part, bias_part, grad_two, grad_cmixed, cross_out_grad, out_sums = feed_backward(
        grad_three, unit_two, inverse_two, vector_all, hidden, slope, feed_full, cross_full, cross_mixed
    )
    cross_gq, cross_sums, memory_grad, memory_parts, feed_grad = cross_backward(
        Reduction(wide, narrow, [feed_part], 4),
        cross_query,
        cross_keys,
        cross_values,
        memory_length,
        cross_logs,
        grad_cmixed,
        memory_low,
        cross_full,
        2,
    )
    places = [(0, 1), (0, 2), (0, 3), (0, 0), (1, 3), (1, 0), (1, 1), (1, 2)]
    input_grad, cross_grad, self_weight_gradient, vectors_grad, hidden_bias_grad = self_backward(
        Reduction(
            wide,
            narrow,
            [memory_parts, cross_out_grad[None]],
            2,
            5,
            places,
            [vectors.shape, hidden_bias.shape],
        ),
        3,
        decoder_input,
        decoder_mask,
        vector_all,
        self_full,
        cross_full,
        (qkv, self_mixed, self_logs, unit_one, inverse_one),
        cross_gq,
        grad_two,
        cross_sums,
        feed_sums,
        out_sums,
        bias_part,
    )
    return (
        layer_output,
        input_grad,
        memory_grad.reshape(seq_count, mem_span, model_width),
        self_weight_gradient,
        cross_grad,
        feed_grad,
        vectors_grad,
        hidden_bias_grad,
    )


def solution(mesh):
    placed = (
        P(("wide", "narrow"), None, None),
        P(("wide", "narrow"), None, None),
        P(("wide", "narrow"), None),
        P(("wide", "narrow")),
        P(None, "wide", "narrow"),
        P(None, "wide", "narrow"),
        P(None, "wide", "narrow"),
        P(None, "narrow"),
        P(None, "narrow"),
        P(("wide", "narrow"), None, None),
    )
    return jax.shard_map(
        functools.partial(per_device, mesh.shape["wide"], mesh.shape["narrow"]),
        mesh=mesh,
        in_specs=placed,
        out_specs=(
            P(("wide", "narrow"), None, None),
            P(("wide", "narrow"), None, None),
            P(("wide", "narrow"), None, None),
            P(None, "wide", "narrow"),
            P(None, "wide", "narrow"),
            P(None, "wide", "narrow"),
            P(None, "narrow"),
            P(None, "narrow"),
        ),
        check_vma=False,
    )
```

```python
import functools
import math

import jax
import jax.numpy as jnp
from jax import lax
from jax.experimental import pallas as pl
from jax.experimental.pallas import tpu as pltpu
from jax.sharding import PartitionSpec as P

HEADS = 16
HEAD_DIM = 64


MESH_ID = pl.DeviceIdType.MESH


class Position:
    def __init__(self, wide, narrow):
        self.sizes = {"line": wide // 4, "pair": 2, "core": 2, "column": narrow}

    def get(self, axis):
        if axis == "column":
            return lax.axis_index("narrow")
        index = lax.axis_index("wide")
        if axis == "core":
            return index % 2
        return (index // 2) % 2 if axis == "pair" else index // 4

    def device(self, **moved):
        spot = {name: moved.get(name, self.get(name)) for name in self.sizes}
        return (spot["line"] * 4 + spot["pair"] * 2 + spot["core"], spot["column"])


class Channels:
    def __init__(self, sends, recvs):
        self.sends, self.recvs, self.used = sends, recvs, 0

    def take(self):
        self.used += 1
        number = self.used - 1
        return lambda: (self.sends.at[number], self.recvs.at[number])


def remote(source, target, channel, device):
    return pltpu.make_async_remote_copy(
        src_ref=source,
        dst_ref=target,
        send_sem=channel()[0],
        recv_sem=channel()[1],
        device_id=device,
        device_id_type=MESH_ID,
    )


def flip(index, bit):
    return index + bit - 2 * bit * ((index // bit) % 2)


def peers(position, axis, distance):
    at = (position.get(axis) + distance) % position.sizes[axis]
    return at, position.device(**{axis: at})


def greet(position):
    barrier = pltpu.get_barrier_semaphore()
    expected = 0
    for axis, size in position.sizes.items():
        for distance in range(1, size):
            pl.semaphore_signal(
                barrier,
                inc=1,
                device_id=peers(position, axis, distance)[1],
                device_id_type=MESH_ID,
            )
            expected += 1
    pl.semaphore_wait(barrier, expected)


def advance(generator):
    return next(generator, "done") != "done"


class Rounds:
    def __init__(self, flows, live=()):
        self.waiting, self.live = list(flows), list(live)
        self.all, self.first = None, []

    def run(self, start=0):
        self.live = self.live + self.waiting[:start]
        self.waiting = self.waiting[start:]
        self.live = [flow for flow in self.live if advance(flow)]

    def move(self, groups, size=2):
        if self.all is None:
            self.all = [*self.waiting]
            self.waiting, self.first, self.live = [], self.live, list(self.all)
        for group in groups:
            self.first = [flow for flow in self.first if advance(flow)]
            for flow in self.all[group * size : group * size + size]:
                if not advance(flow):
                    self.live.remove(flow)

    def finish(self, together=2):
        while self.waiting or self.live:
            self.run(together)


def finish_sends(sent):
    for describe in sent:
        describe().wait_send()


def gather_axis(position, axis, channels, block, own, sent):
    arrivals = []
    for distance in range(1, position.sizes[axis]):
        channel = channels.take()

        def send(distance=distance, channel=channel):
            device = peers(position, axis, distance)[1]
            return remote(own(), block(position.get(axis)), channel, device)

        def arrival(distance=distance, channel=channel):
            came, device = peers(position, axis, -distance)
            return remote(block(came), block(came), channel, device)

        send().start()
        sent.append(send)
        arrivals.append(arrival)
    yield
    for arrival in arrivals:
        arrival().wait_recv()


def gather_flow(position, channels, local_sem, own, region, order):
    sent = []

    def place(done, axis=None, at=None):
        spot = {name: None if name in done else position.get(name) for name in position.sizes}
        if axis is not None:
            spot[axis] = at
        return region(**spot)

    def local():
        return pltpu.make_async_copy(own(), place(()), local_sem())

    local().start()
    for number, axis in enumerate(order):
        done = order[:number]

        def block(j, axis=axis, done=done):
            return place(done, axis, j)

        def source(block=block, axis=axis, first=number == 0):
            return own() if first else block(position.get(axis))

        yield from gather_axis(position, axis, channels, block, source, sent)
        if number == 0:
            local().wait()
    finish_sends(sent)


def whole(index):
    return slice(None) if index is None else index


def row_splits(rows, most):
    return max(1, min(most, rows // 16))


def flow_channels(wide, narrow):
    return 2 + (wide // 4 - 1) + (narrow - 1)


ORDER_A = ("line", "pair", "column", "core")
ORDER_B = ("line", "column", "pair", "core")


def lane_parts(wide, narrow, block):
    return block.shape[2] * narrow // (block.shape[1] * wide)


def gather_flows(position, channels, local_sems, parts, blocks, fulls):
    flows = []
    for block_ref, full_ref, count in zip(blocks, fulls, parts):
        width = block_ref.shape[2] // count
        for place in range(full_ref.shape[0]):
            part, matrix = divmod(place, block_ref.shape[0])

            def region(line, pair, core, column, full_ref=full_ref, place=place, width=width):
                lanes = slice(None)
                if column is not None:
                    lanes = pl.ds(pl.multiple_of(column * width, 128), width)
                return full_ref.at[place, whole(line), whole(pair), whole(core), :, lanes]

            def own(block_ref=block_ref, matrix=matrix, part=part, width=width):
                return block_ref.at[matrix, :, part * width : (part + 1) * width]

            number = len(flows)
            order = ORDER_A if number % 2 == 0 else ORDER_B
            flows.append(
                gather_flow(
                    position, channels, lambda number=number: local_sems.at[number], own, region, order
                )
            )
    return flows


def column_flow(position, channels, sem, block_ref, full_ref):
    width = block_ref.shape[1]

    def region(column):
        return full_ref.at[:, pl.ds(pl.multiple_of(column * width, 128), width)]

    def local():
        return pltpu.make_async_copy(block_ref, region(position.get("column")), sem())

    sent = []
    local().start()
    yield from gather_axis(position, "column", channels, region, lambda: block_ref, sent)
    local().wait()
    finish_sends(sent)


class Gather:
    def __init__(self, wide, narrow, arrays, vectors=()):
        self.wide, self.narrow = wide, narrow
        self.arrays, self.vectors = list(arrays), list(vectors)
        self.parts = [lane_parts(wide, narrow, array) for array in arrays]
        self.count = sum(array.shape[0] * part for array, part in zip(arrays, self.parts))

    def operands(self):
        return self.arrays + self.vectors

    def in_specs(self):
        return [pl.BlockSpec(memory_space=pltpu.VMEM)] * len(self.operands())

    def wholes(self):
        return [(vector.shape[0], vector.shape[1] * self.narrow) for vector in self.vectors]

    def outs(self):
        outs = []
        for array, part in zip(self.arrays, self.parts):
            matrices, rows, width = array.shape
            shape = (matrices * part, self.wide // 4, 2, 2, rows, width // part * self.narrow)
            outs.append(jax.ShapeDtypeStruct(shape, array.dtype))
        return outs + [jax.ShapeDtypeStruct(shape, jnp.float32) for shape in self.wholes()]

    def out_specs(self):
        specs = [pl.BlockSpec(memory_space=pl.ANY)] * len(self.arrays)
        return specs + [pl.BlockSpec(memory_space=pltpu.VMEM)] * len(self.vectors)

    def scratch(self):
        flows = self.count + len(self.vectors)
        copies = flow_channels(self.wide, self.narrow) * flows
        return [
            pltpu.SemaphoreType.DMA((copies,)),
            pltpu.SemaphoreType.DMA((copies,)),
            pltpu.SemaphoreType.DMA((flows,)),
        ] + [pltpu.VMEM(shape, jnp.float32) for shape in self.wholes()]

    def rounds(self, operands, outs, scratch):
        position = Position(self.wide, self.narrow)
        channels = Channels(scratch[0], scratch[1])
        count, local_sems, wholes = len(self.arrays), scratch[2], scratch[3:]
        live = [
            column_flow(
                position,
                channels,
                lambda k=k: local_sems.at[self.count + k],
                operands[count + k],
                wholes[k],
            )
            for k in range(len(self.vectors))
        ]
        flows = gather_flows(
            position, channels, local_sems, self.parts, operands[:count], outs[:count]
        )
        return Rounds(flows, live), wholes

    def greet(self):
        greet(Position(self.wide, self.narrow))

    def join(self, results):
        count = len(self.arrays)
        fulls = [full.reshape(full.shape[0], -1, full.shape[-1]) for full in results[:count]]
        return fulls + list(results[count:])


def add_rows(target, parts):
    lead = target.shape[:-2]
    count = math.prod(lead)

    def add(spot):
        total = parts[0][spot].astype(jnp.float32)
        for part in parts[1:]:
            total = total + part[spot].astype(jnp.float32)
        target[spot] = total.astype(target.dtype)

    if count == 1:
        add((0,) * len(lead))
        return

    @pl.loop(0, count)
    def _(k):
        where = []
        for extent in reversed(lead):
            where.insert(0, k % extent)
            k = k // extent
        add(tuple(where))


def reduce_axis(position, axis, channels, local, slots, result, sent):
    size = position.sizes[axis]
    for distance in range(1, size):
        channel = channels.take()

        def send(distance=distance, channel=channel):
            at, device = peers(position, axis, distance)
            return remote(local(at), slots.at[distance - 1], channel, device)

        send().start()
        sent.append(send)
    yield
    for send in sent[1 - size :]:
        send().wait_recv()
    add_rows(
        result(), [local(position.get(axis))] + [slots.at[k] for k in range(size - 1)]
    )


def reduce_flow(position, channels, local_sem, loc, grads, result, buffers, order):
    first, mid, last, line_slots = buffers
    sent = []

    def own():
        return pltpu.make_async_copy(grads(position.get("core")), loc(), local_sem())

    def mine():
        return grads(position.get("core")) if loc is None else loc()

    channel = channels.take()

    def swap():
        core = position.get("core")
        return remote(grads(1 - core), first, channel, position.device(core=1 - core))

    if loc is not None:
        own().start()
    swap().start()
    sent.append(swap)
    yield
    if loc is not None:
        own().wait()
    swap().wait_recv()
    add_rows(first, [first, mine()])
    width = result().shape[-1]

    def columns(j):
        return pl.ds(pl.multiple_of(j * width, 128), width)

    def held():
        return mid.at[0]

    def final():
        return last.at[0]

    if order == "A":
        yield from reduce_axis(
            position, "column", channels, lambda j: first.at[:, :, :, columns(j)], mid, held, sent
        )
        yield from reduce_axis(position, "pair", channels, lambda j: held().at[:, j], last, final, sent)
    else:
        yield from reduce_axis(position, "pair", channels, lambda j: first.at[:, j], mid, held, sent)
        yield from reduce_axis(
            position, "column", channels, lambda j: held().at[:, :, columns(j)], last, final, sent
        )
    yield from reduce_axis(
        position, "line", channels, lambda j: final().at[pl.ds(j, 1)], line_slots, result, sent
    )
    finish_sends(sent)


def double_flow(position, channels, terms, total, inbox, vectors_out, bias_out):
    total[0] = terms[...]
    step = 0
    for axis in ("core", "pair", "line", "column"):
        bit = 1
        while bit < position.sizes[axis]:
            channel = channels.take()

            def describe():
                to = position.device(**{axis: flip(position.get(axis), bit)})
                return remote(total.at[step], inbox.at[step], channel, to)

            describe().start()
            yield
            describe().wait_recv()
            total[step + 1] = total[step] + inbox[step]
            describe().wait_send()
            bit *= 2
            step += 1
    count, width = vectors_out.shape
    lanes = pl.ds(pl.multiple_of(position.get("column") * width, 128), width)
    vectors_out[...] = total[step, 0:count, lanes]
    for k in range(bias_out.shape[1] // width):
        bias_out[:, k * width : (k + 1) * width] = total[step, count + k : count + k + 1, lanes]


class Reduction:
    RING = 4

    def __init__(self, wide, narrow, arrays, parts, places, matrices, held=0, shapes=()):
        self.wide, self.narrow, self.held, self.shapes = wide, narrow, held, list(shapes)
        depth, span = arrays[0].shape[1:]
        self.rows = rows = depth // wide
        self.parts = row_splits(rows, parts)
        self.piece = rows // self.parts
        self.line, self.span, self.width = wide // 4, span, span // narrow
        self.matrices = matrices
        sources = [(s, m) for s, array in enumerate(arrays) for m in range(array.shape[0])]
        sources += [(None, m) for m in range(held)]
        self.pieces = [
            source + (part,) + place
            for source, place in zip(sources, places)
            for part in range(self.parts)
        ]
        self.views = [array.reshape(array.shape[0], self.line, 2, 2, rows, span) for array in arrays]

    def order(self, number):
        return "A" if number % 2 == 0 else "B"

    def operands(self):
        return self.views

    def in_specs(self):
        return [pl.BlockSpec(memory_space=pl.ANY)] * len(self.views)

    def outs(self):
        outs = [
            jax.ShapeDtypeStruct((count, self.rows, self.width * parts), jnp.float32)
            for count, parts in self.matrices
        ]
        return outs + [jax.ShapeDtypeStruct(shape, jnp.float32) for shape in self.shapes]

    def out_specs(self):
        return [pl.BlockSpec(memory_space=pltpu.VMEM)] * len(self.outs())

    def steps(self):
        return (self.wide * self.narrow).bit_length() - 1

    def terms_shape(self):
        count = self.shapes[0][0] + self.shapes[1][1] * self.narrow // self.span
        return (count + -count % 8, self.span)

    def scratch(self):
        low, line, piece = jnp.bfloat16, self.line, self.piece
        copies = flow_channels(self.wide, self.narrow) * len(self.pieces) + 16
        shapes = [
            pltpu.SemaphoreType.DMA((copies,)),
            pltpu.SemaphoreType.DMA((copies,)),
            pltpu.SemaphoreType.DMA((len(self.pieces),)),
            pltpu.VMEM((self.RING, line, 2, piece, self.span), low),
        ]
        if self.held:
            shapes.append(pltpu.VMEM((self.held, line, 2, 2, self.rows, self.span), low))
        if self.shapes:
            shapes.append(pltpu.VMEM(self.terms_shape(), jnp.float32))
            shapes.append(pltpu.VMEM((self.steps() + 1,) + self.terms_shape(), jnp.float32))
            shapes.append(pltpu.VMEM((self.steps(),) + self.terms_shape(), jnp.float32))
        for number in range(len(self.pieces)):
            shapes.append(pltpu.VMEM((line, 2, piece, self.span), low))
            if self.order(number) == "A":
                shapes.append(pltpu.VMEM((self.narrow - 1, line, 2, piece, self.width), low))
                shapes.append(pltpu.VMEM((1, line, piece, self.width), low))
            else:
                shapes.append(pltpu.VMEM((1, line, piece, self.span), low))
                shapes.append(pltpu.VMEM((self.narrow - 1, line, piece, self.width), low))
            shapes.append(pltpu.VMEM((line - 1, 1, piece, self.width), low))
        return shapes

    def rounds(self, operands, outs, scratch):
        position = Position(self.wide, self.narrow)
        channels = Channels(scratch[0], scratch[1])
        local_sems, ring, buffers = scratch[2], scratch[3], list(scratch[4:])
        made = buffers.pop(0) if self.held else None
        terms, vector_flow = None, None
        if self.shapes:
            terms, total, inbox = buffers[:3]
            buffers = buffers[3:]
            vector_flow = double_flow(position, channels, terms, total, inbox, *outs[-2:])
        flows = []
        for number, (source, inner, part, out, matrix, slot) in enumerate(self.pieces):
            at = pl.ds(part * self.piece, self.piece)
            lanes = pl.ds(slot * self.width, self.width)

            def grads(core, source=source, inner=inner, at=at):
                array = made if source is None else operands[source]
                return array.at[inner, :, :, core, at]

            flows.append(
                reduce_flow(
                    position,
                    channels,
                    lambda number=number: local_sems.at[number],
                    None if source is None else lambda number=number: ring.at[number % self.RING],
                    grads,
                    lambda out=out, at=(pl.ds(matrix, 1), at, lanes): outs[out].at[at],
                    buffers[4 * number : 4 * number + 4],
                    self.order(number),
                )
            )
        return Rounds(flows), made, terms, vector_flow

    def greet(self):
        greet(Position(self.wide, self.narrow))


LOW = jnp.bfloat16
NEGATIVE = -1000000000.0
EPSILON = 1e-05
PAIR = 2 * HEAD_DIM
SCALE = HEAD_DIM ** (-0.5)
BUDGET = 65000 * 1024


def dot_nn(left, right):
    return jnp.dot(left, right, preferred_element_type=jnp.float32)


def dot_nt(left, right):
    return lax.dot_general(
        left, right, (((1,), (1,)), ((), ())), preferred_element_type=jnp.float32
    )


def dot_tn(left, right):
    return lax.dot_general(
        left, right, (((0,), (0,)), ((), ())), preferred_element_type=jnp.float32
    )


def padded(length):
    return -(-length // 16) * 16


def column_sum(rows):
    return jnp.sum(rows.astype(jnp.float32), axis=0, keepdims=True)


def standardise(hidden):
    centre = hidden - jnp.mean(hidden, axis=-1, keepdims=True)
    spread = jnp.mean(centre * centre, axis=-1, keepdims=True)
    inverse = lax.rsqrt(spread + EPSILON)
    return centre * inverse, inverse


def norm_back(grad, unit, inverse, gain):
    scaled = grad * gain
    first = jnp.mean(scaled, axis=-1, keepdims=True)
    second = jnp.mean(scaled * unit, axis=-1, keepdims=True)
    return inverse * (scaled - first - unit * second)


def for_rows(total, function):
    chunk = next(size for size in (48, 64, 32, 16) if total % size == 0)

    @pl.loop(0, total // chunk)
    def _(k):
        function(pl.ds(pl.multiple_of(k * chunk, 16), chunk))


def add_norm_sums(sums, first, low, grad, unit):
    sums[first : first + 1] += column_sum(low)
    sums[first + 1 : first + 2] += column_sum(grad * unit)
    sums[first + 2 : first + 3] += column_sum(grad)


def fill_tokens(target, source):
    count, length, span = source.shape
    rows = padded(length)
    for s in range(count):
        if rows > length:
            base = s * rows + length // 16 * 16
            target[base : (s + 1) * rows] = jnp.zeros(((s + 1) * rows - base, span), target.dtype)
        target[s * rows : s * rows + length] = source[s].astype(target.dtype)


def store_tokens(target, values):
    count, length, span = target.shape
    rows = padded(length)
    for s in range(count):
        target[s] = values[s * rows : s * rows + length].astype(target.dtype)


def head_lanes(rows, which):
    lane = lax.broadcasted_iota(jnp.int32, rows.shape, 1)
    return (lane >= HEAD_DIM) == (which == 1)


def one_head(rows, which):
    return jnp.where(head_lanes(rows, which), rows, jnp.zeros_like(rows))


def pick_column(table, number):
    lane = lax.broadcasted_iota(jnp.int32, table.shape, 1)
    return jnp.sum(jnp.where(lane == number, table, 0.0), axis=1, keepdims=True)


def attend_pair(query, keys, values, allowed):
    mixed, logs = [], []
    for which in range(2):
        scores = dot_nt(one_head(query, which), keys)
        scores = jnp.where(allowed, scores, NEGATIVE)
        peak = jnp.max(scores, axis=-1, keepdims=True)
        expo = jnp.exp(scores - peak)
        total = jnp.sum(expo, axis=-1, keepdims=True)
        weights = (expo * (1.0 / total)).astype(LOW)
        mixed.append(dot_nn(weights, values))
        logs.append(peak + jnp.log(total))
    both = jnp.where(head_lanes(mixed[0], 0), mixed[0], mixed[1])
    return both.astype(LOW), logs


def attend_pair_back(query, keys, values, allowed, logs, grad):
    grad_query, grad_keys, grad_values = [], None, None
    for which in range(2):
        query_one, grad_one = one_head(query, which), one_head(grad, which)
        scores = jnp.where(allowed, dot_nt(query_one, keys), NEGATIVE)
        probs = jnp.exp(scores - logs[which])
        grad_probs = dot_nt(grad_one, values)
        slope = jnp.sum(grad_probs * probs, axis=-1, keepdims=True)
        grad_scores = (probs * (grad_probs - slope)).astype(LOW)
        grad_query.append(dot_nn(grad_scores, keys))
        part_keys = dot_tn(grad_scores, query_one)
        part_values = dot_tn(probs.astype(LOW), grad_one)
        grad_keys = part_keys if which == 0 else grad_keys + part_keys
        grad_values = part_values if which == 0 else grad_values + part_values
    both = jnp.where(head_lanes(grad_query[0], 0), grad_query[0], grad_query[1])
    return both.astype(LOW), grad_keys.astype(LOW), grad_values.astype(LOW)


def causal_allowed(rows, mask_row):
    valid = jnp.sum(mask_row, axis=-1, keepdims=True)
    query_at = lax.broadcasted_iota(jnp.int32, (rows, rows), 0)
    key_at = lax.broadcasted_iota(jnp.int32, (rows, rows), 1)
    return (query_at >= key_at) & (key_at < valid)


GROUP_PAIRS = 2


def for_head_groups(span, function):
    lanes = min(span, GROUP_PAIRS * PAIR)

    @pl.loop(0, span // lanes)
    def _(g):
        for p in range(lanes // PAIR):
            function(pl.multiple_of(g * lanes + p * PAIR, PAIR), 2 * (g * (lanes // PAIR) + p))


def whole_spec(shape):
    return pl.BlockSpec(shape, lambda *at: (0,) * len(shape))


def params(**more):
    return pltpu.CompilerParams(vmem_limit_bytes=BUDGET, **more)


CROSS_LANES = 2 * PAIR


def once_spec(shape):
    return pl.BlockSpec(shape, lambda *at: (0,) * len(shape), pipeline_mode=pl.Buffered(1))


def front(load, tokens, mask, lengths, memory, cotangent, collective_id):
    count, length, span = tokens.shape
    rows = padded(length)
    total, slots = count * rows, memory.shape[0] // count
    tiles = 4
    tile = memory.shape[0] // tiles
    groups = span // CROSS_LANES
    attend, join, ask = 3, 3 + count, 4 + count
    recall = ask + 1
    look = recall + tiles
    add = look + count * groups
    feed = add + 1
    parts = load.parts[2]
    last = feed + parts - 1
    carried = len(load.operands())
    plan = {
        0: (0, 0, 1, 0, 1, 2, 0, 1, 2, 3, 0),
        2: (1, 2, 3, 4, 1),
        ask: (2, 3, 4, 5, 2),
        recall: (3, 4, 5, 6, 3),
        look: (4, 5, 6, 7),
        look + 5: (4, 5, 6, 7),
        feed + 1: (5, 6, 7),
        feed + 2: (6,),
        feed + 3: (7, 7),
    }

    def kernel(*refs):
        tokens, mask, lengths, memory, cotangent = refs[:5]
        operands, refs = refs[5 : 5 + carried], refs[5 + carried :]
        stored, (logs, inverse, cross_logs) = refs[: len(kept)], refs[len(kept) : len(kept) + 3]
        hidden, slope, output, inverse_two, grad_three, sums = refs[len(kept) + 3 : len(kept) + 9]
        refs = refs[len(kept) + 9 :]
        results, refs = refs[:carried], refs[carried:]
        low, spare, running, weights, weight_sem, store_sems = refs[:6]
        held, scratch = refs[6 : 6 + len(kept)], refs[6 + len(kept) :]
        qkv, mixed, unit, query, keys, values, cross_mixed, unit_two = held
        step = pl.program_id(0)
        rounds, (vectors, bias) = load.rounds(operands, results, scratch)
        for start, begins in plan.items():

            @pl.when(step == start)
            def _():
                if start == 0:
                    load.greet()
                rounds.move(begins)

        def store(*numbers, wait=False):
            for number in numbers:
                copy = pltpu.make_async_copy(
                    held[number], stored[number], store_sems.at[number]
                )
                copy.wait() if wait else copy.start()

        @pl.when(step == recall)
        def _():
            store(0, 1, 2, 3)

        @pl.when(step == look)
        def _():
            store(4, 5)

        @pl.when(step == feed)
        def _():
            store(6, 7)

        def fetch(array, matrix, slot):
            copy = pltpu.make_async_copy(results[array].at[matrix], weights.at[slot], weight_sem)
            copy.start()
            copy.wait()

        def weight(slot):
            return weights[slot].reshape(span, span)

        @pl.when(step == 0)
        def _():
            fill_tokens(low, tokens)

        @pl.when(step < attend)
        def _():
            fetch(0, step, 0)
            product = dot_nn(low[...], weight(0))
            none = jnp.zeros_like(vectors[0:1])
            shift = jnp.where(step == 0, vectors[0:1], jnp.where(step == 2, vectors[1:2], none))
            product = (product + shift) * jnp.where(step == 0, SCALE, 1.0)
            qkv[step] = product.astype(LOW)

        @pl.when((step >= attend) & (step < join))
        def _():
            s = step - attend
            allowed = causal_allowed(rows, mask[pl.ds(s, 1)])
            table_at = pl.ds(pl.multiple_of(s * rows, 16), rows)
            logs[table_at] = jnp.zeros((rows, 128), jnp.float32)

            def pair(lane, head):
                where = (table_at, pl.ds(lane, PAIR))
                both, sums = attend_pair(
                    qkv[(0,) + where], qkv[(1,) + where], qkv[(2,) + where], allowed
                )
                mixed[where] = both
                table = logs[table_at]
                spot = lax.broadcasted_iota(jnp.int32, table.shape, 1)
                for which in range(2):
                    table = jnp.where(spot == head + which, sums[which], table)
                logs[table_at] = table

            for_head_groups(span, pair)

        @pl.when(step == join)
        def _():
            fetch(0, 3, 0)
            running[...] = dot_nn(mixed[...], weight(0))

            def first_norm(at):
                summed = low[at].astype(jnp.float32) + (running[at] + vectors[2:3])
                found, inverse[at] = standardise(summed)
                unit[at] = found
                spare[at] = (found * vectors[3:4] + vectors[4:5]).astype(LOW)

            for_rows(total, first_norm)

        @pl.when(step == ask)
        def _():
            fetch(1, 0, 0)
            product = dot_nn(spare[...], weight(0))
            query[...] = ((product + vectors[5:6]) * SCALE).astype(LOW)

        @pl.when(step == recall)
        def _():
            fetch(1, 1, 0)
            fetch(1, 2, 1)

        @pl.when((step >= recall) & (step < look))
        def _():
            at = pl.ds(pl.multiple_of((step - recall) * tile, 16), tile)
            keys[at] = dot_nn(memory[...], weight(0)).astype(LOW)
            values[at] = (dot_nn(memory[...], weight(1)) + vectors[6:7]).astype(LOW)

        @pl.when((step >= look) & (step < add))
        def _():
            s, g = (step - look) // groups, (step - look) % groups
            slot = lax.broadcasted_iota(jnp.int32, (1, slots), 1)
            allowed = slot < lengths[s]
            token_at = pl.ds(pl.multiple_of(s * rows, 16), rows)
            slot_at = pl.ds(pl.multiple_of(s * slots, 16), slots)
            cross_logs[...] = jnp.zeros_like(cross_logs)

            @pl.loop(0, CROSS_LANES // PAIR)
            def _(p):
                lanes = pl.ds(pl.multiple_of(g * CROSS_LANES + p * PAIR, PAIR), PAIR)
                both, sums = attend_pair(
                    query[token_at, lanes], keys[slot_at, lanes], values[slot_at, lanes], allowed
                )
                cross_mixed[token_at, lanes] = both
                table = cross_logs[0]
                spot = lax.broadcasted_iota(jnp.int32, table.shape, 1)
                for which in range(2):
                    table = jnp.where(spot == 2 * p + which, sums[which], table)
                cross_logs[0] = table

        @pl.when(step == add)
        def _():
            fetch(1, 3, 0)
            running[...] = dot_nn(cross_mixed[...], weight(0))

            def second_norm(at):
                first = unit[at] * vectors[3:4] + vectors[4:5]
                found, inverse_two[at] = standardise(first + (running[at] + vectors[7:8]))
                unit_two[at] = found
                low[at] = (found * vectors[8:9] + vectors[9:10]).astype(LOW)
                running[at] = jnp.zeros_like(found)

            for_rows(total, second_norm)
            fill_tokens(spare, cotangent)

        @pl.when(step >= feed)
        def _():
            part = step - feed
            fetch(2, 2 * part, 0)
            fetch(2, 2 * part + 1, 1)
            width = bias.shape[1] // parts // load.narrow
            shift = jnp.concatenate(
                [
                    bias[:, pl.ds(pl.multiple_of((n * parts + part) * width, 128), width)]
                    for n in range(load.narrow)
                ],
                axis=1,
            )
            half_lanes = span // 2
            row = lax.broadcasted_iota(jnp.int32, (8, span), 0)
            sums[...] = jnp.where(row == 0, shift, 0.0)

            @pl.loop(0, 2)
            def _(k):
                lanes = pl.ds(pl.multiple_of(k * half_lanes, 128), half_lanes)
                up = weights[0, :, :, :, :, lanes].reshape(span, half_lanes)
                down = weights[1, :, :, :, :, lanes].reshape(span, half_lanes)
                inner = dot_nn(low[...], up) + sums[0:1, lanes]
                half = 0.5 + 0.5 * lax.erf(inner * (0.5**0.5))
                bell = jnp.exp(-0.5 * inner * inner) * ((0.5 / math.pi) ** 0.5)
                active = (inner * half).astype(LOW)
                hidden[:, lanes] = active
                slope[:, lanes] = (half + inner * bell).astype(LOW)
                running[...] += dot_nt(active, down)

        @pl.when(step == last)
        def _():
            rounds.finish()
            results[-2][...], results[-1][...] = vectors[...], bias[...]
            sums[...] = jnp.zeros_like(sums)

            def third_norm(at):
                second = unit_two[at] * vectors[8:9] + vectors[9:10]
                found, inverse_three = standardise(second + (running[at] + vectors[10:11]))
                low[at] = (found * vectors[11:12] + vectors[12:13]).astype(LOW)
                grad = spare[at].astype(jnp.float32)
                down_grad = norm_back(grad, found, inverse_three, vectors[11:12])
                grad_three[at] = down_grad
                add_norm_sums(sums, 0, down_grad.astype(LOW), grad, found)

            for_rows(total, third_norm)
            store_tokens(output, low)
            store(*range(len(kept)), wait=True)

    def token(dtype, lanes=span):
        return jax.ShapeDtypeStruct((total, lanes), dtype)

    kept = [
        jax.ShapeDtypeStruct((3, total, span), LOW),
        token(LOW),
        token(jnp.float32),
        token(LOW),
        jax.ShapeDtypeStruct(memory.shape, LOW),
        jax.ShapeDtypeStruct(memory.shape, LOW),
        token(LOW),
        token(jnp.float32),
    ]
    outs = kept + [
        token(jnp.float32, 128),
        token(jnp.float32, 1),
        jax.ShapeDtypeStruct((count * groups, rows, 128), jnp.float32),
        token(LOW, parts * span),
        token(LOW, parts * span),
        jax.ShapeDtypeStruct(cotangent.shape, LOW),
        token(jnp.float32, 1),
        token(jnp.float32),
        jax.ShapeDtypeStruct((8, span), jnp.float32),
    ]
    wide_tile = pl.BlockSpec((total, span), lambda i: (0, jnp.clip(i - feed, 0, parts - 1)))

    results = pl.pallas_call(
        kernel,
        grid=(last + 1,),
        in_specs=[
            once_spec(tokens.shape),
            once_spec(mask.shape),
            pl.BlockSpec(memory_space=pltpu.SMEM),
            pl.BlockSpec((tile, span), lambda i: (jnp.clip(i - recall, 0, tiles - 1), 0)),
            once_spec(cotangent.shape),
        ]
        + load.in_specs(),
        out_specs=[pl.BlockSpec(memory_space=pl.ANY)] * len(kept)
        + [
            once_spec((total, 128)),
            once_spec((total, 1)),
            pl.BlockSpec((1, rows, 128), lambda i: (jnp.clip(i - look, 0, count * groups - 1), 0, 0)),
            wide_tile,
            wide_tile,
        ]
        + [once_spec(out.shape) for out in outs[len(kept) + 5 :]]
        + load.out_specs(),
        out_shape=outs + load.outs(),
        scratch_shapes=[
            pltpu.VMEM((total, span), LOW),
            pltpu.VMEM((total, span), LOW),
            pltpu.VMEM((total, span), jnp.float32),
            pltpu.VMEM((2,) + load.outs()[0].shape[1:], LOW),
            pltpu.SemaphoreType.DMA,
            pltpu.SemaphoreType.DMA((len(kept),)),
        ]
        + [pltpu.VMEM(keep.shape, keep.dtype) for keep in kept]
        + load.scratch(),
        compiler_params=params(collective_id=collective_id, has_side_effects=True),
        name="front",
    )(tokens, mask, lengths, memory, cotangent, *load.operands())
    return results[: len(outs)], load.join(results[len(outs) :])


FEED_TILE = 512


def feed_backward_kernel(
    tiles,
    grad_three,
    unit_two,
    inverse_two,
    vectors,
    hidden,
    slope,
    up,
    down,
    out_weight,
    mixed,
    feed_grad,
    bias_grad,
    grad_two,
    grad_mixed,
    out_grad,
    sums,
    low,
    branch,
    total,
):
    step = pl.program_id(0)

    @pl.when(step == 0)
    def _():
        def begin(at):
            low[at] = (unit_two[at] * vectors[8:9] + vectors[9:10]).astype(LOW)
            branch[at] = grad_three[at].astype(LOW)
            total[at] = grad_three[at]

        for_rows(total.shape[0], begin)

    grad_inner = (slope[...].astype(jnp.float32) * dot_nn(branch[...], down[0])).astype(LOW)
    feed_grad[0] = dot_tn(low[...], grad_inner).astype(LOW)
    feed_grad[1] = dot_tn(branch[...], hidden[...]).astype(LOW)
    bias_grad[...] = column_sum(grad_inner)
    total[...] += dot_nt(grad_inner, up[0])

    @pl.when(step == tiles - 1)
    def _():
        sums[...] = jnp.zeros_like(sums)

        def second_norm(at):
            grad, unit = total[at], unit_two[at]
            down_grad = norm_back(grad, unit, inverse_two[at], vectors[8:9])
            grad_two[at] = down_grad
            branch[at] = down_grad.astype(LOW)
            add_norm_sums(sums, 0, branch[at], grad, unit)

        for_rows(total.shape[0], second_norm)
        grad_mixed[...] = dot_nt(branch[...], out_weight[0]).astype(LOW)
        out_grad[...] = dot_tn(mixed[...], branch[...]).astype(LOW)


def feed_backward(grad_three, unit_two, inverse_two, vectors, hidden, slope, feed_full, cross_full, mixed):
    total, span = mixed.shape
    width = feed_full.shape[0] // 2 * span
    tiles, split = width // FEED_TILE, span // FEED_TILE
    tile = pl.BlockSpec((total, FEED_TILE), lambda j: (0, j))
    outs = [
        jax.ShapeDtypeStruct(feed_full.shape, LOW),
        jax.ShapeDtypeStruct((1, width), jnp.float32),
        jax.ShapeDtypeStruct((total, span), jnp.float32),
        jax.ShapeDtypeStruct((total, span), LOW),
        jax.ShapeDtypeStruct((span, span), LOW),
        jax.ShapeDtypeStruct((8, span), jnp.float32),
    ]
    return pl.pallas_call(
        functools.partial(feed_backward_kernel, tiles),
        grid=(tiles,),
        in_specs=[
            whole_spec(grad_three.shape),
            whole_spec(unit_two.shape),
            whole_spec(inverse_two.shape),
            whole_spec(vectors.shape),
            tile,
            tile,
            pl.BlockSpec((1, span, FEED_TILE), lambda j: (2 * (j // split), 0, j % split)),
            pl.BlockSpec((1, span, FEED_TILE), lambda j: (2 * (j // split) + 1, 0, j % split)),
            pl.BlockSpec((1, span, span), lambda j: (3, 0, 0)),
            whole_spec(mixed.shape),
        ],
        out_specs=[
            pl.BlockSpec((2, span, FEED_TILE), lambda j: (j // split, 0, j % split)),
            pl.BlockSpec((1, FEED_TILE), lambda j: (0, j)),
        ]
        + [whole_spec(out.shape) for out in outs[2:]],
        out_shape=outs,
        scratch_shapes=[
            pltpu.VMEM((total, span), LOW),
            pltpu.VMEM((total, span), LOW),
            pltpu.VMEM((total, span), jnp.float32),
        ],
        compiler_params=params(),
        name="feed_backward",
    )(grad_three, unit_two, inverse_two, vectors, hidden, slope, feed_full, feed_full, cross_full, mixed)


def cross_backward(
    reduction, query, keys, values, lengths, logs, grad_mixed, memory, cross_full, collective_id
):
    count = lengths.shape[0]
    rows, slots, span = query.shape[0] // count, keys.shape[0] // count, query.shape[1]
    groups = span // CROSS_LANES
    heads_steps = count * groups
    tiles = 4
    tile_rows, tile_lanes = keys.shape[0] // tiles, span // tiles
    last = heads_steps + tiles - 1
    carried, produced = len(reduction.operands()), len(reduction.outs())

    def kernel(*refs):
        lengths, query, keys, values, logs, grad, memory, cross_full = refs[:8]
        operands, refs = refs[8 : 8 + carried], refs[8 + carried :]
        grad_query, sums, memory_grad, weight_grad = refs[:4]
        results, refs = refs[4 : 4 + produced], refs[4 + produced :]
        stored, memory_low, weights, load_sems, scratch = *refs[:4], refs[4:]
        step = pl.program_id(0)
        loads = [
            pltpu.make_async_copy(memory, memory_low, load_sems.at[0]),
            pltpu.make_async_copy(cross_full.at[1], weights.at[0], load_sems.at[1]),
            pltpu.make_async_copy(cross_full.at[2], weights.at[1], load_sems.at[2]),
        ]

        @pl.when(step == 1)
        def _():
            for copy in loads:
                copy.start()

        @pl.when(step == heads_steps)
        def _():
            for copy in loads:
                copy.wait()

        rounds = reduction.rounds(operands, results, scratch)[0]
        plan = {0: (2,), 1: (2,), 4: (2,), 7: (2,), 9: (0,), 10: (0,), 11: (0,)}
        for start, begins in plan.items():

            @pl.when(step == start)
            def _():
                if start == 0:
                    reduction.greet()
                for begin in begins:
                    rounds.run(begin)

        @pl.when(step < heads_steps)
        def _():
            s, g = step // groups, step % groups
            slot = lax.broadcasted_iota(jnp.int32, (1, slots), 1)
            allowed = slot < lengths[s]
            sums[...] = jnp.zeros_like(sums)
            at = pl.ds(pl.multiple_of(s * slots, 16), slots)

            @pl.loop(0, CROSS_LANES // PAIR)
            def _(p):
                where = pl.ds(pl.multiple_of(p * PAIR, PAIR), PAIR)
                columns = [pick_column(logs[0], 2 * p + which) for which in range(2)]
                found = attend_pair_back(
                    query[:, where], keys[:, where], values[:, where], allowed, columns, grad[:, where]
                )
                lanes = pl.ds(pl.multiple_of(g * CROSS_LANES + p * PAIR, PAIR), PAIR)
                grad_query[:, where] = found[0]
                stored[0, at, lanes], stored[1, at, lanes] = found[1:]
                sums[0, 0:1, where] = column_sum(found[0])
                sums[0, 1:2, where] = column_sum(found[2])

        @pl.when(step >= heads_steps)
        def _():
            t = step - heads_steps
            at = pl.ds(pl.multiple_of(t * tile_rows, 16), tile_rows)
            lanes = pl.ds(pl.multiple_of(t * tile_lanes, 128), tile_lanes)
            memory_grad[...] = dot_nt(stored[0, at], weights[0]) + dot_nt(stored[1, at], weights[1])

            @pl.loop(0, 2)
            def _(number):
                product = dot_tn(memory_low[...], stored[number, :, lanes])
                weight_grad[number] = product.astype(LOW)

        @pl.when(step == last)
        def _():
            rounds.finish()

    def head(i):
        return jnp.minimum(i, heads_steps - 1)

    def later(i):
        return jnp.maximum(i - heads_steps, 0)

    token = pl.BlockSpec((rows, CROSS_LANES), lambda i: (head(i) // groups, head(i) % groups))
    held = pl.BlockSpec((slots, CROSS_LANES), lambda i: (head(i) // groups, head(i) % groups))
    return pl.pallas_call(
        kernel,
        grid=(last + 1,),
        in_specs=[
            pl.BlockSpec(memory_space=pltpu.SMEM),
            token,
            held,
            held,
            pl.BlockSpec((1, rows, 128), lambda i: (head(i), 0, 0)),
            token,
            pl.BlockSpec(memory_space=pl.ANY),
            pl.BlockSpec(memory_space=pl.ANY),
        ]
        + reduction.in_specs(),
        out_specs=[
            token,
            pl.BlockSpec((1, 8, CROSS_LANES), lambda i: (head(i) // groups, 0, head(i) % groups)),
            pl.BlockSpec((tile_rows, span), lambda i: (later(i), 0)),
            pl.BlockSpec((2, span, tile_lanes), lambda i: (0, 0, later(i))),
        ]
        + reduction.out_specs(),
        out_shape=[
            jax.ShapeDtypeStruct(query.shape, LOW),
            jax.ShapeDtypeStruct((count, 8, span), jnp.float32),
            jax.ShapeDtypeStruct(memory.shape, jnp.float32),
            jax.ShapeDtypeStruct((2, span, span), LOW),
        ]
        + reduction.outs(),
        scratch_shapes=[
            pltpu.VMEM((2,) + keys.shape, LOW),
            pltpu.VMEM(memory.shape, LOW),
            pltpu.VMEM((2, span, span), LOW),
            pltpu.SemaphoreType.DMA((3,)),
        ]
        + reduction.scratch(),
        compiler_params=params(collective_id=collective_id, has_side_effects=True),
        name="cross_backward",
    )(
        lengths, query, keys, values, logs, grad_mixed, memory, cross_full, *reduction.operands()
    )


def self_backward(
    reduction, collective_id, tokens, mask, vectors, self_full, cross_full, saved, cross_query_grad,
    grad_two, cross_sums, feed_sums, out_sums, bias_grad
):
    count, length, span = tokens.shape
    qkv, mixed, logs, unit, inverse = saved
    rows, total_rows = padded(length), mixed.shape[0]
    attend = 2
    project = attend + count
    last = project + 2
    carried, produced = len(reduction.operands()), len(reduction.outs())
    pair = reduction.parts
    fetched = (cross_query_grad, cross_full, unit, grad_two, mixed, qkv, logs, tokens)
    plan = {0: (pair,), 1: (pair,), 3: (pair,), 4: (pair,), 5: (2 * pair,), 6: (pair,)}

    def kernel(*refs):
        mask, vectors, weight, inverse, cross_sums, feed_sums, out_sums, bias_grad = refs[:8]
        sources, refs = refs[8 : 8 + len(fetched)], refs[8 + len(fetched) :]
        operands, refs = refs[:carried], refs[carried:]
        input_grad, results, refs = refs[0], refs[1 : 1 + produced], refs[1 + produced :]
        (low, grads, total, load_sems), refs = refs[:4], refs[4:]
        held, scratch = refs[: len(fetched)], refs[len(fetched) :]
        cross_query_grad, query_weight, unit, grad_two, mixed, qkv, logs, tokens = held

        def load(numbers, wait=False):
            for number in numbers:
                source = sources[number]
                if number == 1:
                    source = source.at[0]
                copy = pltpu.make_async_copy(source, held[number], load_sems.at[number])
                copy.wait() if wait else copy.start()

        step = pl.program_id(0)
        rounds, made, terms, vector_flow = reduction.rounds(operands, results, scratch)
        for start, begins in plan.items():

            @pl.when(step == start)
            def _():
                if start == 0:
                    load(range(len(fetched)))
                    reduction.greet()
                if start == project:
                    rounds.live.append(vector_flow)
                for begin in begins:
                    rounds.run(begin)

        def keep(number, product):
            made[number] = product.astype(LOW).reshape(made.shape[1:])

        @pl.when(step == 0)
        def _():
            terms[...] = jnp.zeros_like(terms)
            load(range(4), wait=True)

            def remake(at):
                grads[1, at] = (unit[at] * vectors[3:4] + vectors[4:5]).astype(LOW)

            for_rows(total_rows, remake)
            keep(0, dot_tn(grads[1], cross_query_grad[...]) * SCALE)
            total[...] = dot_nt(cross_query_grad[...], query_weight[...]) * SCALE

            def first_norm(at):
                grad = grad_two[at] + total[at]
                down_grad = norm_back(grad, unit[at], inverse[at], vectors[3:4])
                total[at] = down_grad
                grads[2, at] = down_grad.astype(LOW)
                add_norm_sums(terms, 2, grads[2, at], grad, unit[at])

            for_rows(total_rows, first_norm)
            spread = jnp.sum(cross_sums[...], axis=0)
            terms[5:6] = spread[0:1] * SCALE
            terms[6:7] = spread[1:2]
            terms[7:10] = out_sums[0:3]
            terms[10:13] = feed_sums[0:3]
            for k in range(bias_grad.shape[1] // span):
                terms[13 + k : 14 + k] = bias_grad[:, k * span : (k + 1) * span]

        @pl.when(step == 1)
        def _():
            load(range(4, len(fetched)), wait=True)
            fill_tokens(low, tokens)
            keep(1, dot_tn(mixed[...], grads[2]))
            grads[0] = dot_nt(grads[2], weight[0]).astype(LOW)

        @pl.when((step >= attend) & (step < project))
        def _():
            s = step - attend
            allowed = causal_allowed(rows, mask[pl.ds(s, 1)])
            table_at = pl.ds(pl.multiple_of(s * rows, 16), rows)

            def pair(lane, head):
                where = (table_at, pl.ds(lane, PAIR))
                table = logs[table_at]
                columns = [pick_column(table, head + which) for which in range(2)]
                found = attend_pair_back(
                    qkv[(0,) + where],
                    qkv[(1,) + where],
                    qkv[(2,) + where],
                    allowed,
                    columns,
                    grads[(0,) + where],
                )
                for number in range(3):
                    grads[(1 + number,) + where] = found[number]

            for_head_groups(span, pair)

        @pl.when(step == project - 1)
        def _():
            terms[0:1] = column_sum(grads[1]) * SCALE
            terms[1:2] = column_sum(grads[3])

        @pl.when(step >= project)
        def _():
            factor = jnp.where(step == project, SCALE, 1.0)
            part = grads[step - project + 1]
            keep(step - project + 2, dot_tn(low[...], part) * factor)
            total[...] += dot_nt(part, weight[0]) * factor

        @pl.when(step == last)
        def _():
            store_tokens(input_grad, total[...])
            rounds.finish(pair)

    small = (mask, vectors, self_full, inverse, cross_sums, feed_sums, out_sums, bias_grad)
    specs = [once_spec(operand.shape) for operand in small]
    specs[2] = pl.BlockSpec(
        (1, span, span), lambda i: (jnp.where(i < project, 3, i - project), 0, 0)
    )
    return pl.pallas_call(
        kernel,
        grid=(last + 1,),
        in_specs=specs
        + [pl.BlockSpec(memory_space=pl.ANY)] * len(fetched)
        + reduction.in_specs(),
        out_specs=[once_spec(tokens.shape)] + reduction.out_specs(),
        out_shape=[jax.ShapeDtypeStruct(tokens.shape, jnp.float32)] + reduction.outs(),
        scratch_shapes=[
            pltpu.VMEM((total_rows, span), LOW),
            pltpu.VMEM((4, total_rows, span), LOW),
            pltpu.VMEM((total_rows, span), jnp.float32),
            pltpu.SemaphoreType.DMA((len(fetched),)),
        ]
        + [
            pltpu.VMEM((span, span) if number == 1 else array.shape, array.dtype)
            for number, array in enumerate(fetched)
        ]
        + reduction.scratch(),
        compiler_params=params(collective_id=collective_id, has_side_effects=True),
        name="self_backward",
    )(*small, *fetched, *reduction.operands())


def per_device(
    wide,
    narrow,
    decoder_input,
    memory,
    decoder_mask,
    memory_length,
    self_weights,
    cross_weights,
    feed_weights,
    vectors,
    hidden_bias,
    cotangent,
):
    seq_count, seq_length, model_width = decoder_input.shape
    mem_span = memory.shape[1]
    memory_low = memory.reshape(seq_count * mem_span, model_width)
    saved, (self_full, cross_full, feed_full, vector_all, unused_bias) = front(
        Gather(
            wide, narrow, [self_weights, cross_weights, feed_weights], [vectors, hidden_bias]
        ),
        decoder_input,
        decoder_mask,
        memory_length,
        memory_low,
        cotangent,
        1,
    )
    qkv, self_mixed, unit_one, cross_query, cross_keys, cross_values, cross_mixed, unit_two = saved[:8]
    self_logs, inverse_one, cross_logs = saved[8:11]
    hidden, slope, layer_output, inverse_two, grad_three, feed_sums = saved[11:]
    feed_part, bias_part, grad_two, grad_cmixed, cross_out_grad, out_sums = feed_backward(
        grad_three, unit_two, inverse_two, vector_all, hidden, slope, feed_full, cross_full, cross_mixed
    )
    parts = feed_part.shape[0] // 2
    cross_gq, cross_sums, memory_grad, memory_parts, feed_grad = cross_backward(
        Reduction(
            wide,
            narrow,
            [feed_part],
            1,
            [(0, matrix, part) for part in range(parts) for matrix in range(2)],
            [(2, parts)],
        ),
        cross_query,
        cross_keys,
        cross_values,
        memory_length,
        cross_logs,
        grad_cmixed,
        memory_low,
        cross_full,
        2,
    )
    places = [(0, 1), (0, 2), (0, 3), (0, 0), (1, 3), (1, 0), (1, 1), (1, 2)]
    input_grad, cross_grad, self_weight_gradient, vectors_grad, hidden_bias_grad = self_backward(
        Reduction(
            wide,
            narrow,
            [memory_parts, cross_out_grad[None]],
            2,
            [place + (0,) for place in places],
            [(4, 1), (4, 1)],
            5,
            [vectors.shape, hidden_bias.shape],
        ),
        3,
        decoder_input,
        decoder_mask,
        vector_all,
        self_full,
        cross_full,
        (qkv, self_mixed, self_logs, unit_one, inverse_one),
        cross_gq,
        grad_two,
        cross_sums,
        feed_sums,
        out_sums,
        bias_part,
    )
    return (
        layer_output,
        input_grad,
        memory_grad.reshape(seq_count, mem_span, model_width),
        self_weight_gradient,
        cross_grad,
        feed_grad,
        vectors_grad,
        hidden_bias_grad,
    )


def solution(mesh):
    placed = (
        P(("wide", "narrow"), None, None),
        P(("wide", "narrow"), None, None),
        P(("wide", "narrow"), None),
        P(("wide", "narrow")),
        P(None, "wide", "narrow"),
        P(None, "wide", "narrow"),
        P(None, "wide", "narrow"),
        P(None, "narrow"),
        P(None, "narrow"),
        P(("wide", "narrow"), None, None),
    )
    return jax.shard_map(
        functools.partial(per_device, mesh.shape["wide"], mesh.shape["narrow"]),
        mesh=mesh,
        in_specs=placed,
        out_specs=(
            P(("wide", "narrow"), None, None),
            P(("wide", "narrow"), None, None),
            P(("wide", "narrow"), None, None),
            P(None, "wide", "narrow"),
            P(None, "wide", "narrow"),
            P(None, "wide", "narrow"),
            P(None, "narrow"),
            P(None, "narrow"),
        ),
        check_vma=False,
    )
```

```python
import functools
import math

import jax
import jax.numpy as jnp
from jax import lax
from jax.experimental import pallas as pl
from jax.experimental.pallas import tpu as pltpu
from jax.sharding import PartitionSpec as P

HEADS = 16
HEAD_DIM = 64


MESH_ID = pl.DeviceIdType.MESH


class Position:
    def __init__(self, wide, narrow):
        self.sizes = {"line": wide // 4, "pair": 2, "core": 2, "column": narrow}

    def get(self, axis):
        if axis == "column":
            return lax.axis_index("narrow")
        index = lax.axis_index("wide")
        if axis == "core":
            return index % 2
        return (index // 2) % 2 if axis == "pair" else index // 4

    def device(self, **moved):
        spot = {name: moved.get(name, self.get(name)) for name in self.sizes}
        return (spot["line"] * 4 + spot["pair"] * 2 + spot["core"], spot["column"])


class Channels:
    def __init__(self, sends, recvs):
        self.sends, self.recvs, self.used = sends, recvs, 0

    def take(self):
        self.used += 1
        number = self.used - 1
        return lambda: (self.sends.at[number], self.recvs.at[number])


def remote(source, target, channel, device):
    return pltpu.make_async_remote_copy(
        src_ref=source,
        dst_ref=target,
        send_sem=channel()[0],
        recv_sem=channel()[1],
        device_id=device,
        device_id_type=MESH_ID,
    )


def flip(index, bit):
    return index + bit - 2 * bit * ((index // bit) % 2)


def peers(position, axis, distance):
    at = (position.get(axis) + distance) % position.sizes[axis]
    return at, position.device(**{axis: at})


def greet(position):
    barrier = pltpu.get_barrier_semaphore()
    expected = 0
    for axis, size in position.sizes.items():
        for distance in range(1, size):
            pl.semaphore_signal(
                barrier,
                inc=1,
                device_id=peers(position, axis, distance)[1],
                device_id_type=MESH_ID,
            )
            expected += 1
    pl.semaphore_wait(barrier, expected)


def advance(generator):
    return next(generator, "done") != "done"


class Rounds:
    def __init__(self, flows, live=()):
        self.waiting, self.live = list(flows), list(live)
        self.all, self.first = None, []

    def run(self, start=0):
        self.live = self.live + self.waiting[:start]
        self.waiting = self.waiting[start:]
        self.live = [flow for flow in self.live if advance(flow)]

    def move(self, groups, size=2):
        if self.all is None:
            self.all = [*self.waiting]
            self.waiting, self.first, self.live = [], self.live, list(self.all)
        for group in groups:
            self.first = [flow for flow in self.first if advance(flow)]
            for flow in self.all[group * size : group * size + size]:
                if not advance(flow):
                    self.live.remove(flow)

    def finish(self, together=2):
        self.live, self.first = self.live + self.first, []
        while self.waiting or self.live:
            self.run(together)


def finish_sends(sent):
    for describe in sent:
        describe().wait_send()


def gather_axis(position, axis, channels, block, own, sent):
    arrivals = []
    for distance in range(1, position.sizes[axis]):
        channel = channels.take()

        def send(distance=distance, channel=channel):
            device = peers(position, axis, distance)[1]
            return remote(own(), block(position.get(axis)), channel, device)

        def arrival(distance=distance, channel=channel):
            came, device = peers(position, axis, -distance)
            return remote(block(came), block(came), channel, device)

        send().start()
        sent.append(send)
        arrivals.append(arrival)
    yield
    for arrival in arrivals:
        arrival().wait_recv()


def gather_flow(position, channels, local_sem, own, region, order):
    sent = []

    def place(done, axis=None, at=None):
        spot = {name: None if name in done else position.get(name) for name in position.sizes}
        if axis is not None:
            spot[axis] = at
        return region(**spot)

    def local():
        return pltpu.make_async_copy(own(), place(()), local_sem())

    local().start()
    for number, axis in enumerate(order):
        done = order[:number]

        def block(j, axis=axis, done=done):
            return place(done, axis, j)

        def source(block=block, axis=axis, first=number == 0):
            return own() if first else block(position.get(axis))

        yield from gather_axis(position, axis, channels, block, source, sent)
        if number == 0:
            local().wait()
    finish_sends(sent)


def whole(index):
    return slice(None) if index is None else index


def row_splits(rows, most):
    return max(1, min(most, rows // 16))


def flow_channels(wide, narrow):
    return 2 + (wide // 4 - 1) + (narrow - 1)


ORDER_A = ("line", "pair", "column", "core")
ORDER_B = ("line", "column", "pair", "core")


def lane_parts(wide, narrow, block):
    return block.shape[2] * narrow // (block.shape[1] * wide)


def gather_flows(position, channels, local_sems, parts, blocks, fulls):
    flows = []
    for block_ref, full_ref, count in zip(blocks, fulls, parts):
        width = block_ref.shape[2] // count
        for place in range(full_ref.shape[0]):
            part, matrix = divmod(place, block_ref.shape[0])

            def region(line, pair, core, column, full_ref=full_ref, place=place, width=width):
                lanes = slice(None)
                if column is not None:
                    lanes = pl.ds(pl.multiple_of(column * width, 128), width)
                return full_ref.at[place, whole(line), whole(pair), whole(core), :, lanes]

            def own(block_ref=block_ref, matrix=matrix, part=part, width=width):
                return block_ref.at[matrix, :, part * width : (part + 1) * width]

            number = len(flows)
            order = ORDER_A if number % 2 == 0 else ORDER_B
            flows.append(
                gather_flow(
                    position, channels, lambda number=number: local_sems.at[number], own, region, order
                )
            )
    return flows


def column_flow(position, channels, sem, block_ref, full_ref):
    width = block_ref.shape[1]

    def region(column):
        return full_ref.at[:, pl.ds(pl.multiple_of(column * width, 128), width)]

    def local():
        return pltpu.make_async_copy(block_ref, region(position.get("column")), sem())

    sent = []
    local().start()
    yield from gather_axis(position, "column", channels, region, lambda: block_ref, sent)
    local().wait()
    finish_sends(sent)


class Gather:
    def __init__(self, wide, narrow, arrays, vectors=()):
        self.wide, self.narrow = wide, narrow
        self.arrays, self.vectors = list(arrays), list(vectors)
        self.parts = [lane_parts(wide, narrow, array) for array in arrays]
        self.count = sum(array.shape[0] * part for array, part in zip(arrays, self.parts))

    def operands(self):
        return self.arrays + self.vectors

    def in_specs(self):
        return [pl.BlockSpec(memory_space=pltpu.VMEM)] * len(self.operands())

    def wholes(self):
        return [(vector.shape[0], vector.shape[1] * self.narrow) for vector in self.vectors]

    def outs(self):
        outs = []
        for array, part in zip(self.arrays, self.parts):
            matrices, rows, width = array.shape
            shape = (matrices * part, self.wide // 4, 2, 2, rows, width // part * self.narrow)
            outs.append(jax.ShapeDtypeStruct(shape, array.dtype))
        return outs + [jax.ShapeDtypeStruct(shape, jnp.float32) for shape in self.wholes()]

    def out_specs(self):
        specs = [pl.BlockSpec(memory_space=pl.ANY)] * len(self.arrays)
        return specs + [pl.BlockSpec(memory_space=pltpu.VMEM)] * len(self.vectors)

    def scratch(self):
        flows = self.count + len(self.vectors)
        copies = flow_channels(self.wide, self.narrow) * flows
        return [
            pltpu.SemaphoreType.DMA((copies,)),
            pltpu.SemaphoreType.DMA((copies,)),
            pltpu.SemaphoreType.DMA((flows,)),
        ] + [pltpu.VMEM(shape, jnp.float32) for shape in self.wholes()]

    def rounds(self, operands, outs, scratch):
        position = Position(self.wide, self.narrow)
        channels = Channels(scratch[0], scratch[1])
        count, local_sems, wholes = len(self.arrays), scratch[2], scratch[3:]
        live = [
            column_flow(
                position,
                channels,
                lambda k=k: local_sems.at[self.count + k],
                operands[count + k],
                wholes[k],
            )
            for k in range(len(self.vectors))
        ]
        flows = gather_flows(
            position, channels, local_sems, self.parts, operands[:count], outs[:count]
        )
        return Rounds(flows, live), wholes

    def greet(self):
        greet(Position(self.wide, self.narrow))

    def join(self, results):
        count = len(self.arrays)
        fulls = [full.reshape(full.shape[0], -1, full.shape[-1]) for full in results[:count]]
        return fulls + list(results[count:])


def add_rows(target, parts):
    lead = target.shape[:-2]
    count = math.prod(lead)

    def add(spot):
        total = parts[0][spot].astype(jnp.float32)
        for part in parts[1:]:
            total = total + part[spot].astype(jnp.float32)
        target[spot] = total.astype(target.dtype)

    if count == 1:
        add((0,) * len(lead))
        return

    @pl.loop(0, count)
    def _(k):
        where = []
        for extent in reversed(lead):
            where.insert(0, k % extent)
            k = k // extent
        add(tuple(where))


def reduce_axis(position, axis, channels, local, slots, result, sent):
    size = position.sizes[axis]
    for distance in range(1, size):
        channel = channels.take()

        def send(distance=distance, channel=channel):
            at, device = peers(position, axis, distance)
            return remote(local(at), slots.at[distance - 1], channel, device)

        send().start()
        sent.append(send)
    yield
    for send in sent[1 - size :]:
        send().wait_recv()
    add_rows(
        result(), [local(position.get(axis))] + [slots.at[k] for k in range(size - 1)]
    )


def reduce_flow(position, channels, local_sem, loc, grads, result, buffers, order):
    first, mid, last, line_slots = buffers
    sent = []

    def own():
        return pltpu.make_async_copy(grads(position.get("core")), loc(), local_sem())

    def mine():
        return grads(position.get("core")) if loc is None else loc()

    channel = channels.take()

    def swap():
        core = position.get("core")
        return remote(grads(1 - core), first, channel, position.device(core=1 - core))

    if loc is not None:
        own().start()
    swap().start()
    yield
    if loc is not None:
        own().wait()
    swap().wait_recv()
    add_rows(first, [first, mine()])
    swap().wait_send()
    width = result().shape[-1]

    def columns(j):
        return pl.ds(pl.multiple_of(j * width, 128), width)

    def held():
        return mid.at[0]

    def final():
        return last.at[0]

    if order == "A":
        yield from reduce_axis(
            position, "column", channels, lambda j: first.at[:, :, :, columns(j)], mid, held, sent
        )
        yield from reduce_axis(position, "pair", channels, lambda j: held().at[:, j], last, final, sent)
    else:
        yield from reduce_axis(position, "pair", channels, lambda j: first.at[:, j], mid, held, sent)
        yield from reduce_axis(
            position, "column", channels, lambda j: held().at[:, :, columns(j)], last, final, sent
        )
    yield from reduce_axis(
        position, "line", channels, lambda j: final().at[pl.ds(j, 1)], line_slots, result, sent
    )
    finish_sends(sent)


def double_flow(position, channels, terms, total, inbox, vectors_out, bias_out):
    total[0] = terms[...]
    step = 0
    for axis in ("core", "pair", "line", "column"):
        bit = 1
        while bit < position.sizes[axis]:
            channel = channels.take()

            def describe():
                to = position.device(**{axis: flip(position.get(axis), bit)})
                return remote(total.at[step], inbox.at[step], channel, to)

            describe().start()
            yield
            describe().wait_recv()
            total[step + 1] = total[step] + inbox[step]
            describe().wait_send()
            bit *= 2
            step += 1
    count, width = vectors_out.shape
    lanes = pl.ds(pl.multiple_of(position.get("column") * width, 128), width)
    vectors_out[...] = total[step, 0:count, lanes]
    for k in range(bias_out.shape[1] // width):
        bias_out[:, k * width : (k + 1) * width] = total[step, count + k : count + k + 1, lanes]


class Reduction:
    RING = 6

    def __init__(self, wide, narrow, depth, arrays, parts, places, matrices, held=(), shapes=()):
        self.wide, self.narrow, self.held, self.shapes = wide, narrow, held, list(shapes)
        depth = span = depth
        self.rows = rows = depth // wide
        self.parts = row_splits(rows, parts)
        self.piece = rows // self.parts
        self.line, self.span, self.width = wide // 4, span, span // narrow
        self.matrices = matrices
        sources = [(s, m) for s, array in enumerate(arrays) for m in range(array.shape[0])]
        sources += [(None, m) for m in held]
        self.pieces = [
            source + (part,) + place
            for source, place in zip(sources, places)
            for part in range(self.parts)
        ]
        self.views = [array.reshape(array.shape[0], self.line, 2, 2, rows, span) for array in arrays]

    def order(self, number):
        return "A" if number % 2 == 0 else "B"

    def operands(self):
        return self.views

    def in_specs(self):
        return [pl.BlockSpec(memory_space=pl.ANY)] * len(self.views)

    def outs(self):
        outs = [
            jax.ShapeDtypeStruct((count, self.rows, self.width * parts), jnp.float32)
            for count, parts in self.matrices
        ]
        return outs + [jax.ShapeDtypeStruct(shape, jnp.float32) for shape in self.shapes]

    def out_specs(self):
        return [pl.BlockSpec(memory_space=pltpu.VMEM)] * len(self.outs())

    def steps(self):
        return (self.wide * self.narrow).bit_length() - 1

    def terms_shape(self):
        count = self.shapes[0][0] + self.shapes[1][1] * self.narrow // self.span
        return (count + -count % 8, self.span)

    def scratch(self):
        low, line, piece = jnp.bfloat16, self.line, self.piece
        copies = flow_channels(self.wide, self.narrow) * len(self.pieces) + 16
        shapes = [
            pltpu.SemaphoreType.DMA((copies,)),
            pltpu.SemaphoreType.DMA((copies,)),
            pltpu.SemaphoreType.DMA((len(self.pieces),)),
            pltpu.VMEM((self.RING, line, 2, piece, self.span), low)
            if self.views
            else pltpu.VMEM((8, 128), low),
        ]
        if self.held:
            shapes.append(pltpu.VMEM((1 + max(self.held), line, 2, 2, self.rows, self.span), low))
        if self.shapes:
            shapes.append(pltpu.VMEM(self.terms_shape(), jnp.float32))
            shapes.append(pltpu.VMEM((self.steps() + 1,) + self.terms_shape(), jnp.float32))
            shapes.append(pltpu.VMEM((self.steps(),) + self.terms_shape(), jnp.float32))
        for number in range(len(self.pieces)):
            shapes.append(pltpu.VMEM((line, 2, piece, self.span), low))
            if self.order(number) == "A":
                shapes.append(pltpu.VMEM((self.narrow - 1, line, 2, piece, self.width), low))
                shapes.append(pltpu.VMEM((1, line, piece, self.width), low))
            else:
                shapes.append(pltpu.VMEM((1, line, piece, self.span), low))
                shapes.append(pltpu.VMEM((self.narrow - 1, line, piece, self.width), low))
            shapes.append(pltpu.VMEM((line - 1, 1, piece, self.width), low))
        return shapes

    def rounds(self, operands, outs, scratch):
        position = Position(self.wide, self.narrow)
        channels = Channels(scratch[0], scratch[1])
        local_sems, ring, buffers = scratch[2], scratch[3], list(scratch[4:])
        made = buffers.pop(0) if self.held else None
        terms, vector_flow = None, None
        if self.shapes:
            terms, total, inbox = buffers[:3]
            buffers = buffers[3:]
            vector_flow = double_flow(position, channels, terms, total, inbox, *outs[-2:])
        flows = []
        for number, (source, inner, part, out, matrix, slot) in enumerate(self.pieces):
            at = pl.ds(part * self.piece, self.piece)
            lanes = pl.ds(slot * self.width, self.width)

            def grads(core, source=source, inner=inner, at=at):
                array = made if source is None else operands[source]
                return array.at[inner, :, :, core, at]

            flows.append(
                reduce_flow(
                    position,
                    channels,
                    lambda number=number: local_sems.at[number],
                    None if source is None else lambda number=number: ring.at[number % self.RING],
                    grads,
                    lambda out=out, at=(pl.ds(matrix, 1), at, lanes): outs[out].at[at],
                    buffers[4 * number : 4 * number + 4],
                    self.order(number),
                )
            )
        return Rounds(flows), made, terms, vector_flow

    def greet(self):
        greet(Position(self.wide, self.narrow))


LOW = jnp.bfloat16
NEGATIVE = -1000000000.0
EPSILON = 1e-05
PAIR = 2 * HEAD_DIM
SCALE = HEAD_DIM ** (-0.5)
BUDGET = 65000 * 1024


def dot_nn(left, right):
    return jnp.dot(left, right, preferred_element_type=jnp.float32)


def dot_nt(left, right):
    return lax.dot_general(
        left, right, (((1,), (1,)), ((), ())), preferred_element_type=jnp.float32
    )


def dot_tn(left, right):
    return lax.dot_general(
        left, right, (((0,), (0,)), ((), ())), preferred_element_type=jnp.float32
    )


def padded(length):
    return -(-length // 16) * 16


def column_sum(rows):
    return jnp.sum(rows.astype(jnp.float32), axis=0, keepdims=True)


def standardise(hidden):
    centre = hidden - jnp.mean(hidden, axis=-1, keepdims=True)
    spread = jnp.mean(centre * centre, axis=-1, keepdims=True)
    inverse = lax.rsqrt(spread + EPSILON)
    return centre * inverse, inverse


def norm_back(grad, unit, inverse, gain):
    scaled = grad * gain
    first = jnp.mean(scaled, axis=-1, keepdims=True)
    second = jnp.mean(scaled * unit, axis=-1, keepdims=True)
    return inverse * (scaled - first - unit * second)


def for_rows(total, function):
    chunk = next(size for size in (48, 64, 32, 16) if total % size == 0)

    @pl.loop(0, total // chunk)
    def _(k):
        function(pl.ds(pl.multiple_of(k * chunk, 16), chunk))


def add_norm_sums(sums, first, low, grad, unit):
    sums[first : first + 1] += column_sum(low)
    sums[first + 1 : first + 2] += column_sum(grad * unit)
    sums[first + 2 : first + 3] += column_sum(grad)


def fill_tokens(target, source):
    count, length, span = source.shape
    rows = padded(length)
    for s in range(count):
        if rows > length:
            base = s * rows + length // 16 * 16
            target[base : (s + 1) * rows] = jnp.zeros(((s + 1) * rows - base, span), target.dtype)
        target[s * rows : s * rows + length] = source[s].astype(target.dtype)


def store_tokens(target, values):
    count, length, span = target.shape
    rows = padded(length)
    for s in range(count):
        target[s] = values[s * rows : s * rows + length].astype(target.dtype)


def head_lanes(rows, which):
    lane = lax.broadcasted_iota(jnp.int32, rows.shape, 1)
    return (lane >= HEAD_DIM) == (which == 1)


def one_head(rows, which):
    return jnp.where(head_lanes(rows, which), rows, jnp.zeros_like(rows))


def pick_column(table, number):
    lane = lax.broadcasted_iota(jnp.int32, table.shape, 1)
    return jnp.sum(jnp.where(lane == number, table, 0.0), axis=1, keepdims=True)


def attend_pair(query, keys, values, allowed):
    mixed, logs = [], []
    for which in range(2):
        scores = dot_nt(one_head(query, which), keys)
        scores = jnp.where(allowed, scores, NEGATIVE)
        peak = jnp.max(scores, axis=-1, keepdims=True)
        expo = jnp.exp(scores - peak)
        total = jnp.sum(expo, axis=-1, keepdims=True)
        weights = (expo * (1.0 / total)).astype(LOW)
        mixed.append(dot_nn(weights, values))
        logs.append(peak + jnp.log(total))
    both = jnp.where(head_lanes(mixed[0], 0), mixed[0], mixed[1])
    return both.astype(LOW), logs


def attend_pair_back(query, keys, values, allowed, logs, grad):
    grad_query, grad_keys, grad_values = [], None, None
    for which in range(2):
        query_one, grad_one = one_head(query, which), one_head(grad, which)
        scores = jnp.where(allowed, dot_nt(query_one, keys), NEGATIVE)
        probs = jnp.exp(scores - logs[which])
        grad_probs = dot_nt(grad_one, values)
        slope = jnp.sum(grad_probs * probs, axis=-1, keepdims=True)
        grad_scores = (probs * (grad_probs - slope)).astype(LOW)
        grad_query.append(dot_nn(grad_scores, keys))
        part_keys = dot_tn(grad_scores, query_one)
        part_values = dot_tn(probs.astype(LOW), grad_one)
        grad_keys = part_keys if which == 0 else grad_keys + part_keys
        grad_values = part_values if which == 0 else grad_values + part_values
    both = jnp.where(head_lanes(grad_query[0], 0), grad_query[0], grad_query[1])
    return both.astype(LOW), grad_keys.astype(LOW), grad_values.astype(LOW)


def causal_allowed(rows, mask_row):
    valid = jnp.sum(mask_row, axis=-1, keepdims=True)
    query_at = lax.broadcasted_iota(jnp.int32, (rows, rows), 0)
    key_at = lax.broadcasted_iota(jnp.int32, (rows, rows), 1)
    return (query_at >= key_at) & (key_at < valid)


GROUP_PAIRS = 2


def for_head_groups(span, function):
    lanes = min(span, GROUP_PAIRS * PAIR)

    @pl.loop(0, span // lanes)
    def _(g):
        for p in range(lanes // PAIR):
            function(pl.multiple_of(g * lanes + p * PAIR, PAIR), 2 * (g * (lanes // PAIR) + p))


def whole_spec(shape):
    return pl.BlockSpec(shape, lambda *at: (0,) * len(shape))


def params(**more):
    return pltpu.CompilerParams(vmem_limit_bytes=BUDGET, **more)


CROSS_LANES = 2 * PAIR


def once_spec(shape):
    return pl.BlockSpec(shape, lambda *at: (0,) * len(shape), pipeline_mode=pl.Buffered(1))


def front(load, tokens, mask, lengths, memory, cotangent, collective_id):
    count, length, span = tokens.shape
    rows = padded(length)
    total, slots = count * rows, memory.shape[0] // count
    tiles = 4
    tile = memory.shape[0] // tiles
    groups = span // CROSS_LANES
    attend, join, ask = 3, 3 + count, 4 + count
    recall = ask + 1
    look = recall + tiles
    add = look + count * groups
    feed = add + 1
    parts = load.parts[2]
    last = feed + parts - 1
    carried = len(load.operands())
    plan = {
        0: (0, 0, 1, 0, 1, 2, 0, 1, 2, 3, 0),
        2: (1, 2, 3, 4, 1),
        ask: (2, 3, 4, 5, 2),
        recall: (3, 4, 5, 6, 3),
        look: (4, 5, 6, 7),
        look + 5: (4, 5, 6, 7),
        feed + 1: (5, 6, 7),
        feed + 2: (6,),
        feed + 3: (7, 7),
    }

    def kernel(*refs):
        tokens, mask, lengths, memory, cotangent = refs[:5]
        operands, refs = refs[5 : 5 + carried], refs[5 + carried :]
        stored, (logs, inverse, cross_logs) = refs[: len(kept)], refs[len(kept) : len(kept) + 3]
        hidden, slope, output, inverse_two, grad_three, sums = refs[len(kept) + 3 : len(kept) + 9]
        refs = refs[len(kept) + 9 :]
        results, refs = refs[:carried], refs[carried:]
        low, spare, running, weights, weight_sem, store_sems = refs[:6]
        held, scratch = refs[6 : 6 + len(kept)], refs[6 + len(kept) :]
        qkv, mixed, unit, query, keys, values, cross_mixed, unit_two = held
        step = pl.program_id(0)
        rounds, (vectors, bias) = load.rounds(operands, results, scratch)
        for start, begins in plan.items():

            @pl.when(step == start)
            def _():
                if start == 0:
                    load.greet()
                rounds.move(begins)

        def store(*numbers, wait=False):
            for number in numbers:
                copy = pltpu.make_async_copy(
                    held[number], stored[number], store_sems.at[number]
                )
                copy.wait() if wait else copy.start()

        @pl.when(step == recall)
        def _():
            store(0, 1, 2, 3)

        @pl.when(step == look)
        def _():
            store(4, 5)

        @pl.when(step == feed)
        def _():
            store(6, 7)

        def fetch(array, matrix, slot):
            copy = pltpu.make_async_copy(results[array].at[matrix], weights.at[slot], weight_sem)
            copy.start()
            copy.wait()

        def weight(slot):
            return weights[slot].reshape(span, span)

        @pl.when(step == 0)
        def _():
            fill_tokens(low, tokens)

        @pl.when(step < attend)
        def _():
            fetch(0, step, 0)
            product = dot_nn(low[...], weight(0))
            none = jnp.zeros_like(vectors[0:1])
            shift = jnp.where(step == 0, vectors[0:1], jnp.where(step == 2, vectors[1:2], none))
            product = (product + shift) * jnp.where(step == 0, SCALE, 1.0)
            qkv[step] = product.astype(LOW)

        @pl.when((step >= attend) & (step < join))
        def _():
            s = step - attend
            allowed = causal_allowed(rows, mask[pl.ds(s, 1)])
            table_at = pl.ds(pl.multiple_of(s * rows, 16), rows)
            logs[table_at] = jnp.zeros((rows, 128), jnp.float32)

            def pair(lane, head):
                where = (table_at, pl.ds(lane, PAIR))
                both, sums = attend_pair(
                    qkv[(0,) + where], qkv[(1,) + where], qkv[(2,) + where], allowed
                )
                mixed[where] = both
                table = logs[table_at]
                spot = lax.broadcasted_iota(jnp.int32, table.shape, 1)
                for which in range(2):
                    table = jnp.where(spot == head + which, sums[which], table)
                logs[table_at] = table

            for_head_groups(span, pair)

        @pl.when(step == join)
        def _():
            fetch(0, 3, 0)
            running[...] = dot_nn(mixed[...], weight(0))

            def first_norm(at):
                summed = low[at].astype(jnp.float32) + (running[at] + vectors[2:3])
                found, inverse[at] = standardise(summed)
                unit[at] = found
                spare[at] = (found * vectors[3:4] + vectors[4:5]).astype(LOW)

            for_rows(total, first_norm)

        @pl.when(step == ask)
        def _():
            fetch(1, 0, 0)
            product = dot_nn(spare[...], weight(0))
            query[...] = ((product + vectors[5:6]) * SCALE).astype(LOW)

        @pl.when(step == recall)
        def _():
            fetch(1, 1, 0)
            fetch(1, 2, 1)

        @pl.when((step >= recall) & (step < look))
        def _():
            at = pl.ds(pl.multiple_of((step - recall) * tile, 16), tile)
            keys[at] = dot_nn(memory[...], weight(0)).astype(LOW)
            values[at] = (dot_nn(memory[...], weight(1)) + vectors[6:7]).astype(LOW)

        @pl.when((step >= look) & (step < add))
        def _():
            s, g = (step - look) // groups, (step - look) % groups
            slot = lax.broadcasted_iota(jnp.int32, (1, slots), 1)
            allowed = slot < lengths[s]
            token_at = pl.ds(pl.multiple_of(s * rows, 16), rows)
            slot_at = pl.ds(pl.multiple_of(s * slots, 16), slots)
            cross_logs[...] = jnp.zeros_like(cross_logs)

            @pl.loop(0, CROSS_LANES // PAIR)
            def _(p):
                lanes = pl.ds(pl.multiple_of(g * CROSS_LANES + p * PAIR, PAIR), PAIR)
                both, sums = attend_pair(
                    query[token_at, lanes], keys[slot_at, lanes], values[slot_at, lanes], allowed
                )
                cross_mixed[token_at, lanes] = both
                table = cross_logs[0]
                spot = lax.broadcasted_iota(jnp.int32, table.shape, 1)
                for which in range(2):
                    table = jnp.where(spot == 2 * p + which, sums[which], table)
                cross_logs[0] = table

        @pl.when(step == add)
        def _():
            fetch(1, 3, 0)
            running[...] = dot_nn(cross_mixed[...], weight(0))

            def second_norm(at):
                first = unit[at] * vectors[3:4] + vectors[4:5]
                found, inverse_two[at] = standardise(first + (running[at] + vectors[7:8]))
                unit_two[at] = found
                low[at] = (found * vectors[8:9] + vectors[9:10]).astype(LOW)
                running[at] = jnp.zeros_like(found)

            for_rows(total, second_norm)
            fill_tokens(spare, cotangent)

        @pl.when(step >= feed)
        def _():
            part = step - feed
            fetch(2, 2 * part, 0)
            fetch(2, 2 * part + 1, 1)
            width = bias.shape[1] // parts // load.narrow
            shift = jnp.concatenate(
                [
                    bias[:, pl.ds(pl.multiple_of((n * parts + part) * width, 128), width)]
                    for n in range(load.narrow)
                ],
                axis=1,
            )
            half_lanes = span // 2
            row = lax.broadcasted_iota(jnp.int32, (8, span), 0)
            sums[...] = jnp.where(row == 0, shift, 0.0)

            @pl.loop(0, 2)
            def _(k):
                lanes = pl.ds(pl.multiple_of(k * half_lanes, 128), half_lanes)
                up = weights[0, :, :, :, :, lanes].reshape(span, half_lanes)
                down = weights[1, :, :, :, :, lanes].reshape(span, half_lanes)
                inner = dot_nn(low[...], up) + sums[0:1, lanes]
                half = 0.5 + 0.5 * lax.erf(inner * (0.5**0.5))
                bell = jnp.exp(-0.5 * inner * inner) * ((0.5 / math.pi) ** 0.5)
                active = (inner * half).astype(LOW)
                hidden[:, lanes] = active
                slope[:, lanes] = (half + inner * bell).astype(LOW)
                running[...] += dot_nt(active, down)

        @pl.when(step == last)
        def _():
            rounds.finish()
            results[-2][...], results[-1][...] = vectors[...], bias[...]
            sums[...] = jnp.zeros_like(sums)

            def third_norm(at):
                second = unit_two[at] * vectors[8:9] + vectors[9:10]
                found, inverse_three = standardise(second + (running[at] + vectors[10:11]))
                low[at] = (found * vectors[11:12] + vectors[12:13]).astype(LOW)
                grad = spare[at].astype(jnp.float32)
                down_grad = norm_back(grad, found, inverse_three, vectors[11:12])
                grad_three[at] = down_grad
                add_norm_sums(sums, 0, down_grad.astype(LOW), grad, found)

            for_rows(total, third_norm)
            store_tokens(output, low)
            store(*range(len(kept)), wait=True)

    def token(dtype, lanes=span):
        return jax.ShapeDtypeStruct((total, lanes), dtype)

    kept = [
        jax.ShapeDtypeStruct((3, total, span), LOW),
        token(LOW),
        token(jnp.float32),
        token(LOW),
        jax.ShapeDtypeStruct(memory.shape, LOW),
        jax.ShapeDtypeStruct(memory.shape, LOW),
        token(LOW),
        token(jnp.float32),
    ]
    outs = kept + [
        token(jnp.float32, 128),
        token(jnp.float32, 1),
        jax.ShapeDtypeStruct((count * groups, rows, 128), jnp.float32),
        token(LOW, parts * span),
        token(LOW, parts * span),
        jax.ShapeDtypeStruct(cotangent.shape, LOW),
        token(jnp.float32, 1),
        token(jnp.float32),
        jax.ShapeDtypeStruct((8, span), jnp.float32),
    ]
    wide_tile = pl.BlockSpec((total, span), lambda i: (0, jnp.clip(i - feed, 0, parts - 1)))

    results = pl.pallas_call(
        kernel,
        grid=(last + 1,),
        in_specs=[
            once_spec(tokens.shape),
            once_spec(mask.shape),
            pl.BlockSpec(memory_space=pltpu.SMEM),
            pl.BlockSpec((tile, span), lambda i: (jnp.clip(i - recall, 0, tiles - 1), 0)),
            once_spec(cotangent.shape),
        ]
        + load.in_specs(),
        out_specs=[pl.BlockSpec(memory_space=pl.ANY)] * len(kept)
        + [
            once_spec((total, 128)),
            once_spec((total, 1)),
            pl.BlockSpec((1, rows, 128), lambda i: (jnp.clip(i - look, 0, count * groups - 1), 0, 0)),
            wide_tile,
            wide_tile,
        ]
        + [once_spec(out.shape) for out in outs[len(kept) + 5 :]]
        + load.out_specs(),
        out_shape=outs + load.outs(),
        scratch_shapes=[
            pltpu.VMEM((total, span), LOW),
            pltpu.VMEM((total, span), LOW),
            pltpu.VMEM((total, span), jnp.float32),
            pltpu.VMEM((2,) + load.outs()[0].shape[1:], LOW),
            pltpu.SemaphoreType.DMA,
            pltpu.SemaphoreType.DMA((len(kept),)),
        ]
        + [pltpu.VMEM(keep.shape, keep.dtype) for keep in kept]
        + load.scratch(),
        compiler_params=params(collective_id=collective_id, has_side_effects=True),
        name="front",
    )(tokens, mask, lengths, memory, cotangent, *load.operands())
    return results[: len(outs)], load.join(results[len(outs) :])


FEED_TILE = 512


def middle_backward(
    reduction, grad_three, unit_two, inverse_two, vectors, hidden, slope, feed_full, cross_full, mixed,
    query, keys, values, lengths, logs, memory, collective_id
):
    count = lengths.shape[0]
    total_rows, span = query.shape
    rows, slots = total_rows // count, keys.shape[0] // count
    groups = span // CROSS_LANES
    split = span // FEED_TILE
    feeds = feed_full.shape[0] // 2 * split
    heads, recall = feeds, feeds + count * groups
    tiles = 2 * count
    tile_rows, tile_lanes = keys.shape[0] // tiles, span // tiles
    last = recall + tiles - 1
    carried, produced = len(reduction.operands()), len(reduction.outs())
    plan = {
        2: (0,),
        3: (0,),
        4: (1,),
        6: (1,),
        7: (2,),
        heads: (3, 0, 1, 2, 3),
        heads + 1: (0,),
        heads + 2: (1,),
        heads + 6: (2,),
        heads + 7: (0,),
        recall: (2, 3),
        recall + 1: (3,),
        last: (1, 2, 3),
    }

    def kernel(*refs):
        lengths, unit_two, inverse_two, vectors, hidden, slope, up, down, mixed = refs[:9]
        query, keys, values, logs, grad_three, memory, cross_full = refs[9:16]
        operands, refs = refs[16 : 16 + carried], refs[16 + carried :]
        bias_grad, grad_two, out_grad, feed_sums, grad_query, sums = refs[:6]
        memory_grad, weight_grad = refs[6:8]
        results, refs = refs[8 : 8 + produced], refs[8 + produced :]
        low, branch, total, memory_low, weights, load_sems, scratch = *refs[:6], refs[6:]
        step = pl.program_id(0)
        rounds, made, *unused = reduction.rounds(operands, results, scratch)

        def load(number, wait=False):
            source, target = (
                (grad_three, total),
                (cross_full.at[3], weights.at[0]),
                (memory, memory_low),
                (cross_full.at[1], weights.at[0]),
                (cross_full.at[2], weights.at[1]),
            )[number]
            copy = pltpu.make_async_copy(source, target, load_sems.at[number])
            copy.wait() if wait else copy.start()

        @pl.when(step == 0)
        def _():
            load(0)
            load(1)
            reduction.greet()

            def begin(at):
                low[at] = (unit_two[at] * vectors[8:9] + vectors[9:10]).astype(LOW)
                branch[at] = total[at].astype(LOW)

            load(0, wait=True)
            for_rows(total_rows, begin)

        @pl.when(step == heads)
        def _():
            for number in (2, 3, 4):
                load(number)

        for start, begins in plan.items():

            @pl.when(step == start)
            def _():
                rounds.move(begins)

        @pl.when(step == recall)
        def _():
            for number in (2, 3, 4):
                load(number, wait=True)

        @pl.when(step < feeds)
        def _():
            lanes = pl.ds(pl.multiple_of(step % split * FEED_TILE, 128), FEED_TILE)
            place = 2 * (step // split % 2)
            inner = dot_nn(branch[...], down[0])
            grad_inner = (slope[...].astype(jnp.float32) * inner).astype(LOW)
            shape = made.shape[1:-1] + (FEED_TILE,)
            made[place, :, :, :, :, lanes] = dot_tn(low[...], grad_inner).astype(LOW).reshape(shape)
            made[place + 1, :, :, :, :, lanes] = (
                dot_tn(branch[...], hidden[...]).astype(LOW).reshape(shape)
            )
            bias_grad[...] = column_sum(grad_inner)
            total[...] += dot_nt(grad_inner, up[0])

        @pl.when(step == feeds - 1)
        def _():
            feed_sums[...] = jnp.zeros_like(feed_sums)

            def second_norm(at):
                grad, unit = total[at], unit_two[at]
                down_grad = norm_back(grad, unit, inverse_two[at], vectors[8:9])
                grad_two[at] = down_grad
                branch[at] = down_grad.astype(LOW)
                add_norm_sums(feed_sums, 0, branch[at], grad, unit)

            for_rows(total_rows, second_norm)
            load(1, wait=True)
            out_grad[...] = dot_tn(mixed[...], branch[...]).astype(LOW)
            low[...] = dot_nt(branch[...], weights[0]).astype(LOW)

        @pl.when((step >= heads) & (step < recall))
        def _():
            s, g = (step - heads) // groups, (step - heads) % groups
            slot = lax.broadcasted_iota(jnp.int32, (1, slots), 1)
            allowed = slot < lengths[s]
            sums[...] = jnp.zeros_like(sums)
            token_at = pl.ds(pl.multiple_of(s * rows, 16), rows)

            @pl.loop(0, CROSS_LANES // PAIR)
            def _(p):
                where = pl.ds(pl.multiple_of(p * PAIR, PAIR), PAIR)
                lanes = pl.ds(pl.multiple_of(g * CROSS_LANES + p * PAIR, PAIR), PAIR)
                columns = [pick_column(logs[0], 2 * p + which) for which in range(2)]
                found = attend_pair_back(
                    query[:, where], keys[:, where], values[:, where], allowed, columns,
                    low[token_at, lanes],
                )
                grad_query[:, where] = found[0]
                shape = made.shape[1:-1] + (PAIR,)
                made[s, :, :, :, :, lanes] = found[1].reshape(shape)
                made[count + s, :, :, :, :, lanes] = found[2].reshape(shape)
                sums[0, 0:1, where] = column_sum(found[0])
                sums[0, 1:2, where] = column_sum(found[2])

        @pl.when(step >= recall)
        def _():
            t = step - recall
            half = made.shape[1] // 2
            at = pl.ds(t % 2 * half, half)
            lanes = pl.ds(pl.multiple_of(t * tile_lanes, 128), tile_lanes)
            memory_grad[...] = dot_nt(
                made[t // 2, at].reshape(tile_rows, span), weights[0]
            ) + dot_nt(made[count + t // 2, at].reshape(tile_rows, span), weights[1])

            @pl.loop(0, 2)
            def _(number):
                part = made[pl.ds(count * number, count), :, :, :, :, lanes]
                product = dot_tn(memory_low[...], part.reshape(count * slots, tile_lanes))
                weight_grad[number] = product.astype(LOW)

        @pl.when(step == last)
        def _():
            rounds.finish()

    def feed(i):
        return jnp.minimum(i, feeds - 1)

    def head(i):
        return jnp.clip(i - heads, 0, recall - heads - 1)

    def later(i):
        return jnp.maximum(i - recall, 0)

    tile = pl.BlockSpec((total_rows, FEED_TILE), lambda i: (0, feed(i)))

    def feed_spec(number):
        return pl.BlockSpec(
            (1, span, FEED_TILE), lambda i: (2 * (feed(i) // split) + number, 0, feed(i) % split)
        )

    token = pl.BlockSpec((rows, CROSS_LANES), lambda i: (head(i) // groups, head(i) % groups))
    held = pl.BlockSpec((slots, CROSS_LANES), lambda i: (head(i) // groups, head(i) % groups))
    anywhere = pl.BlockSpec(memory_space=pl.ANY)
    return pl.pallas_call(
        kernel,
        grid=(last + 1,),
        in_specs=[
            pl.BlockSpec(memory_space=pltpu.SMEM),
            once_spec(unit_two.shape),
            once_spec(inverse_two.shape),
            once_spec(vectors.shape),
            tile,
            tile,
            feed_spec(0),
            feed_spec(1),
            once_spec(mixed.shape),
            token,
            held,
            held,
            pl.BlockSpec((1, rows, 128), lambda i: (head(i), 0, 0)),
            anywhere,
            anywhere,
            anywhere,
        ]
        + reduction.in_specs(),
        out_specs=[
            pl.BlockSpec((1, FEED_TILE), lambda i: (0, feed(i))),
            once_spec((total_rows, span)),
            once_spec((span, span)),
            once_spec((8, span)),
            token,
            pl.BlockSpec((1, 8, CROSS_LANES), lambda i: (head(i) // groups, 0, head(i) % groups)),
            pl.BlockSpec((tile_rows, span), lambda i: (later(i), 0)),
            pl.BlockSpec((2, span, tile_lanes), lambda i: (0, 0, later(i))),
        ]
        + reduction.out_specs(),
        out_shape=[
            jax.ShapeDtypeStruct((1, feeds * FEED_TILE), jnp.float32),
            jax.ShapeDtypeStruct((total_rows, span), jnp.float32),
            jax.ShapeDtypeStruct((span, span), LOW),
            jax.ShapeDtypeStruct((8, span), jnp.float32),
            jax.ShapeDtypeStruct(query.shape, LOW),
            jax.ShapeDtypeStruct((count, 8, span), jnp.float32),
            jax.ShapeDtypeStruct(memory.shape, jnp.float32),
            jax.ShapeDtypeStruct((2, span, span), LOW),
        ]
        + reduction.outs(),
        scratch_shapes=[
            pltpu.VMEM((total_rows, span), LOW),
            pltpu.VMEM((total_rows, span), LOW),
            pltpu.VMEM((total_rows, span), jnp.float32),
            pltpu.VMEM(memory.shape, LOW),
            pltpu.VMEM((2, span, span), LOW),
            pltpu.SemaphoreType.DMA((5,)),
        ]
        + reduction.scratch(),
        compiler_params=params(collective_id=collective_id, has_side_effects=True),
        name="middle_backward",
    )(
        lengths, unit_two, inverse_two, vectors, hidden, slope, feed_full, feed_full, mixed,
        query, keys, values, logs, grad_three, memory, cross_full, *reduction.operands(),
    )


def self_backward(
    reduction, collective_id, tokens, mask, vectors, self_full, cross_full, saved, cross_query_grad,
    grad_two, cross_sums, feed_sums, out_sums, bias_grad
):
    count, length, span = tokens.shape
    qkv, mixed, logs, unit, inverse = saved
    rows, total_rows = padded(length), mixed.shape[0]
    attend = 2
    project = attend + count
    last = project + 2
    carried, produced = len(reduction.operands()), len(reduction.outs())
    fetched = (cross_query_grad, cross_full, unit, grad_two, mixed, qkv, logs, tokens)
    plan = {
        0: (0, 1, 2, 0),
        1: (2,),
        attend: (0, 1, 4),
        attend + 1: (2, 4, 3),
        project: (0, 3, 2),
        project + 1: (4,),
        last: (6, 1, 5, 0, 2, 6, 4),
    }

    def kernel(*refs):
        mask, vectors, weight, inverse, cross_sums, feed_sums, out_sums, bias_grad = refs[:8]
        sources, refs = refs[8 : 8 + len(fetched)], refs[8 + len(fetched) :]
        operands, refs = refs[:carried], refs[carried:]
        input_grad, results, refs = refs[0], refs[1 : 1 + produced], refs[1 + produced :]
        (low, grads, total, load_sems), refs = refs[:4], refs[4:]
        held, scratch = refs[: len(fetched)], refs[len(fetched) :]
        cross_query_grad, query_weight, unit, grad_two, mixed, qkv, logs, tokens = held

        def load(numbers, wait=False):
            for number in numbers:
                source = sources[number]
                if number == 1:
                    source = source.at[0]
                copy = pltpu.make_async_copy(source, held[number], load_sems.at[number])
                copy.wait() if wait else copy.start()

        step = pl.program_id(0)
        rounds, made, terms, vector_flow = reduction.rounds(operands, results, scratch)
        for start, begins in plan.items():

            @pl.when(step == start)
            def _():
                if start == 0:
                    load(range(len(fetched)))
                    reduction.greet()
                if start == project:
                    rounds.first.append(vector_flow)
                rounds.move(begins, reduction.parts)

        def keep(number, product):
            made[number] = product.astype(LOW).reshape(made.shape[1:])

        @pl.when(step == 0)
        def _():
            terms[...] = jnp.zeros_like(terms)
            load(range(4), wait=True)

            def remake(at):
                grads[1, at] = (unit[at] * vectors[3:4] + vectors[4:5]).astype(LOW)

            for_rows(total_rows, remake)
            keep(0, dot_tn(grads[1], cross_query_grad[...]) * SCALE)
            total[...] = dot_nt(cross_query_grad[...], query_weight[...]) * SCALE

            def first_norm(at):
                grad = grad_two[at] + total[at]
                down_grad = norm_back(grad, unit[at], inverse[at], vectors[3:4])
                total[at] = down_grad
                grads[2, at] = down_grad.astype(LOW)
                add_norm_sums(terms, 2, grads[2, at], grad, unit[at])

            for_rows(total_rows, first_norm)
            spread = jnp.sum(cross_sums[...], axis=0)
            terms[5:6] = spread[0:1] * SCALE
            terms[6:7] = spread[1:2]
            terms[7:10] = out_sums[0:3]
            terms[10:13] = feed_sums[0:3]
            for k in range(bias_grad.shape[1] // span):
                terms[13 + k : 14 + k] = bias_grad[:, k * span : (k + 1) * span]

        @pl.when(step == 1)
        def _():
            load(range(4, len(fetched)), wait=True)
            fill_tokens(low, tokens)
            keep(1, dot_tn(mixed[...], grads[2]))
            grads[0] = dot_nt(grads[2], weight[0]).astype(LOW)

        @pl.when((step >= attend) & (step < project))
        def _():
            s = step - attend
            allowed = causal_allowed(rows, mask[pl.ds(s, 1)])
            table_at = pl.ds(pl.multiple_of(s * rows, 16), rows)

            def pair(lane, head):
                where = (table_at, pl.ds(lane, PAIR))
                table = logs[table_at]
                columns = [pick_column(table, head + which) for which in range(2)]
                found = attend_pair_back(
                    qkv[(0,) + where],
                    qkv[(1,) + where],
                    qkv[(2,) + where],
                    allowed,
                    columns,
                    grads[(0,) + where],
                )
                for number in range(3):
                    grads[(1 + number,) + where] = found[number]

            for_head_groups(span, pair)

        @pl.when(step == project - 1)
        def _():
            terms[0:1] = column_sum(grads[1]) * SCALE
            terms[1:2] = column_sum(grads[3])

        @pl.when(step >= project)
        def _():
            factor = jnp.where(step == project, SCALE, 1.0)
            part = grads[step - project + 1]
            keep(step - project + 2, dot_tn(low[...], part) * factor)
            total[...] += dot_nt(part, weight[0]) * factor

        @pl.when(step == last)
        def _():
            store_tokens(input_grad, total[...])
            rounds.finish()

    small = (mask, vectors, self_full, inverse, cross_sums, feed_sums, out_sums, bias_grad)
    specs = [once_spec(operand.shape) for operand in small]
    specs[2] = pl.BlockSpec(
        (1, span, span), lambda i: (jnp.where(i < project, 3, i - project), 0, 0)
    )
    return pl.pallas_call(
        kernel,
        grid=(last + 1,),
        in_specs=specs
        + [pl.BlockSpec(memory_space=pl.ANY)] * len(fetched)
        + reduction.in_specs(),
        out_specs=[once_spec(tokens.shape)] + reduction.out_specs(),
        out_shape=[jax.ShapeDtypeStruct(tokens.shape, jnp.float32)] + reduction.outs(),
        scratch_shapes=[
            pltpu.VMEM((total_rows, span), LOW),
            pltpu.VMEM((4, total_rows, span), LOW),
            pltpu.VMEM((total_rows, span), jnp.float32),
            pltpu.SemaphoreType.DMA((len(fetched),)),
        ]
        + [
            pltpu.VMEM((span, span) if number == 1 else array.shape, array.dtype)
            for number, array in enumerate(fetched)
        ]
        + reduction.scratch(),
        compiler_params=params(collective_id=collective_id, has_side_effects=True),
        name="self_backward",
    )(*small, *fetched, *reduction.operands())


def per_device(
    wide,
    narrow,
    decoder_input,
    memory,
    decoder_mask,
    memory_length,
    self_weights,
    cross_weights,
    feed_weights,
    vectors,
    hidden_bias,
    cotangent,
):
    seq_count, seq_length, model_width = decoder_input.shape
    mem_span = memory.shape[1]
    memory_low = memory.reshape(seq_count * mem_span, model_width)
    saved, (self_full, cross_full, feed_full, vector_all, unused_bias) = front(
        Gather(
            wide, narrow, [self_weights, cross_weights, feed_weights], [vectors, hidden_bias]
        ),
        decoder_input,
        decoder_mask,
        memory_length,
        memory_low,
        cotangent,
        1,
    )
    qkv, self_mixed, unit_one, cross_query, cross_keys, cross_values, cross_mixed, unit_two = saved[:8]
    self_logs, inverse_one, cross_logs = saved[8:11]
    hidden, slope, layer_output, inverse_two, grad_three, feed_sums = saved[11:]
    parts = feed_full.shape[0] // 2
    (
        bias_part, grad_two, cross_out_grad, out_sums, cross_gq, cross_sums, memory_grad, memory_parts, feed_grad
    ) = middle_backward(
        Reduction(
            wide,
            narrow,
            model_width,
            [],
            1,
            [(0, matrix, part) for part in range(parts) for matrix in range(2)],
            [(2, parts)],
            [2 * (part % 2) + matrix for part in range(parts) for matrix in range(2)],
        ),
        grad_three,
        unit_two,
        inverse_two,
        vector_all,
        hidden,
        slope,
        feed_full,
        cross_full,
        cross_mixed,
        cross_query,
        cross_keys,
        cross_values,
        memory_length,
        cross_logs,
        memory_low,
        2,
    )
    places = [(0, 1), (0, 2), (0, 3), (0, 0), (1, 3), (1, 0), (1, 1), (1, 2)]
    input_grad, cross_grad, self_weight_gradient, vectors_grad, hidden_bias_grad = self_backward(
        Reduction(
            wide,
            narrow,
            model_width,
            [memory_parts, cross_out_grad[None]],
            2,
            [place + (0,) for place in places],
            [(4, 1), (4, 1)],
            range(5),
            [vectors.shape, hidden_bias.shape],
        ),
        3,
        decoder_input,
        decoder_mask,
        vector_all,
        self_full,
        cross_full,
        (qkv, self_mixed, self_logs, unit_one, inverse_one),
        cross_gq,
        grad_two,
        cross_sums,
        feed_sums,
        out_sums,
        bias_part,
    )
    return (
        layer_output,
        input_grad,
        memory_grad.reshape(seq_count, mem_span, model_width),
        self_weight_gradient,
        cross_grad,
        feed_grad,
        vectors_grad,
        hidden_bias_grad,
    )


def solution(mesh):
    placed = (
        P(("wide", "narrow"), None, None),
        P(("wide", "narrow"), None, None),
        P(("wide", "narrow"), None),
        P(("wide", "narrow")),
        P(None, "wide", "narrow"),
        P(None, "wide", "narrow"),
        P(None, "wide", "narrow"),
        P(None, "narrow"),
        P(None, "narrow"),
        P(("wide", "narrow"), None, None),
    )
    return jax.shard_map(
        functools.partial(per_device, mesh.shape["wide"], mesh.shape["narrow"]),
        mesh=mesh,
        in_specs=placed,
        out_specs=(
            P(("wide", "narrow"), None, None),
            P(("wide", "narrow"), None, None),
            P(("wide", "narrow"), None, None),
            P(None, "wide", "narrow"),
            P(None, "wide", "narrow"),
            P(None, "wide", "narrow"),
            P(None, "narrow"),
            P(None, "narrow"),
        ),
        check_vma=False,
    )
```

```python
import functools
import math

import jax
import jax.numpy as jnp
from jax import lax
from jax.experimental import pallas as pl
from jax.experimental.pallas import tpu as pltpu
from jax.sharding import PartitionSpec as P

HEADS = 16
HEAD_DIM = 64


MESH_ID = pl.DeviceIdType.MESH


class Position:
    def __init__(self, wide, narrow):
        self.sizes = {"line": wide // 4, "pair": 2, "core": 2, "column": narrow}

    def get(self, axis):
        if axis == "column":
            return lax.axis_index("narrow")
        index = lax.axis_index("wide")
        if axis == "core":
            return index % 2
        return (index // 2) % 2 if axis == "pair" else index // 4

    def device(self, **moved):
        spot = {name: moved.get(name, self.get(name)) for name in self.sizes}
        return (spot["line"] * 4 + spot["pair"] * 2 + spot["core"], spot["column"])


class Channels:
    def __init__(self, sends, recvs):
        self.sends, self.recvs, self.used = sends, recvs, 0

    def take(self):
        self.used += 1
        number = self.used - 1
        return lambda: (self.sends.at[number], self.recvs.at[number])


def remote(source, target, channel, device):
    return pltpu.make_async_remote_copy(
        src_ref=source,
        dst_ref=target,
        send_sem=channel()[0],
        recv_sem=channel()[1],
        device_id=device,
        device_id_type=MESH_ID,
    )


def flip(index, bit):
    return index + bit - 2 * bit * ((index // bit) % 2)


def peers(position, axis, distance):
    at = (position.get(axis) + distance) % position.sizes[axis]
    return at, position.device(**{axis: at})


def greet(position):
    barrier = pltpu.get_barrier_semaphore()
    expected = 0
    for axis, size in position.sizes.items():
        for distance in range(1, size):
            pl.semaphore_signal(
                barrier,
                inc=1,
                device_id=peers(position, axis, distance)[1],
                device_id_type=MESH_ID,
            )
            expected += 1
    pl.semaphore_wait(barrier, expected)


def advance(generator):
    return next(generator, "done") != "done"


class Rounds:
    def __init__(self, flows, live=()):
        self.waiting, self.live = list(flows), list(live)
        self.all, self.first = None, []

    def run(self, start=0):
        self.live = self.live + self.waiting[:start]
        self.waiting = self.waiting[start:]
        self.live = [flow for flow in self.live if advance(flow)]

    def move(self, groups, size=2):
        if self.all is None:
            self.all = [*self.waiting]
            self.waiting, self.first, self.live = [], self.live, list(self.all)
        for group in groups:
            self.first = [flow for flow in self.first if advance(flow)]
            for flow in self.all[group * size : group * size + size]:
                if not advance(flow):
                    self.live.remove(flow)

    def finish(self, together=2):
        self.live, self.first = self.live + self.first, []
        while self.waiting or self.live:
            self.run(together)


def finish_sends(sent):
    for describe in sent:
        describe().wait_send()


def gather_axis(position, axis, channels, block, own, sent):
    arrivals = []
    for distance in range(1, position.sizes[axis]):
        channel = channels.take()

        def send(distance=distance, channel=channel):
            device = peers(position, axis, distance)[1]
            return remote(own(), block(position.get(axis)), channel, device)

        def arrival(distance=distance, channel=channel):
            came, device = peers(position, axis, -distance)
            return remote(block(came), block(came), channel, device)

        send().start()
        sent.append(send)
        arrivals.append(arrival)
    yield
    for arrival in arrivals:
        arrival().wait_recv()


def gather_flow(position, channels, local_sem, own, region, order):
    sent = []

    def place(done, axis=None, at=None):
        spot = {name: None if name in done else position.get(name) for name in position.sizes}
        if axis is not None:
            spot[axis] = at
        return region(**spot)

    def local():
        return pltpu.make_async_copy(own(), place(()), local_sem())

    local().start()
    for number, axis in enumerate(order):
        done = order[:number]

        def block(j, axis=axis, done=done):
            return place(done, axis, j)

        def source(block=block, axis=axis, first=number == 0):
            return own() if first else block(position.get(axis))

        yield from gather_axis(position, axis, channels, block, source, sent)
        if number == 0:
            local().wait()
    finish_sends(sent)


def whole(index):
    return slice(None) if index is None else index


def row_splits(rows, most):
    return max(1, min(most, rows // 16))


def flow_channels(wide, narrow):
    return 2 + (wide // 4 - 1) + (narrow - 1)


ORDER_A = ("line", "pair", "column", "core")
ORDER_B = ("line", "column", "pair", "core")


def lane_parts(wide, narrow, block):
    return block.shape[2] * narrow // (block.shape[1] * wide)


def gather_flows(position, channels, local_sems, parts, blocks, fulls):
    jobs = []
    for block_ref, full_ref, count in zip(blocks, fulls, parts):
        jobs += [(block_ref, full_ref, count, place, 0, 1) for place in range(full_ref.shape[0])]
    jobs = [job[:4] + (half, 2) for half in range(2) for job in jobs[:2]] + jobs[2:]
    flows = []
    for block_ref, full_ref, count, place, half, halves in jobs:
        width, rows = block_ref.shape[2] // count, block_ref.shape[1] // halves
        part, matrix = divmod(place, block_ref.shape[0])
        at = pl.ds(half * rows, rows)

        def region(line, pair, core, column, full_ref=full_ref, place=place, width=width, at=at):
            lanes = slice(None)
            if column is not None:
                lanes = pl.ds(pl.multiple_of(column * width, 128), width)
            return full_ref.at[place, whole(line), whole(pair), whole(core), at, lanes]

        def own(block_ref=block_ref, matrix=matrix, part=part, width=width, at=at):
            return block_ref.at[matrix, at, part * width : (part + 1) * width]

        number = len(flows)
        order = ORDER_A if number % 2 == 0 else ORDER_B
        flows.append(
            gather_flow(
                position, channels, lambda number=number: local_sems.at[number], own, region, order
            )
        )
    return flows


def column_flow(position, channels, sem, block_ref, full_ref):
    width = block_ref.shape[1]

    def region(column):
        return full_ref.at[:, pl.ds(pl.multiple_of(column * width, 128), width)]

    def local():
        return pltpu.make_async_copy(block_ref, region(position.get("column")), sem())

    sent = []
    local().start()
    yield from gather_axis(position, "column", channels, region, lambda: block_ref, sent)
    local().wait()
    finish_sends(sent)


class Gather:
    def __init__(self, wide, narrow, arrays, vectors=()):
        self.wide, self.narrow = wide, narrow
        self.arrays, self.vectors = list(arrays), list(vectors)
        self.parts = [lane_parts(wide, narrow, array) for array in arrays]
        self.count = 2 + sum(array.shape[0] * part for array, part in zip(arrays, self.parts))

    def operands(self):
        return self.arrays + self.vectors

    def in_specs(self):
        return [pl.BlockSpec(memory_space=pltpu.VMEM)] * len(self.operands())

    def wholes(self):
        return [(vector.shape[0], vector.shape[1] * self.narrow) for vector in self.vectors]

    def outs(self):
        outs = []
        for array, part in zip(self.arrays, self.parts):
            matrices, rows, width = array.shape
            shape = (matrices * part, self.wide // 4, 2, 2, rows, width // part * self.narrow)
            outs.append(jax.ShapeDtypeStruct(shape, array.dtype))
        return outs + [jax.ShapeDtypeStruct(shape, jnp.float32) for shape in self.wholes()]

    def out_specs(self):
        specs = [pl.BlockSpec(memory_space=pl.ANY)] * len(self.arrays)
        return specs + [pl.BlockSpec(memory_space=pltpu.VMEM)] * len(self.vectors)

    def scratch(self):
        flows = self.count + len(self.vectors)
        copies = flow_channels(self.wide, self.narrow) * flows
        return [
            pltpu.SemaphoreType.DMA((copies,)),
            pltpu.SemaphoreType.DMA((copies,)),
            pltpu.SemaphoreType.DMA((flows,)),
        ] + [pltpu.VMEM(shape, jnp.float32) for shape in self.wholes()]

    def rounds(self, operands, outs, scratch):
        position = Position(self.wide, self.narrow)
        channels = Channels(scratch[0], scratch[1])
        count, local_sems, wholes = len(self.arrays), scratch[2], scratch[3:]
        live = [
            column_flow(
                position,
                channels,
                lambda k=k: local_sems.at[self.count + k],
                operands[count + k],
                wholes[k],
            )
            for k in range(len(self.vectors))
        ]
        flows = gather_flows(
            position, channels, local_sems, self.parts, operands[:count], outs[:count]
        )
        return Rounds(flows, live), wholes

    def greet(self):
        greet(Position(self.wide, self.narrow))

    def join(self, results):
        count = len(self.arrays)
        fulls = [full.reshape(full.shape[0], -1, full.shape[-1]) for full in results[:count]]
        return fulls + list(results[count:])


def add_rows(target, parts):
    lead = target.shape[:-2]
    count = math.prod(lead)

    def add(spot):
        total = parts[0][spot].astype(jnp.float32)
        for part in parts[1:]:
            total = total + part[spot].astype(jnp.float32)
        target[spot] = total.astype(target.dtype)

    if count == 1:
        add((0,) * len(lead))
        return

    @pl.loop(0, count)
    def _(k):
        where = []
        for extent in reversed(lead):
            where.insert(0, k % extent)
            k = k // extent
        add(tuple(where))


def reduce_axis(position, axis, channels, local, slots, result, sent):
    size = position.sizes[axis]
    for distance in range(1, size):
        channel = channels.take()

        def send(distance=distance, channel=channel):
            at, device = peers(position, axis, distance)
            return remote(local(at), slots.at[distance - 1], channel, device)

        send().start()
        sent.append(send)
    yield
    for send in sent[1 - size :]:
        send().wait_recv()
    add_rows(
        result(), [local(position.get(axis))] + [slots.at[k] for k in range(size - 1)]
    )


def reduce_flow(position, channels, local_sem, loc, grads, result, buffers, order):
    first, mid, last, line_slots = buffers
    sent = []

    def own():
        return pltpu.make_async_copy(grads(position.get("core")), loc(), local_sem())

    def mine():
        return grads(position.get("core")) if loc is None else loc()

    channel = channels.take()

    def swap():
        core = position.get("core")
        return remote(grads(1 - core), first, channel, position.device(core=1 - core))

    if loc is not None:
        own().start()
    swap().start()
    yield
    if loc is not None:
        own().wait()
    swap().wait_recv()
    add_rows(first, [first, mine()])
    swap().wait_send()
    width = result().shape[-1]

    def columns(j):
        return pl.ds(pl.multiple_of(j * width, 128), width)

    def held():
        return mid.at[0]

    def final():
        return last.at[0]

    if order == "A":
        yield from reduce_axis(
            position, "column", channels, lambda j: first.at[:, :, :, columns(j)], mid, held, sent
        )
        yield from reduce_axis(position, "pair", channels, lambda j: held().at[:, j], last, final, sent)
    else:
        yield from reduce_axis(position, "pair", channels, lambda j: first.at[:, j], mid, held, sent)
        yield from reduce_axis(
            position, "column", channels, lambda j: held().at[:, :, columns(j)], last, final, sent
        )
    yield from reduce_axis(
        position, "line", channels, lambda j: final().at[pl.ds(j, 1)], line_slots, result, sent
    )
    finish_sends(sent)


def double_flow(position, channels, terms, total, inbox, vectors_out, bias_out):
    total[0] = terms[...]
    step = 0
    for axis in ("core", "pair", "line", "column"):
        bit = 1
        while bit < position.sizes[axis]:
            channel = channels.take()

            def describe():
                to = position.device(**{axis: flip(position.get(axis), bit)})
                return remote(total.at[step], inbox.at[step], channel, to)

            describe().start()
            yield
            describe().wait_recv()
            total[step + 1] = total[step] + inbox[step]
            describe().wait_send()
            bit *= 2
            step += 1
    count, width = vectors_out.shape
    lanes = pl.ds(pl.multiple_of(position.get("column") * width, 128), width)
    vectors_out[...] = total[step, 0:count, lanes]
    for k in range(bias_out.shape[1] // width):
        bias_out[:, k * width : (k + 1) * width] = total[step, count + k : count + k + 1, lanes]


class Reduction:
    RING = 6

    def __init__(self, wide, narrow, depth, arrays, parts, places, matrices, held=(), shapes=()):
        self.wide, self.narrow, self.held, self.shapes = wide, narrow, held, list(shapes)
        depth = span = depth
        self.rows = rows = depth // wide
        self.parts = row_splits(rows, parts)
        self.piece = rows // self.parts
        self.line, self.span, self.width = wide // 4, span, span // narrow
        self.matrices = matrices
        sources = [(s, m) for s, array in enumerate(arrays) for m in range(array.shape[0])]
        sources += [(None, m) for m in held]
        self.pieces = [
            source + (part,) + place
            for source, place in zip(sources, places)
            for part in range(self.parts)
        ]
        self.views = [array.reshape(array.shape[0], self.line, 2, 2, rows, span) for array in arrays]

    def order(self, number):
        return "A" if number % 2 == 0 else "B"

    def operands(self):
        return self.views

    def in_specs(self):
        return [pl.BlockSpec(memory_space=pl.ANY)] * len(self.views)

    def outs(self):
        outs = [
            jax.ShapeDtypeStruct((count, self.rows, self.width * parts), jnp.float32)
            for count, parts in self.matrices
        ]
        return outs + [jax.ShapeDtypeStruct(shape, jnp.float32) for shape in self.shapes]

    def out_specs(self):
        return [pl.BlockSpec(memory_space=pltpu.VMEM)] * len(self.outs())

    def steps(self):
        return (self.wide * self.narrow).bit_length() - 1

    def terms_shape(self):
        count = self.shapes[0][0] + self.shapes[1][1] * self.narrow // self.span
        return (count + -count % 8, self.span)

    def scratch(self):
        low, line, piece = jnp.bfloat16, self.line, self.piece
        copies = flow_channels(self.wide, self.narrow) * len(self.pieces) + 16
        shapes = [
            pltpu.SemaphoreType.DMA((copies,)),
            pltpu.SemaphoreType.DMA((copies,)),
            pltpu.SemaphoreType.DMA((len(self.pieces),)),
            pltpu.VMEM((self.RING, line, 2, piece, self.span), low)
            if self.views
            else pltpu.VMEM((8, 128), low),
        ]
        if self.held:
            shapes.append(pltpu.VMEM((1 + max(self.held), line, 2, 2, self.rows, self.span), low))
        if self.shapes:
            shapes.append(pltpu.VMEM(self.terms_shape(), jnp.float32))
            shapes.append(pltpu.VMEM((self.steps() + 1,) + self.terms_shape(), jnp.float32))
            shapes.append(pltpu.VMEM((self.steps(),) + self.terms_shape(), jnp.float32))
        for number in range(len(self.pieces)):
            shapes.append(pltpu.VMEM((line, 2, piece, self.span), low))
            if self.order(number) == "A":
                shapes.append(pltpu.VMEM((self.narrow - 1, line, 2, piece, self.width), low))
                shapes.append(pltpu.VMEM((1, line, piece, self.width), low))
            else:
                shapes.append(pltpu.VMEM((1, line, piece, self.span), low))
                shapes.append(pltpu.VMEM((self.narrow - 1, line, piece, self.width), low))
            shapes.append(pltpu.VMEM((line - 1, 1, piece, self.width), low))
        return shapes

    def rounds(self, operands, outs, scratch):
        position = Position(self.wide, self.narrow)
        channels = Channels(scratch[0], scratch[1])
        local_sems, ring, buffers = scratch[2], scratch[3], list(scratch[4:])
        made = buffers.pop(0) if self.held else None
        terms, vector_flow = None, None
        if self.shapes:
            terms, total, inbox = buffers[:3]
            buffers = buffers[3:]
            vector_flow = double_flow(position, channels, terms, total, inbox, *outs[-2:])
        flows = []
        for number, (source, inner, part, out, matrix, slot) in enumerate(self.pieces):
            at = pl.ds(part * self.piece, self.piece)
            lanes = pl.ds(slot * self.width, self.width)

            def grads(core, source=source, inner=inner, at=at):
                array = made if source is None else operands[source]
                return array.at[inner, :, :, core, at]

            flows.append(
                reduce_flow(
                    position,
                    channels,
                    lambda number=number: local_sems.at[number],
                    None if source is None else lambda number=number: ring.at[number % self.RING],
                    grads,
                    lambda out=out, at=(pl.ds(matrix, 1), at, lanes): outs[out].at[at],
                    buffers[4 * number : 4 * number + 4],
                    self.order(number),
                )
            )
        return Rounds(flows), made, terms, vector_flow

    def greet(self):
        greet(Position(self.wide, self.narrow))


LOW = jnp.bfloat16
NEGATIVE = -1000000000.0
EPSILON = 1e-05
PAIR = 2 * HEAD_DIM
SCALE = HEAD_DIM ** (-0.5)
BUDGET = 65000 * 1024


def dot_nn(left, right):
    return jnp.dot(left, right, preferred_element_type=jnp.float32)


def dot_nt(left, right):
    return lax.dot_general(
        left, right, (((1,), (1,)), ((), ())), preferred_element_type=jnp.float32
    )


def dot_tn(left, right):
    return lax.dot_general(
        left, right, (((0,), (0,)), ((), ())), preferred_element_type=jnp.float32
    )


def padded(length):
    return -(-length // 16) * 16


def column_sum(rows):
    return jnp.sum(rows.astype(jnp.float32), axis=0, keepdims=True)


def standardise(hidden):
    centre = hidden - jnp.mean(hidden, axis=-1, keepdims=True)
    spread = jnp.mean(centre * centre, axis=-1, keepdims=True)
    inverse = lax.rsqrt(spread + EPSILON)
    return centre * inverse, inverse


def norm_back(grad, unit, inverse, gain):
    scaled = grad * gain
    first = jnp.mean(scaled, axis=-1, keepdims=True)
    second = jnp.mean(scaled * unit, axis=-1, keepdims=True)
    return inverse * (scaled - first - unit * second)


def for_rows(total, function, most=48):
    chunk = next(size for size in range(most, 0, -16) if total % size == 0)

    @pl.loop(0, total // chunk)
    def _(k):
        function(pl.ds(pl.multiple_of(k * chunk, 16), chunk))


def add_norm_sums(sums, first, low, grad, unit):
    sums[first : first + 1] += column_sum(low)
    sums[first + 1 : first + 2] += column_sum(grad * unit)
    sums[first + 2 : first + 3] += column_sum(grad)


def fill_tokens(target, source):
    count, length, span = source.shape
    rows = padded(length)
    for s in range(count):
        if rows > length:
            base = s * rows + length // 16 * 16
            target[base : (s + 1) * rows] = jnp.zeros(((s + 1) * rows - base, span), target.dtype)
        target[s * rows : s * rows + length] = source[s].astype(target.dtype)


def store_tokens(target, values):
    count, length, span = target.shape
    rows = padded(length)
    for s in range(count):
        target[s] = values[s * rows : s * rows + length].astype(target.dtype)


def head_lanes(rows, which):
    lane = lax.broadcasted_iota(jnp.int32, rows.shape, 1)
    return (lane >= HEAD_DIM) == (which == 1)


def one_head(rows, which):
    return jnp.where(head_lanes(rows, which), rows, jnp.zeros_like(rows))


def pick_column(table, number):
    lane = lax.broadcasted_iota(jnp.int32, table.shape, 1)
    return jnp.sum(jnp.where(lane == number, table, 0.0), axis=1, keepdims=True)


def attend_pair(query, keys, values, allowed):
    mixed, logs = [], []
    for which in range(2):
        scores = dot_nt(one_head(query, which), keys)
        scores = jnp.where(allowed, scores, NEGATIVE)
        peak = jnp.max(scores, axis=-1, keepdims=True)
        expo = jnp.exp(scores - peak)
        total = jnp.sum(expo, axis=-1, keepdims=True)
        weights = (expo * (1.0 / total)).astype(LOW)
        mixed.append(dot_nn(weights, values))
        logs.append(peak + jnp.log(total))
    both = jnp.where(head_lanes(mixed[0], 0), mixed[0], mixed[1])
    return both.astype(LOW), logs


def attend_pair_back(query, keys, values, allowed, logs, grad):
    grad_query, grad_keys, grad_values = [], None, None
    for which in range(2):
        query_one, grad_one = one_head(query, which), one_head(grad, which)
        scores = jnp.where(allowed, dot_nt(query_one, keys), NEGATIVE)
        probs = jnp.exp(scores - logs[which])
        grad_probs = dot_nt(grad_one, values)
        slope = jnp.sum(grad_probs * probs, axis=-1, keepdims=True)
        grad_scores = (probs * (grad_probs - slope)).astype(LOW)
        grad_query.append(dot_nn(grad_scores, keys))
        part_keys = dot_tn(grad_scores, query_one)
        part_values = dot_tn(probs.astype(LOW), grad_one)
        grad_keys = part_keys if which == 0 else grad_keys + part_keys
        grad_values = part_values if which == 0 else grad_values + part_values
    both = jnp.where(head_lanes(grad_query[0], 0), grad_query[0], grad_query[1])
    return both.astype(LOW), grad_keys.astype(LOW), grad_values.astype(LOW)


def causal_allowed(rows, mask_row):
    valid = jnp.sum(mask_row, axis=-1, keepdims=True)
    query_at = lax.broadcasted_iota(jnp.int32, (rows, rows), 0)
    key_at = lax.broadcasted_iota(jnp.int32, (rows, rows), 1)
    return (query_at >= key_at) & (key_at < valid)


GROUP_PAIRS = 2


def for_head_groups(span, function):
    lanes = min(span, GROUP_PAIRS * PAIR)

    @pl.loop(0, span // lanes)
    def _(g):
        for p in range(lanes // PAIR):
            function(pl.multiple_of(g * lanes + p * PAIR, PAIR), 2 * (g * (lanes // PAIR) + p))


def whole_spec(shape):
    return pl.BlockSpec(shape, lambda *at: (0,) * len(shape))


def params(**more):
    return pltpu.CompilerParams(vmem_limit_bytes=BUDGET, **more)


CROSS_LANES = 2 * PAIR


def once_spec(shape):
    return pl.BlockSpec(shape, lambda *at: (0,) * len(shape), pipeline_mode=pl.Buffered(1))


def front(load, tokens, mask, lengths, memory, cotangent, collective_id):
    count, length, span = tokens.shape
    rows = padded(length)
    total, slots = count * rows, memory.shape[0] // count
    tiles = 4
    tile = memory.shape[0] // tiles
    groups = span // CROSS_LANES
    attend, join, ask = 3, 3 + count, 4 + count
    recall = ask + 1
    look = recall + tiles
    add = look + count * groups
    feed = add + 1
    parts = load.parts[2]
    last = feed + parts - 1
    carried = len(load.operands())
    plan = {
        0: (0, 1, 0, 2, 1, 0, 1, 2, 3, 0, 1, 2, 3, 4, 0, 1),
        2: (2, 3, 4, 5, 2),
        ask: (3, 4, 5, 6, 3),
        recall: (4, 5, 6, 7, 4),
        look: (5, 6, 7, 8),
        look + 5: (5, 6, 7, 8),
        feed + 1: (6, 7, 8),
        feed + 2: (7,),
        feed + 3: (8, 8),
    }

    def kernel(*refs):
        tokens, mask, lengths, memory, cotangent = refs[:5]
        operands, refs = refs[5 : 5 + carried], refs[5 + carried :]
        stored, (logs, inverse, cross_logs) = refs[: len(kept)], refs[len(kept) : len(kept) + 3]
        hidden, slope, output, inverse_two, grad_three, sums = refs[len(kept) + 3 : len(kept) + 9]
        refs = refs[len(kept) + 9 :]
        results, refs = refs[:carried], refs[carried:]
        low, spare, running, weights, weight_sem, store_sems = refs[:6]
        held, scratch = refs[6 : 6 + len(kept)], refs[6 + len(kept) :]
        qkv, mixed, unit, query, keys, values, cross_mixed, unit_two = held
        step = pl.program_id(0)
        rounds, (vectors, bias) = load.rounds(operands, results, scratch)
        for start, begins in plan.items():

            @pl.when(step == start)
            def _():
                if start == 0:
                    load.greet()
                rounds.move(begins)

        def store(*numbers, wait=False):
            for number in numbers:
                copy = pltpu.make_async_copy(
                    held[number], stored[number], store_sems.at[number]
                )
                copy.wait() if wait else copy.start()

        @pl.when(step == recall)
        def _():
            store(0, 1, 2, 3)

        @pl.when(step == look)
        def _():
            store(4, 5)

        @pl.when(step == feed)
        def _():
            store(6, 7)

        def fetch(array, matrix, slot):
            copy = pltpu.make_async_copy(results[array].at[matrix], weights.at[slot], weight_sem)
            copy.start()
            copy.wait()

        def weight(slot):
            return weights[slot].reshape(span, span)

        @pl.when(step == 0)
        def _():
            fill_tokens(low, tokens)

        @pl.when(step < attend)
        def _():
            fetch(0, step, 0)
            product = dot_nn(low[...], weight(0))
            none = jnp.zeros_like(vectors[0:1])
            shift = jnp.where(step == 0, vectors[0:1], jnp.where(step == 2, vectors[1:2], none))
            product = (product + shift) * jnp.where(step == 0, SCALE, 1.0)
            qkv[step] = product.astype(LOW)

        @pl.when((step >= attend) & (step < join))
        def _():
            s = step - attend
            allowed = causal_allowed(rows, mask[pl.ds(s, 1)])
            table_at = pl.ds(pl.multiple_of(s * rows, 16), rows)
            logs[table_at] = jnp.zeros((rows, 128), jnp.float32)

            def pair(lane, head):
                where = (table_at, pl.ds(lane, PAIR))
                both, sums = attend_pair(
                    qkv[(0,) + where], qkv[(1,) + where], qkv[(2,) + where], allowed
                )
                mixed[where] = both
                table = logs[table_at]
                spot = lax.broadcasted_iota(jnp.int32, table.shape, 1)
                for which in range(2):
                    table = jnp.where(spot == head + which, sums[which], table)
                logs[table_at] = table

            for_head_groups(span, pair)

        @pl.when(step == join)
        def _():
            fetch(0, 3, 0)
            running[...] = dot_nn(mixed[...], weight(0))

            def first_norm(at):
                summed = low[at].astype(jnp.float32) + (running[at] + vectors[2:3])
                found, inverse[at] = standardise(summed)
                unit[at] = found
                spare[at] = (found * vectors[3:4] + vectors[4:5]).astype(LOW)

            for_rows(total, first_norm, 160)

        @pl.when(step == ask)
        def _():
            fetch(1, 0, 0)
            product = dot_nn(spare[...], weight(0))
            query[...] = ((product + vectors[5:6]) * SCALE).astype(LOW)

        @pl.when(step == recall)
        def _():
            fetch(1, 1, 0)
            fetch(1, 2, 1)

        @pl.when((step >= recall) & (step < look))
        def _():
            at = pl.ds(pl.multiple_of((step - recall) * tile, 16), tile)
            keys[at] = dot_nn(memory[...], weight(0)).astype(LOW)
            values[at] = (dot_nn(memory[...], weight(1)) + vectors[6:7]).astype(LOW)

        @pl.when((step >= look) & (step < add))
        def _():
            s, g = (step - look) // groups, (step - look) % groups
            slot = lax.broadcasted_iota(jnp.int32, (1, slots), 1)
            allowed = slot < lengths[s]
            token_at = pl.ds(pl.multiple_of(s * rows, 16), rows)
            slot_at = pl.ds(pl.multiple_of(s * slots, 16), slots)
            cross_logs[...] = jnp.zeros_like(cross_logs)

            @pl.loop(0, CROSS_LANES // PAIR)
            def _(p):
                lanes = pl.ds(pl.multiple_of(g * CROSS_LANES + p * PAIR, PAIR), PAIR)
                both, sums = attend_pair(
                    query[token_at, lanes], keys[slot_at, lanes], values[slot_at, lanes], allowed
                )
                cross_mixed[token_at, lanes] = both
                table = cross_logs[0]
                spot = lax.broadcasted_iota(jnp.int32, table.shape, 1)
                for which in range(2):
                    table = jnp.where(spot == 2 * p + which, sums[which], table)
                cross_logs[0] = table

        @pl.when(step == add)
        def _():
            fetch(1, 3, 0)
            running[...] = dot_nn(cross_mixed[...], weight(0))

            def second_norm(at):
                first = unit[at] * vectors[3:4] + vectors[4:5]
                found, inverse_two[at] = standardise(first + (running[at] + vectors[7:8]))
                unit_two[at] = found
                low[at] = (found * vectors[8:9] + vectors[9:10]).astype(LOW)
                running[at] = jnp.zeros_like(found)

            for_rows(total, second_norm, 160)
            fill_tokens(spare, cotangent)

        @pl.when(step >= feed)
        def _():
            part = step - feed
            fetch(2, 2 * part, 0)
            fetch(2, 2 * part + 1, 1)
            width = bias.shape[1] // parts // load.narrow
            shift = jnp.concatenate(
                [
                    bias[:, pl.ds(pl.multiple_of((n * parts + part) * width, 128), width)]
                    for n in range(load.narrow)
                ],
                axis=1,
            )
            half_lanes = span // 2
            row = lax.broadcasted_iota(jnp.int32, (8, span), 0)
            sums[...] = jnp.where(row == 0, shift, 0.0)

            @pl.loop(0, 2)
            def _(k):
                lanes = pl.ds(pl.multiple_of(k * half_lanes, 128), half_lanes)
                up = weights[0, :, :, :, :, lanes].reshape(span, half_lanes)
                down = weights[1, :, :, :, :, lanes].reshape(span, half_lanes)
                inner = dot_nn(low[...], up) + sums[0:1, lanes]
                half = 0.5 + 0.5 * lax.erf(inner * (0.5**0.5))
                bell = jnp.exp(-0.5 * inner * inner) * ((0.5 / math.pi) ** 0.5)
                active = (inner * half).astype(LOW)
                hidden[:, lanes] = active
                slope[:, lanes] = (half + inner * bell).astype(LOW)
                running[...] += dot_nt(active, down)

        @pl.when(step == last)
        def _():
            rounds.finish()
            results[-2][...], results[-1][...] = vectors[...], bias[...]
            sums[...] = jnp.zeros_like(sums)

            def third_norm(at):
                second = unit_two[at] * vectors[8:9] + vectors[9:10]
                found, inverse_three = standardise(second + (running[at] + vectors[10:11]))
                low[at] = (found * vectors[11:12] + vectors[12:13]).astype(LOW)
                grad = spare[at].astype(jnp.float32)
                down_grad = norm_back(grad, found, inverse_three, vectors[11:12])
                grad_three[at] = down_grad
                add_norm_sums(sums, 0, down_grad.astype(LOW), grad, found)

            for_rows(total, third_norm, 160)
            store_tokens(output, low)
            store(*range(len(kept)), wait=True)

    def token(dtype, lanes=span):
        return jax.ShapeDtypeStruct((total, lanes), dtype)

    kept = [
        jax.ShapeDtypeStruct((3, total, span), LOW),
        token(LOW),
        token(jnp.float32),
        token(LOW),
        jax.ShapeDtypeStruct(memory.shape, LOW),
        jax.ShapeDtypeStruct(memory.shape, LOW),
        token(LOW),
        token(jnp.float32),
    ]
    outs = kept + [
        token(jnp.float32, 128),
        token(jnp.float32, 1),
        jax.ShapeDtypeStruct((count * groups, rows, 128), jnp.float32),
        token(LOW, parts * span),
        token(LOW, parts * span),
        jax.ShapeDtypeStruct(cotangent.shape, LOW),
        token(jnp.float32, 1),
        token(jnp.float32),
        jax.ShapeDtypeStruct((8, span), jnp.float32),
    ]
    wide_tile = pl.BlockSpec((total, span), lambda i: (0, jnp.clip(i - feed, 0, parts - 1)))

    results = pl.pallas_call(
        kernel,
        grid=(last + 1,),
        in_specs=[
            once_spec(tokens.shape),
            once_spec(mask.shape),
            pl.BlockSpec(memory_space=pltpu.SMEM),
            pl.BlockSpec((tile, span), lambda i: (jnp.clip(i - recall, 0, tiles - 1), 0)),
            once_spec(cotangent.shape),
        ]
        + load.in_specs(),
        out_specs=[pl.BlockSpec(memory_space=pl.ANY)] * len(kept)
        + [
            once_spec((total, 128)),
            once_spec((total, 1)),
            pl.BlockSpec((1, rows, 128), lambda i: (jnp.clip(i - look, 0, count * groups - 1), 0, 0)),
            wide_tile,
            wide_tile,
        ]
        + [once_spec(out.shape) for out in outs[len(kept) + 5 :]]
        + load.out_specs(),
        out_shape=outs + load.outs(),
        scratch_shapes=[
            pltpu.VMEM((total, span), LOW),
            pltpu.VMEM((total, span), LOW),
            pltpu.VMEM((total, span), jnp.float32),
            pltpu.VMEM((2,) + load.outs()[0].shape[1:], LOW),
            pltpu.SemaphoreType.DMA,
            pltpu.SemaphoreType.DMA((len(kept),)),
        ]
        + [pltpu.VMEM(keep.shape, keep.dtype) for keep in kept]
        + load.scratch(),
        compiler_params=params(collective_id=collective_id, has_side_effects=True),
        name="front",
    )(tokens, mask, lengths, memory, cotangent, *load.operands())
    return results[: len(outs)], load.join(results[len(outs) :])


FEED_TILE = 512


def middle_backward(
    reduction, grad_three, unit_two, inverse_two, vectors, hidden, slope, feed_full, cross_full, mixed,
    query, keys, values, lengths, logs, memory, collective_id
):
    count = lengths.shape[0]
    total_rows, span = query.shape
    rows, slots = total_rows // count, keys.shape[0] // count
    groups = span // CROSS_LANES
    split = span // FEED_TILE
    feeds = feed_full.shape[0] // 2 * split
    heads, recall = feeds, feeds + count * groups
    tiles = 2 * count
    tile_rows, tile_lanes = keys.shape[0] // tiles, span // tiles
    last = recall + tiles - 1
    carried, produced = len(reduction.operands()), len(reduction.outs())
    plan = {
        2: (0,),
        3: (0,),
        4: (1,),
        6: (1,),
        7: (2,),
        heads: (3, 0, 1, 2, 3),
        heads + 1: (0,),
        heads + 2: (1,),
        heads + 6: (2,),
        heads + 7: (0,),
        recall: (2, 3),
        recall + 1: (3,),
        last: (1, 2, 3),
    }

    def kernel(*refs):
        lengths, unit_two, inverse_two, vectors, hidden, slope, up, down, mixed = refs[:9]
        query, keys, values, logs, grad_three, memory, cross_full = refs[9:16]
        operands, refs = refs[16 : 16 + carried], refs[16 + carried :]
        bias_grad, grad_two, out_grad, feed_sums, grad_query, sums = refs[:6]
        memory_grad, weight_grad = refs[6:8]
        results, refs = refs[8 : 8 + produced], refs[8 + produced :]
        low, branch, total, memory_low, weights, load_sems, scratch = *refs[:6], refs[6:]
        step = pl.program_id(0)
        rounds, made, *unused = reduction.rounds(operands, results, scratch)

        def load(number, wait=False):
            source, target = (
                (grad_three, total),
                (cross_full.at[3], weights.at[0]),
                (memory, memory_low),
                (cross_full.at[1], weights.at[0]),
                (cross_full.at[2], weights.at[1]),
            )[number]
            copy = pltpu.make_async_copy(source, target, load_sems.at[number])
            copy.wait() if wait else copy.start()

        @pl.when(step == 0)
        def _():
            load(0)
            load(1)
            reduction.greet()

            def begin(at):
                low[at] = (unit_two[at] * vectors[8:9] + vectors[9:10]).astype(LOW)
                branch[at] = total[at].astype(LOW)

            load(0, wait=True)
            for_rows(total_rows, begin)

        @pl.when(step == heads)
        def _():
            for number in (2, 3, 4):
                load(number)

        for start, begins in plan.items():

            @pl.when(step == start)
            def _():
                rounds.move(begins)

        @pl.when(step == recall)
        def _():
            for number in (2, 3, 4):
                load(number, wait=True)

        @pl.when(step < feeds)
        def _():
            lanes = pl.ds(pl.multiple_of(step % split * FEED_TILE, 128), FEED_TILE)
            place = 2 * (step // split % 2)
            inner = dot_nn(branch[...], down[0])
            grad_inner = (slope[...].astype(jnp.float32) * inner).astype(LOW)
            shape = made.shape[1:-1] + (FEED_TILE,)
            made[place, :, :, :, :, lanes] = dot_tn(low[...], grad_inner).astype(LOW).reshape(shape)
            made[place + 1, :, :, :, :, lanes] = (
                dot_tn(branch[...], hidden[...]).astype(LOW).reshape(shape)
            )
            bias_grad[...] = column_sum(grad_inner)
            total[...] += dot_nt(grad_inner, up[0])

        @pl.when(step == feeds - 1)
        def _():
            feed_sums[...] = jnp.zeros_like(feed_sums)

            def second_norm(at):
                grad, unit = total[at], unit_two[at]
                down_grad = norm_back(grad, unit, inverse_two[at], vectors[8:9])
                grad_two[at] = down_grad
                branch[at] = down_grad.astype(LOW)
                add_norm_sums(feed_sums, 0, branch[at], grad, unit)

            for_rows(total_rows, second_norm)
            load(1, wait=True)
            out_grad[...] = dot_tn(mixed[...], branch[...]).astype(LOW)
            low[...] = dot_nt(branch[...], weights[0]).astype(LOW)

        @pl.when((step >= heads) & (step < recall))
        def _():
            s, g = (step - heads) // groups, (step - heads) % groups
            slot = lax.broadcasted_iota(jnp.int32, (1, slots), 1)
            allowed = slot < lengths[s]
            sums[...] = jnp.zeros_like(sums)
            token_at = pl.ds(pl.multiple_of(s * rows, 16), rows)

            @pl.loop(0, CROSS_LANES // PAIR)
            def _(p):
                where = pl.ds(pl.multiple_of(p * PAIR, PAIR), PAIR)
                lanes = pl.ds(pl.multiple_of(g * CROSS_LANES + p * PAIR, PAIR), PAIR)
                columns = [pick_column(logs[0], 2 * p + which) for which in range(2)]
                found = attend_pair_back(
                    query[:, where], keys[:, where], values[:, where], allowed, columns,
                    low[token_at, lanes],
                )
                grad_query[:, where] = found[0]
                shape = made.shape[1:-1] + (PAIR,)
                made[s, :, :, :, :, lanes] = found[1].reshape(shape)
                made[count + s, :, :, :, :, lanes] = found[2].reshape(shape)
                sums[0, 0:1, where] = column_sum(found[0])
                sums[0, 1:2, where] = column_sum(found[2])

        @pl.when(step >= recall)
        def _():
            t = step - recall
            half = made.shape[1] // 2
            at = pl.ds(t % 2 * half, half)
            lanes = pl.ds(pl.multiple_of(t * tile_lanes, 128), tile_lanes)
            memory_grad[...] = dot_nt(
                made[t // 2, at].reshape(tile_rows, span), weights[0]
            ) + dot_nt(made[count + t // 2, at].reshape(tile_rows, span), weights[1])

            @pl.loop(0, 2)
            def _(number):
                part = made[pl.ds(count * number, count), :, :, :, :, lanes]
                product = dot_tn(memory_low[...], part.reshape(count * slots, tile_lanes))
                weight_grad[number] = product.astype(LOW)

        @pl.when(step == last)
        def _():
            rounds.finish()

    def feed(i):
        return jnp.minimum(i, feeds - 1)

    def head(i):
        return jnp.clip(i - heads, 0, recall - heads - 1)

    def later(i):
        return jnp.maximum(i - recall, 0)

    tile = pl.BlockSpec((total_rows, FEED_TILE), lambda i: (0, feed(i)))

    def feed_spec(number):
        return pl.BlockSpec(
            (1, span, FEED_TILE), lambda i: (2 * (feed(i) // split) + number, 0, feed(i) % split)
        )

    token = pl.BlockSpec((rows, CROSS_LANES), lambda i: (head(i) // groups, head(i) % groups))
    held = pl.BlockSpec((slots, CROSS_LANES), lambda i: (head(i) // groups, head(i) % groups))
    anywhere = pl.BlockSpec(memory_space=pl.ANY)
    return pl.pallas_call(
        kernel,
        grid=(last + 1,),
        in_specs=[
            pl.BlockSpec(memory_space=pltpu.SMEM),
            once_spec(unit_two.shape),
            once_spec(inverse_two.shape),
            once_spec(vectors.shape),
            tile,
            tile,
            feed_spec(0),
            feed_spec(1),
            once_spec(mixed.shape),
            token,
            held,
            held,
            pl.BlockSpec((1, rows, 128), lambda i: (head(i), 0, 0)),
            anywhere,
            anywhere,
            anywhere,
        ]
        + reduction.in_specs(),
        out_specs=[
            pl.BlockSpec((1, FEED_TILE), lambda i: (0, feed(i))),
            once_spec((total_rows, span)),
            once_spec((span, span)),
            once_spec((8, span)),
            token,
            pl.BlockSpec((1, 8, CROSS_LANES), lambda i: (head(i) // groups, 0, head(i) % groups)),
            pl.BlockSpec((tile_rows, span), lambda i: (later(i), 0)),
            pl.BlockSpec((2, span, tile_lanes), lambda i: (0, 0, later(i))),
        ]
        + reduction.out_specs(),
        out_shape=[
            jax.ShapeDtypeStruct((1, feeds * FEED_TILE), jnp.float32),
            jax.ShapeDtypeStruct((total_rows, span), jnp.float32),
            jax.ShapeDtypeStruct((span, span), LOW),
            jax.ShapeDtypeStruct((8, span), jnp.float32),
            jax.ShapeDtypeStruct(query.shape, LOW),
            jax.ShapeDtypeStruct((count, 8, span), jnp.float32),
            jax.ShapeDtypeStruct(memory.shape, jnp.float32),
            jax.ShapeDtypeStruct((2, span, span), LOW),
        ]
        + reduction.outs(),
        scratch_shapes=[
            pltpu.VMEM((total_rows, span), LOW),
            pltpu.VMEM((total_rows, span), LOW),
            pltpu.VMEM((total_rows, span), jnp.float32),
            pltpu.VMEM(memory.shape, LOW),
            pltpu.VMEM((2, span, span), LOW),
            pltpu.SemaphoreType.DMA((5,)),
        ]
        + reduction.scratch(),
        compiler_params=params(collective_id=collective_id, has_side_effects=True),
        name="middle_backward",
    )(
        lengths, unit_two, inverse_two, vectors, hidden, slope, feed_full, feed_full, mixed,
        query, keys, values, logs, grad_three, memory, cross_full, *reduction.operands(),
    )


def self_backward(
    reduction, collective_id, tokens, mask, vectors, self_full, cross_full, saved, cross_query_grad,
    grad_two, cross_sums, feed_sums, out_sums, bias_grad
):
    count, length, span = tokens.shape
    qkv, mixed, logs, unit, inverse = saved
    rows, total_rows = padded(length), mixed.shape[0]
    attend = 2
    project = attend + count
    last = project + 2
    carried, produced = len(reduction.operands()), len(reduction.outs())
    fetched = (cross_query_grad, cross_full, unit, grad_two, mixed, qkv, logs, tokens)
    plan = {
        0: (0, 1, 2, 0),
        1: (2,),
        attend: (0, 1, 4),
        attend + 1: (2, 4, 3),
        project: (0, 3, 2),
        project + 1: (4,),
        last: (6, 1, 5, 0, 2, 6, 4),
    }

    def kernel(*refs):
        mask, vectors, weight, inverse, cross_sums, feed_sums, out_sums, bias_grad = refs[:8]
        sources, refs = refs[8 : 8 + len(fetched)], refs[8 + len(fetched) :]
        operands, refs = refs[:carried], refs[carried:]
        input_grad, results, refs = refs[0], refs[1 : 1 + produced], refs[1 + produced :]
        (low, grads, total, load_sems), refs = refs[:4], refs[4:]
        held, scratch = refs[: len(fetched)], refs[len(fetched) :]
        cross_query_grad, query_weight, unit, grad_two, mixed, qkv, logs, tokens = held

        def load(numbers, wait=False):
            for number in numbers:
                source = sources[number]
                if number == 1:
                    source = source.at[0]
                copy = pltpu.make_async_copy(source, held[number], load_sems.at[number])
                copy.wait() if wait else copy.start()

        step = pl.program_id(0)
        rounds, made, terms, vector_flow = reduction.rounds(operands, results, scratch)
        for start, begins in plan.items():

            @pl.when(step == start)
            def _():
                if start == 0:
                    load(range(len(fetched)))
                    reduction.greet()
                if start == project:
                    rounds.first.append(vector_flow)
                rounds.move(begins, reduction.parts)

        def keep(number, product):
            made[number] = product.astype(LOW).reshape(made.shape[1:])

        @pl.when(step == 0)
        def _():
            terms[...] = jnp.zeros_like(terms)
            load(range(4), wait=True)

            def remake(at):
                grads[1, at] = (unit[at] * vectors[3:4] + vectors[4:5]).astype(LOW)

            for_rows(total_rows, remake)
            keep(0, dot_tn(grads[1], cross_query_grad[...]) * SCALE)
            total[...] = dot_nt(cross_query_grad[...], query_weight[...]) * SCALE

            def first_norm(at):
                grad = grad_two[at] + total[at]
                down_grad = norm_back(grad, unit[at], inverse[at], vectors[3:4])
                total[at] = down_grad
                grads[2, at] = down_grad.astype(LOW)
                add_norm_sums(terms, 2, grads[2, at], grad, unit[at])

            for_rows(total_rows, first_norm)
            spread = jnp.sum(cross_sums[...], axis=0)
            terms[5:6] = spread[0:1] * SCALE
            terms[6:7] = spread[1:2]
            terms[7:10] = out_sums[0:3]
            terms[10:13] = feed_sums[0:3]
            for k in range(bias_grad.shape[1] // span):
                terms[13 + k : 14 + k] = bias_grad[:, k * span : (k + 1) * span]

        @pl.when(step == 1)
        def _():
            load(range(4, len(fetched)), wait=True)
            fill_tokens(low, tokens)
            keep(1, dot_tn(mixed[...], grads[2]))
            grads[0] = dot_nt(grads[2], weight[0]).astype(LOW)

        @pl.when((step >= attend) & (step < project))
        def _():
            s = step - attend
            allowed = causal_allowed(rows, mask[pl.ds(s, 1)])
            table_at = pl.ds(pl.multiple_of(s * rows, 16), rows)

            def pair(lane, head):
                where = (table_at, pl.ds(lane, PAIR))
                table = logs[table_at]
                columns = [pick_column(table, head + which) for which in range(2)]
                found = attend_pair_back(
                    qkv[(0,) + where],
                    qkv[(1,) + where],
                    qkv[(2,) + where],
                    allowed,
                    columns,
                    grads[(0,) + where],
                )
                for number in range(3):
                    grads[(1 + number,) + where] = found[number]

            for_head_groups(span, pair)

        @pl.when(step == project - 1)
        def _():
            terms[0:1] = column_sum(grads[1]) * SCALE
            terms[1:2] = column_sum(grads[3])

        @pl.when(step >= project)
        def _():
            factor = jnp.where(step == project, SCALE, 1.0)
            part = grads[step - project + 1]
            keep(step - project + 2, dot_tn(low[...], part) * factor)
            total[...] += dot_nt(part, weight[0]) * factor

        @pl.when(step == last)
        def _():
            store_tokens(input_grad, total[...])
            rounds.finish()

    small = (mask, vectors, self_full, inverse, cross_sums, feed_sums, out_sums, bias_grad)
    specs = [once_spec(operand.shape) for operand in small]
    specs[2] = pl.BlockSpec(
        (1, span, span), lambda i: (jnp.where(i < project, 3, i - project), 0, 0)
    )
    return pl.pallas_call(
        kernel,
        grid=(last + 1,),
        in_specs=specs
        + [pl.BlockSpec(memory_space=pl.ANY)] * len(fetched)
        + reduction.in_specs(),
        out_specs=[once_spec(tokens.shape)] + reduction.out_specs(),
        out_shape=[jax.ShapeDtypeStruct(tokens.shape, jnp.float32)] + reduction.outs(),
        scratch_shapes=[
            pltpu.VMEM((total_rows, span), LOW),
            pltpu.VMEM((4, total_rows, span), LOW),
            pltpu.VMEM((total_rows, span), jnp.float32),
            pltpu.SemaphoreType.DMA((len(fetched),)),
        ]
        + [
            pltpu.VMEM((span, span) if number == 1 else array.shape, array.dtype)
            for number, array in enumerate(fetched)
        ]
        + reduction.scratch(),
        compiler_params=params(collective_id=collective_id, has_side_effects=True),
        name="self_backward",
    )(*small, *fetched, *reduction.operands())


def hand_over(arrays):
    pieces = []
    for number, array in enumerate(arrays):
        parts = 8 if array.shape[0] % 64 == 0 else array.shape[0] if array.ndim == 3 else 1
        size = array.shape[0] // parts
        pieces += [(number, part * size, size) for part in range(parts)]
    count = len(arrays)

    def kernel(*refs):
        sources, targets, rest = refs[:count], refs[count : 2 * count], refs[2 * count :]
        buffers, loads, stores = rest[:-2], rest[-2], rest[-1]

        def load(k):
            number, first, size = pieces[k]
            return pltpu.make_async_copy(sources[number].at[pl.ds(first, size)], buffers[k], loads.at[k])

        def store(k):
            number, first, size = pieces[k]
            return pltpu.make_async_copy(buffers[k], targets[number].at[pl.ds(first, size)], stores.at[k])

        for k in range(len(pieces)):
            load(k).start()
        for k in range(len(pieces)):
            load(k).wait()
            store(k).start()
        for k in range(len(pieces)):
            store(k).wait()

    anywhere = pl.BlockSpec(memory_space=pl.ANY)
    return pl.pallas_call(
        kernel,
        in_specs=[anywhere] * count,
        out_specs=[anywhere] * count,
        out_shape=[jax.ShapeDtypeStruct(array.shape, array.dtype) for array in arrays],
        scratch_shapes=[
            pltpu.VMEM((size,) + arrays[number].shape[1:], arrays[number].dtype)
            for number, first, size in pieces
        ]
        + [pltpu.SemaphoreType.DMA((len(pieces),))] * 2,
        compiler_params=params(),
        name="hand_over",
    )(*arrays)


def per_device(
    wide,
    narrow,
    decoder_input,
    memory,
    decoder_mask,
    memory_length,
    self_weights,
    cross_weights,
    feed_weights,
    vectors,
    hidden_bias,
    cotangent,
):
    seq_count, seq_length, model_width = decoder_input.shape
    mem_span = memory.shape[1]
    memory_low = memory.reshape(seq_count * mem_span, model_width)
    saved, (self_full, cross_full, feed_full, vector_all, unused_bias) = front(
        Gather(
            wide, narrow, [self_weights, cross_weights, feed_weights], [vectors, hidden_bias]
        ),
        decoder_input,
        decoder_mask,
        memory_length,
        memory_low,
        cotangent,
        1,
    )
    qkv, self_mixed, unit_one, cross_query, cross_keys, cross_values, cross_mixed, unit_two = saved[:8]
    self_logs, inverse_one, cross_logs = saved[8:11]
    hidden, slope, layer_output, inverse_two, grad_three, feed_sums = saved[11:]
    parts = feed_full.shape[0] // 2
    (
        bias_part, grad_two, cross_out_grad, out_sums, cross_gq, cross_sums, memory_grad, memory_parts, feed_grad
    ) = middle_backward(
        Reduction(
            wide,
            narrow,
            model_width,
            [],
            1,
            [(0, matrix, part) for part in range(parts) for matrix in range(2)],
            [(2, parts)],
            [2 * (part % 2) + matrix for part in range(parts) for matrix in range(2)],
        ),
        grad_three,
        unit_two,
        inverse_two,
        vector_all,
        hidden,
        slope,
        feed_full,
        cross_full,
        cross_mixed,
        cross_query,
        cross_keys,
        cross_values,
        memory_length,
        cross_logs,
        memory_low,
        2,
    )
    places = [(0, 1), (0, 2), (0, 3), (0, 0), (1, 3), (1, 0), (1, 1), (1, 2)]
    input_grad, cross_grad, self_weight_gradient, vectors_grad, hidden_bias_grad = self_backward(
        Reduction(
            wide,
            narrow,
            model_width,
            [memory_parts, cross_out_grad[None]],
            2,
            [place + (0,) for place in places],
            [(4, 1), (4, 1)],
            range(5),
            [vectors.shape, hidden_bias.shape],
        ),
        3,
        decoder_input,
        decoder_mask,
        vector_all,
        self_full,
        cross_full,
        (qkv, self_mixed, self_logs, unit_one, inverse_one),
        cross_gq,
        grad_two,
        cross_sums,
        feed_sums,
        out_sums,
        bias_part,
    )
    (
        memory_grad, input_grad, layer_output, feed_grad, cross_grad, self_weight_gradient, vectors_grad,
        hidden_bias_grad,
    ) = hand_over(
        [
            memory_grad, input_grad, layer_output, feed_grad, cross_grad, self_weight_gradient,
            vectors_grad, hidden_bias_grad,
        ]
    )
    return (
        layer_output,
        input_grad,
        memory_grad.reshape(seq_count, mem_span, model_width),
        self_weight_gradient,
        cross_grad,
        feed_grad,
        vectors_grad,
        hidden_bias_grad,
    )


def solution(mesh):
    placed = (
        P(("wide", "narrow"), None, None),
        P(("wide", "narrow"), None, None),
        P(("wide", "narrow"), None),
        P(("wide", "narrow")),
        P(None, "wide", "narrow"),
        P(None, "wide", "narrow"),
        P(None, "wide", "narrow"),
        P(None, "narrow"),
        P(None, "narrow"),
        P(("wide", "narrow"), None, None),
    )
    return jax.shard_map(
        functools.partial(per_device, mesh.shape["wide"], mesh.shape["narrow"]),
        mesh=mesh,
        in_specs=placed,
        out_specs=(
            P(("wide", "narrow"), None, None),
            P(("wide", "narrow"), None, None),
            P(("wide", "narrow"), None, None),
            P(None, "wide", "narrow"),
            P(None, "wide", "narrow"),
            P(None, "wide", "narrow"),
            P(None, "narrow"),
            P(None, "narrow"),
        ),
        check_vma=False,
    )
```

```python
import functools
import math

import jax
import jax.numpy as jnp
from jax import lax
from jax.experimental import pallas as pl
from jax.experimental.pallas import tpu as pltpu
from jax.sharding import PartitionSpec as P

HEADS = 16
HEAD_DIM = 64


MESH_ID = pl.DeviceIdType.MESH


class Position:
    def __init__(self, wide, narrow):
        self.sizes = {"line": wide // 4, "pair": 2, "core": 2, "column": narrow}

    def get(self, axis):
        if axis == "column":
            return lax.axis_index("narrow")
        index = lax.axis_index("wide")
        if axis == "core":
            return index % 2
        return (index // 2) % 2 if axis == "pair" else index // 4

    def device(self, **moved):
        spot = {name: moved.get(name, self.get(name)) for name in self.sizes}
        return (spot["line"] * 4 + spot["pair"] * 2 + spot["core"], spot["column"])


class Channels:
    def __init__(self, sends, recvs):
        self.sends, self.recvs, self.used = sends, recvs, 0

    def take(self):
        self.used += 1
        number = self.used - 1
        return lambda: (self.sends.at[number], self.recvs.at[number])


def remote(source, target, channel, device):
    return pltpu.make_async_remote_copy(
        src_ref=source,
        dst_ref=target,
        send_sem=channel()[0],
        recv_sem=channel()[1],
        device_id=device,
        device_id_type=MESH_ID,
    )


def flip(index, bit):
    return index + bit - 2 * bit * ((index // bit) % 2)


def peers(position, axis, distance):
    at = (position.get(axis) + distance) % position.sizes[axis]
    return at, position.device(**{axis: at})


def greet(position):
    barrier = pltpu.get_barrier_semaphore()
    expected = 0
    for axis, size in position.sizes.items():
        for distance in range(1, size):
            pl.semaphore_signal(
                barrier,
                inc=1,
                device_id=peers(position, axis, distance)[1],
                device_id_type=MESH_ID,
            )
            expected += 1
    pl.semaphore_wait(barrier, expected)


def advance(generator):
    return next(generator, "done") != "done"


class Rounds:
    def __init__(self, flows, live=()):
        self.waiting, self.live = list(flows), list(live)
        self.all, self.first = None, []

    def run(self, start=0):
        self.live = self.live + self.waiting[:start]
        self.waiting = self.waiting[start:]
        self.live = [flow for flow in self.live if advance(flow)]

    def move(self, groups, size=2):
        if self.all is None:
            self.all = [*self.waiting]
            self.waiting, self.first, self.live = [], self.live, list(self.all)
        for group in groups:
            self.first = [flow for flow in self.first if advance(flow)]
            for flow in self.all[group * size : group * size + size]:
                if not advance(flow):
                    self.live.remove(flow)

    def finish(self, together=2):
        self.live, self.first = self.live + self.first, []
        while self.waiting or self.live:
            self.run(together)


def finish_sends(sent):
    for describe in sent:
        describe().wait_send()


def gather_axis(position, axis, channels, block, own, sent):
    arrivals = []
    for distance in range(1, position.sizes[axis]):
        channel = channels.take()

        def send(distance=distance, channel=channel):
            device = peers(position, axis, distance)[1]
            return remote(own(), block(position.get(axis)), channel, device)

        def arrival(distance=distance, channel=channel):
            came, device = peers(position, axis, -distance)
            return remote(block(came), block(came), channel, device)

        send().start()
        sent.append(send)
        arrivals.append(arrival)
    yield
    for arrival in arrivals:
        arrival().wait_recv()


def gather_flow(position, channels, local_sem, own, region, order):
    sent = []

    def place(done, axis=None, at=None):
        spot = {name: None if name in done else position.get(name) for name in position.sizes}
        if axis is not None:
            spot[axis] = at
        return region(**spot)

    def local():
        return pltpu.make_async_copy(own(), place(()), local_sem())

    local().start()
    for number, axis in enumerate(order):
        done = order[:number]

        def block(j, axis=axis, done=done):
            return place(done, axis, j)

        def source(block=block, axis=axis, first=number == 0):
            return own() if first else block(position.get(axis))

        yield from gather_axis(position, axis, channels, block, source, sent)
        if number == 0:
            local().wait()
    finish_sends(sent)


def whole(index):
    return slice(None) if index is None else index


def row_splits(rows, most):
    return max(1, min(most, rows // 16))


def flow_channels(wide, narrow):
    return 2 + (wide // 4 - 1) + (narrow - 1)


ORDER_A = ("line", "pair", "column", "core")
ORDER_B = ("line", "column", "pair", "core")


def lane_parts(wide, narrow, block):
    return block.shape[2] * narrow // (block.shape[1] * wide)


def gather_flows(position, channels, local_sems, parts, blocks, fulls):
    jobs = []
    for block_ref, full_ref, count in zip(blocks, fulls, parts):
        jobs += [(block_ref, full_ref, count, place, 0, 1) for place in range(full_ref.shape[0])]
    jobs = [job[:4] + (half, 2) for half in range(2) for job in jobs[:2]] + jobs[2:]
    flows = []
    for block_ref, full_ref, count, place, half, halves in jobs:
        width, rows = block_ref.shape[2] // count, block_ref.shape[1] // halves
        part, matrix = divmod(place, block_ref.shape[0])
        at = pl.ds(half * rows, rows)

        def region(line, pair, core, column, full_ref=full_ref, place=place, width=width, at=at):
            lanes = slice(None)
            if column is not None:
                lanes = pl.ds(pl.multiple_of(column * width, 128), width)
            return full_ref.at[place, whole(line), whole(pair), whole(core), at, lanes]

        def own(block_ref=block_ref, matrix=matrix, part=part, width=width, at=at):
            return block_ref.at[matrix, at, part * width : (part + 1) * width]

        number = len(flows)
        order = ORDER_A if number % 2 == 0 else ORDER_B
        flows.append(
            gather_flow(
                position, channels, lambda number=number: local_sems.at[number], own, region, order
            )
        )
    return flows


def column_flow(position, channels, sem, block_ref, full_ref):
    width = block_ref.shape[1]

    def region(column):
        return full_ref.at[:, pl.ds(pl.multiple_of(column * width, 128), width)]

    def local():
        return pltpu.make_async_copy(block_ref, region(position.get("column")), sem())

    sent = []
    local().start()
    yield from gather_axis(position, "column", channels, region, lambda: block_ref, sent)
    local().wait()
    finish_sends(sent)


class Gather:
    def __init__(self, wide, narrow, arrays, vectors=()):
        self.wide, self.narrow = wide, narrow
        self.arrays, self.vectors = list(arrays), list(vectors)
        self.parts = [lane_parts(wide, narrow, array) for array in arrays]
        self.count = 2 + sum(array.shape[0] * part for array, part in zip(arrays, self.parts))

    def operands(self):
        return self.arrays + self.vectors

    def in_specs(self):
        return [pl.BlockSpec(memory_space=pltpu.VMEM)] * len(self.operands())

    def wholes(self):
        return [(vector.shape[0], vector.shape[1] * self.narrow) for vector in self.vectors]

    def outs(self):
        outs = []
        for array, part in zip(self.arrays, self.parts):
            matrices, rows, width = array.shape
            shape = (matrices * part, self.wide // 4, 2, 2, rows, width // part * self.narrow)
            outs.append(jax.ShapeDtypeStruct(shape, array.dtype))
        return outs + [jax.ShapeDtypeStruct(shape, jnp.float32) for shape in self.wholes()]

    def out_specs(self):
        specs = [pl.BlockSpec(memory_space=pl.ANY)] * len(self.arrays)
        return specs + [pl.BlockSpec(memory_space=pltpu.VMEM)] * len(self.vectors)

    def scratch(self):
        flows = self.count + len(self.vectors)
        copies = flow_channels(self.wide, self.narrow) * flows
        return [
            pltpu.SemaphoreType.DMA((copies,)),
            pltpu.SemaphoreType.DMA((copies,)),
            pltpu.SemaphoreType.DMA((flows,)),
        ] + [pltpu.VMEM(shape, jnp.float32) for shape in self.wholes()]

    def rounds(self, operands, outs, scratch):
        position = Position(self.wide, self.narrow)
        channels = Channels(scratch[0], scratch[1])
        count, local_sems, wholes = len(self.arrays), scratch[2], scratch[3:]
        live = [
            column_flow(
                position,
                channels,
                lambda k=k: local_sems.at[self.count + k],
                operands[count + k],
                wholes[k],
            )
            for k in range(len(self.vectors))
        ]
        flows = gather_flows(
            position, channels, local_sems, self.parts, operands[:count], outs[:count]
        )
        return Rounds(flows, live), wholes

    def greet(self):
        greet(Position(self.wide, self.narrow))

    def join(self, results):
        count = len(self.arrays)
        fulls = [full.reshape(full.shape[0], -1, full.shape[-1]) for full in results[:count]]
        return fulls + list(results[count:])


def add_rows(target, parts):
    lead = target.shape[:-2]
    count = math.prod(lead)

    def add(spot):
        total = parts[0][spot].astype(jnp.float32)
        for part in parts[1:]:
            total = total + part[spot].astype(jnp.float32)
        target[spot] = total.astype(target.dtype)

    if count == 1:
        add((0,) * len(lead))
        return

    @pl.loop(0, count)
    def _(k):
        where = []
        for extent in reversed(lead):
            where.insert(0, k % extent)
            k = k // extent
        add(tuple(where))


def reduce_axis(position, axis, channels, local, slots, result, sent):
    size = position.sizes[axis]
    for distance in range(1, size):
        channel = channels.take()

        def send(distance=distance, channel=channel):
            at, device = peers(position, axis, distance)
            return remote(local(at), slots.at[distance - 1], channel, device)

        send().start()
        sent.append(send)
    yield
    for send in sent[1 - size :]:
        send().wait_recv()
    add_rows(
        result(), [local(position.get(axis))] + [slots.at[k] for k in range(size - 1)]
    )


def reduce_flow(position, channels, local_sem, loc, grads, result, buffers, order):
    first, mid, last, line_slots = buffers
    sent = []

    def own():
        return pltpu.make_async_copy(grads(position.get("core")), loc(), local_sem())

    def mine():
        return grads(position.get("core")) if loc is None else loc()

    channel = channels.take()

    def swap():
        core = position.get("core")
        return remote(grads(1 - core), first, channel, position.device(core=1 - core))

    if loc is not None:
        own().start()
    swap().start()
    yield
    if loc is not None:
        own().wait()
    swap().wait_recv()
    add_rows(first, [first, mine()])
    swap().wait_send()
    width = result().shape[-1]

    def columns(j):
        return pl.ds(pl.multiple_of(j * width, 128), width)

    def held():
        return mid.at[0]

    def final():
        return last.at[0]

    if order == "A":
        yield from reduce_axis(
            position, "column", channels, lambda j: first.at[:, :, :, columns(j)], mid, held, sent
        )
        yield from reduce_axis(position, "pair", channels, lambda j: held().at[:, j], last, final, sent)
    else:
        yield from reduce_axis(position, "pair", channels, lambda j: first.at[:, j], mid, held, sent)
        yield from reduce_axis(
            position, "column", channels, lambda j: held().at[:, :, columns(j)], last, final, sent
        )
    yield from reduce_axis(
        position, "line", channels, lambda j: final().at[pl.ds(j, 1)], line_slots, result, sent
    )
    finish_sends(sent)


def double_flow(position, channels, terms, total, inbox, vectors_out, bias_out):
    total[0] = terms[...]
    step = 0
    for axis in ("core", "pair", "line", "column"):
        bit = 1
        while bit < position.sizes[axis]:
            channel = channels.take()

            def describe():
                to = position.device(**{axis: flip(position.get(axis), bit)})
                return remote(total.at[step], inbox.at[step], channel, to)

            describe().start()
            yield
            describe().wait_recv()
            total[step + 1] = total[step] + inbox[step]
            describe().wait_send()
            bit *= 2
            step += 1
    count, width = vectors_out.shape
    lanes = pl.ds(pl.multiple_of(position.get("column") * width, 128), width)
    vectors_out[...] = total[step, 0:count, lanes]
    for k in range(bias_out.shape[1] // width):
        bias_out[:, k * width : (k + 1) * width] = total[step, count + k : count + k + 1, lanes]


class Reduction:
    RING = 6

    def __init__(self, wide, narrow, depth, arrays, parts, places, matrices, held=(), shapes=()):
        self.wide, self.narrow, self.held, self.shapes = wide, narrow, held, list(shapes)
        depth = span = depth
        self.rows = rows = depth // wide
        self.parts = row_splits(rows, parts)
        self.piece = rows // self.parts
        self.line, self.span, self.width = wide // 4, span, span // narrow
        self.matrices = matrices
        sources = [(s, m) for s, array in enumerate(arrays) for m in range(array.shape[0])]
        sources += [(None, m) for m in held]
        self.pieces = [
            source + (part,) + place
            for source, place in zip(sources, places)
            for part in range(self.parts)
        ]
        self.views = [array.reshape(array.shape[0], self.line, 2, 2, rows, span) for array in arrays]

    def order(self, number):
        return "A" if number % 2 == 0 else "B"

    def operands(self):
        return self.views

    def in_specs(self):
        return [pl.BlockSpec(memory_space=pl.ANY)] * len(self.views)

    def outs(self):
        outs = [
            jax.ShapeDtypeStruct((count, self.rows, self.width * parts), jnp.float32)
            for count, parts in self.matrices
        ]
        return outs + [jax.ShapeDtypeStruct(shape, jnp.float32) for shape in self.shapes]

    def out_specs(self):
        return [pl.BlockSpec(memory_space=pltpu.VMEM)] * len(self.outs())

    def steps(self):
        return (self.wide * self.narrow).bit_length() - 1

    def terms_shape(self):
        count = self.shapes[0][0] + self.shapes[1][1] * self.narrow // self.span
        return (count + -count % 8, self.span)

    def scratch(self):
        low, line, piece = jnp.bfloat16, self.line, self.piece
        copies = flow_channels(self.wide, self.narrow) * len(self.pieces) + 16
        shapes = [
            pltpu.SemaphoreType.DMA((copies,)),
            pltpu.SemaphoreType.DMA((copies,)),
            pltpu.SemaphoreType.DMA((len(self.pieces),)),
            pltpu.VMEM((self.RING, line, 2, piece, self.span), low)
            if self.views
            else pltpu.VMEM((8, 128), low),
        ]
        if self.held:
            shapes.append(pltpu.VMEM((1 + max(self.held), line, 2, 2, self.rows, self.span), low))
        if self.shapes:
            shapes.append(pltpu.VMEM(self.terms_shape(), jnp.float32))
            shapes.append(pltpu.VMEM((self.steps() + 1,) + self.terms_shape(), jnp.float32))
            shapes.append(pltpu.VMEM((self.steps(),) + self.terms_shape(), jnp.float32))
        for number in range(len(self.pieces)):
            shapes.append(pltpu.VMEM((line, 2, piece, self.span), low))
            if self.order(number) == "A":
                shapes.append(pltpu.VMEM((self.narrow - 1, line, 2, piece, self.width), low))
                shapes.append(pltpu.VMEM((1, line, piece, self.width), low))
            else:
                shapes.append(pltpu.VMEM((1, line, piece, self.span), low))
                shapes.append(pltpu.VMEM((self.narrow - 1, line, piece, self.width), low))
            shapes.append(pltpu.VMEM((line - 1, 1, piece, self.width), low))
        return shapes

    def rounds(self, operands, outs, scratch):
        position = Position(self.wide, self.narrow)
        channels = Channels(scratch[0], scratch[1])
        local_sems, ring, buffers = scratch[2], scratch[3], list(scratch[4:])
        made = buffers.pop(0) if self.held else None
        terms, vector_flow = None, None
        if self.shapes:
            terms, total, inbox = buffers[:3]
            buffers = buffers[3:]
            vector_flow = double_flow(position, channels, terms, total, inbox, *outs[-2:])
        flows = []
        for number, (source, inner, part, out, matrix, slot) in enumerate(self.pieces):
            at = pl.ds(part * self.piece, self.piece)
            lanes = pl.ds(slot * self.width, self.width)

            def grads(core, source=source, inner=inner, at=at):
                array = made if source is None else operands[source]
                return array.at[inner, :, :, core, at]

            flows.append(
                reduce_flow(
                    position,
                    channels,
                    lambda number=number: local_sems.at[number],
                    None if source is None else lambda number=number: ring.at[number % self.RING],
                    grads,
                    lambda out=out, at=(pl.ds(matrix, 1), at, lanes): outs[out].at[at],
                    buffers[4 * number : 4 * number + 4],
                    self.order(number),
                )
            )
        return Rounds(flows), made, terms, vector_flow

    def greet(self):
        greet(Position(self.wide, self.narrow))


LOW = jnp.bfloat16
NEGATIVE = -1000000000.0
EPSILON = 1e-05
PAIR = 2 * HEAD_DIM
SCALE = HEAD_DIM ** (-0.5)
BUDGET = 65000 * 1024


def dot_nn(left, right):
    return jnp.dot(left, right, preferred_element_type=jnp.float32)


def dot_nt(left, right):
    return lax.dot_general(
        left, right, (((1,), (1,)), ((), ())), preferred_element_type=jnp.float32
    )


def dot_tn(left, right):
    return lax.dot_general(
        left, right, (((0,), (0,)), ((), ())), preferred_element_type=jnp.float32
    )


def padded(length):
    return -(-length // 16) * 16


def column_sum(rows):
    return jnp.sum(rows.astype(jnp.float32), axis=0, keepdims=True)


def standardise(hidden):
    centre = hidden - jnp.mean(hidden, axis=-1, keepdims=True)
    spread = jnp.mean(centre * centre, axis=-1, keepdims=True)
    inverse = lax.rsqrt(spread + EPSILON)
    return centre * inverse, inverse


def norm_back(grad, unit, inverse, gain):
    scaled = grad * gain
    first = jnp.mean(scaled, axis=-1, keepdims=True)
    second = jnp.mean(scaled * unit, axis=-1, keepdims=True)
    return inverse * (scaled - first - unit * second)


def for_rows(total, function, most=48):
    chunk = next(size for size in range(most, 0, -16) if total % size == 0)

    @pl.loop(0, total // chunk)
    def _(k):
        function(pl.ds(pl.multiple_of(k * chunk, 16), chunk))


def add_norm_sums(sums, first, low, grad, unit):
    sums[first : first + 1] += column_sum(low)
    sums[first + 1 : first + 2] += column_sum(grad * unit)
    sums[first + 2 : first + 3] += column_sum(grad)


def fill_tokens(target, source):
    count, length, span = source.shape
    rows = padded(length)
    for s in range(count):
        if rows > length:
            base = s * rows + length // 16 * 16
            target[base : (s + 1) * rows] = jnp.zeros(((s + 1) * rows - base, span), target.dtype)
        target[s * rows : s * rows + length] = source[s].astype(target.dtype)


def store_tokens(target, values):
    count, length, span = target.shape
    rows = padded(length)
    for s in range(count):
        target[s] = values[s * rows : s * rows + length].astype(target.dtype)


def head_lanes(rows, which):
    lane = lax.broadcasted_iota(jnp.int32, rows.shape, 1)
    return (lane >= HEAD_DIM) == (which == 1)


def one_head(rows, which):
    return jnp.where(head_lanes(rows, which), rows, jnp.zeros_like(rows))


def pick_column(table, number):
    lane = lax.broadcasted_iota(jnp.int32, table.shape, 1)
    return jnp.sum(jnp.where(lane == number, table, 0.0), axis=1, keepdims=True)


def attend_pair(query, keys, values, allowed):
    mixed, logs = [], []
    for which in range(2):
        scores = dot_nt(one_head(query, which), keys)
        scores = jnp.where(allowed, scores, NEGATIVE)
        peak = jnp.max(scores, axis=-1, keepdims=True)
        expo = jnp.exp(scores - peak)
        total = jnp.sum(expo, axis=-1, keepdims=True)
        weights = (expo * (1.0 / total)).astype(LOW)
        mixed.append(dot_nn(weights, values))
        logs.append(peak + jnp.log(total))
    both = jnp.where(head_lanes(mixed[0], 0), mixed[0], mixed[1])
    return both.astype(LOW), logs


def attend_pair_back(query, keys, values, allowed, logs, grad):
    grad_query, grad_keys, grad_values = [], None, None
    for which in range(2):
        query_one, grad_one = one_head(query, which), one_head(grad, which)
        scores = jnp.where(allowed, dot_nt(query_one, keys), NEGATIVE)
        probs = jnp.exp(scores - logs[which])
        grad_probs = dot_nt(grad_one, values)
        slope = jnp.sum(grad_probs * probs, axis=-1, keepdims=True)
        grad_scores = (probs * (grad_probs - slope)).astype(LOW)
        grad_query.append(dot_nn(grad_scores, keys))
        part_keys = dot_tn(grad_scores, query_one)
        part_values = dot_tn(probs.astype(LOW), grad_one)
        grad_keys = part_keys if which == 0 else grad_keys + part_keys
        grad_values = part_values if which == 0 else grad_values + part_values
    both = jnp.where(head_lanes(grad_query[0], 0), grad_query[0], grad_query[1])
    return both.astype(LOW), grad_keys.astype(LOW), grad_values.astype(LOW)


def causal_allowed(rows, mask_row):
    valid = jnp.sum(mask_row, axis=-1, keepdims=True)
    query_at = lax.broadcasted_iota(jnp.int32, (rows, rows), 0)
    key_at = lax.broadcasted_iota(jnp.int32, (rows, rows), 1)
    return (query_at >= key_at) & (key_at < valid)


GROUP_PAIRS = 2


def for_head_groups(span, function):
    lanes = min(span, GROUP_PAIRS * PAIR)

    @pl.loop(0, span // lanes)
    def _(g):
        for p in range(lanes // PAIR):
            function(pl.multiple_of(g * lanes + p * PAIR, PAIR), 2 * (g * (lanes // PAIR) + p))


def whole_spec(shape):
    return pl.BlockSpec(shape, lambda *at: (0,) * len(shape))


def params(**more):
    return pltpu.CompilerParams(vmem_limit_bytes=BUDGET, **more)


CROSS_LANES = 2 * PAIR


def once_spec(shape):
    return pl.BlockSpec(shape, lambda *at: (0,) * len(shape), pipeline_mode=pl.Buffered(1))


def front(load, tokens, mask, lengths, memory, cotangent, collective_id):
    count, length, span = tokens.shape
    rows = padded(length)
    total, slots = count * rows, memory.shape[0] // count
    tiles = 4
    tile = memory.shape[0] // tiles
    groups = span // CROSS_LANES
    attend, join, ask = 3, 3 + count, 4 + count
    recall = ask + 1
    look = recall + tiles
    add = look + count * groups
    feed = add + 1
    parts = load.parts[2]
    last = feed + parts - 1
    carried = len(load.operands())
    plan = {
        0: (0, 1, 0, 2, 1, 0, 1, 2, 3, 0, 1, 2, 3, 4, 0, 1),
        2: (2, 3, 4, 5, 2),
        ask: (3, 4, 5, 6, 3),
        recall: (4, 5, 6, 7, 4),
        look: (5, 6, 7, 8),
        look + 5: (5, 6, 7, 8),
        feed + 1: (6, 7, 8),
        feed + 2: (7,),
        feed + 3: (8, 8),
    }

    def kernel(*refs):
        tokens, mask, lengths, memory, cotangent = refs[:5]
        operands, refs = refs[5 : 5 + carried], refs[5 + carried :]
        stored, (logs, inverse, cross_logs) = refs[: len(kept)], refs[len(kept) : len(kept) + 3]
        hidden, slope, output, inverse_two, grad_three, sums = refs[len(kept) + 3 : len(kept) + 9]
        refs = refs[len(kept) + 9 :]
        results, refs = refs[:carried], refs[carried:]
        low, spare, running, weights, weight_sem, store_sems = refs[:6]
        held, scratch = refs[6 : 6 + len(kept)], refs[6 + len(kept) :]
        qkv, mixed, unit, query, keys, values, cross_mixed, unit_two = held
        step = pl.program_id(0)
        rounds, (vectors, bias) = load.rounds(operands, results, scratch)
        for start, begins in plan.items():

            @pl.when(step == start)
            def _():
                if start == 0:
                    load.greet()
                rounds.move(begins)

        def store(*numbers, wait=False):
            for number in numbers:
                copy = pltpu.make_async_copy(
                    held[number], stored[number], store_sems.at[number]
                )
                copy.wait() if wait else copy.start()

        @pl.when(step == recall)
        def _():
            store(0, 1, 2, 3)

        @pl.when(step == look)
        def _():
            store(4, 5)

        @pl.when(step == feed)
        def _():
            store(6, 7)

        def fetch(array, matrix, slot):
            copy = pltpu.make_async_copy(results[array].at[matrix], weights.at[slot], weight_sem)
            copy.start()
            copy.wait()

        def weight(slot):
            return weights[slot].reshape(span, span)

        @pl.when(step == 0)
        def _():
            fill_tokens(low, tokens)

        @pl.when(step < attend)
        def _():
            fetch(0, step, 0)
            product = dot_nn(low[...], weight(0))
            none = jnp.zeros_like(vectors[0:1])
            shift = jnp.where(step == 0, vectors[0:1], jnp.where(step == 2, vectors[1:2], none))
            product = (product + shift) * jnp.where(step == 0, SCALE, 1.0)
            qkv[step] = product.astype(LOW)

        @pl.when((step >= attend) & (step < join))
        def _():
            s = step - attend
            allowed = causal_allowed(rows, mask[pl.ds(s, 1)])
            table_at = pl.ds(pl.multiple_of(s * rows, 16), rows)
            logs[table_at] = jnp.zeros((rows, 128), jnp.float32)

            def pair(lane, head):
                where = (table_at, pl.ds(lane, PAIR))
                both, sums = attend_pair(
                    qkv[(0,) + where], qkv[(1,) + where], qkv[(2,) + where], allowed
                )
                mixed[where] = both
                table = logs[table_at]
                spot = lax.broadcasted_iota(jnp.int32, table.shape, 1)
                for which in range(2):
                    table = jnp.where(spot == head + which, sums[which], table)
                logs[table_at] = table

            for_head_groups(span, pair)

        @pl.when(step == join)
        def _():
            fetch(0, 3, 0)
            running[...] = dot_nn(mixed[...], weight(0))

            def first_norm(at):
                summed = low[at].astype(jnp.float32) + (running[at] + vectors[2:3])
                found, inverse[at] = standardise(summed)
                unit[at] = found
                spare[at] = (found * vectors[3:4] + vectors[4:5]).astype(LOW)

            for_rows(total, first_norm, 160)

        @pl.when(step == ask)
        def _():
            fetch(1, 0, 0)
            product = dot_nn(spare[...], weight(0))
            query[...] = ((product + vectors[5:6]) * SCALE).astype(LOW)

        @pl.when(step == recall)
        def _():
            fetch(1, 1, 0)
            fetch(1, 2, 1)

        @pl.when((step >= recall) & (step < look))
        def _():
            at = pl.ds(pl.multiple_of((step - recall) * tile, 16), tile)
            keys[at] = dot_nn(memory[...], weight(0)).astype(LOW)
            values[at] = (dot_nn(memory[...], weight(1)) + vectors[6:7]).astype(LOW)

        @pl.when((step >= look) & (step < add))
        def _():
            s, g = (step - look) // groups, (step - look) % groups
            slot = lax.broadcasted_iota(jnp.int32, (1, slots), 1)
            allowed = slot < lengths[s]
            token_at = pl.ds(pl.multiple_of(s * rows, 16), rows)
            slot_at = pl.ds(pl.multiple_of(s * slots, 16), slots)
            cross_logs[...] = jnp.zeros_like(cross_logs)

            @pl.loop(0, CROSS_LANES // PAIR)
            def _(p):
                lanes = pl.ds(pl.multiple_of(g * CROSS_LANES + p * PAIR, PAIR), PAIR)
                both, sums = attend_pair(
                    query[token_at, lanes], keys[slot_at, lanes], values[slot_at, lanes], allowed
                )
                cross_mixed[token_at, lanes] = both
                table = cross_logs[0]
                spot = lax.broadcasted_iota(jnp.int32, table.shape, 1)
                for which in range(2):
                    table = jnp.where(spot == 2 * p + which, sums[which], table)
                cross_logs[0] = table

        @pl.when(step == add)
        def _():
            fetch(1, 3, 0)
            running[...] = dot_nn(cross_mixed[...], weight(0))

            def second_norm(at):
                first = unit[at] * vectors[3:4] + vectors[4:5]
                found, inverse_two[at] = standardise(first + (running[at] + vectors[7:8]))
                unit_two[at] = found
                low[at] = (found * vectors[8:9] + vectors[9:10]).astype(LOW)
                running[at] = jnp.zeros_like(found)

            for_rows(total, second_norm, 160)
            fill_tokens(spare, cotangent)

        @pl.when(step >= feed)
        def _():
            part = step - feed
            fetch(2, 2 * part, 0)
            fetch(2, 2 * part + 1, 1)
            width = bias.shape[1] // parts // load.narrow
            shift = jnp.concatenate(
                [
                    bias[:, pl.ds(pl.multiple_of((n * parts + part) * width, 128), width)]
                    for n in range(load.narrow)
                ],
                axis=1,
            )
            half_lanes = span // 2
            row = lax.broadcasted_iota(jnp.int32, (8, span), 0)
            sums[...] = jnp.where(row == 0, shift, 0.0)

            for k in range(2):
                lanes = slice(k * half_lanes, (k + 1) * half_lanes)
                up = weights[0, :, :, :, :, lanes].reshape(span, half_lanes)
                down = weights[1, :, :, :, :, lanes].reshape(span, half_lanes)
                inner = dot_nn(low[...], up) + sums[0:1, lanes]
                half = 0.5 + 0.5 * lax.erf(inner * (0.5**0.5))
                bell = jnp.exp(-0.5 * inner * inner) * ((0.5 / math.pi) ** 0.5)
                active = (inner * half).astype(LOW)
                hidden[:, lanes] = active
                slope[:, lanes] = (half + inner * bell).astype(LOW)
                running[...] += dot_nt(active, down)

        @pl.when(step == last)
        def _():
            rounds.finish()
            results[-2][...], results[-1][...] = vectors[...], bias[...]
            sums[...] = jnp.zeros_like(sums)

            def third_norm(at):
                second = unit_two[at] * vectors[8:9] + vectors[9:10]
                found, inverse_three = standardise(second + (running[at] + vectors[10:11]))
                low[at] = (found * vectors[11:12] + vectors[12:13]).astype(LOW)
                grad = spare[at].astype(jnp.float32)
                down_grad = norm_back(grad, found, inverse_three, vectors[11:12])
                grad_three[at] = down_grad
                add_norm_sums(sums, 0, down_grad.astype(LOW), grad, found)

            for_rows(total, third_norm, 160)
            store_tokens(output, low)
            store(*range(len(kept)), wait=True)

    def token(dtype, lanes=span):
        return jax.ShapeDtypeStruct((total, lanes), dtype)

    kept = [
        jax.ShapeDtypeStruct((3, total, span), LOW),
        token(LOW),
        token(jnp.float32),
        token(LOW),
        jax.ShapeDtypeStruct(memory.shape, LOW),
        jax.ShapeDtypeStruct(memory.shape, LOW),
        token(LOW),
        token(jnp.float32),
    ]
    outs = kept + [
        token(jnp.float32, 128),
        token(jnp.float32, 1),
        jax.ShapeDtypeStruct((count * groups, rows, 128), jnp.float32),
        token(LOW, parts * span),
        token(LOW, parts * span),
        jax.ShapeDtypeStruct(cotangent.shape, LOW),
        token(jnp.float32, 1),
        token(jnp.float32),
        jax.ShapeDtypeStruct((8, span), jnp.float32),
    ]
    wide_tile = pl.BlockSpec((total, span), lambda i: (0, jnp.clip(i - feed, 0, parts - 1)))

    results = pl.pallas_call(
        kernel,
        grid=(last + 1,),
        in_specs=[
            once_spec(tokens.shape),
            once_spec(mask.shape),
            pl.BlockSpec(memory_space=pltpu.SMEM),
            pl.BlockSpec((tile, span), lambda i: (jnp.clip(i - recall, 0, tiles - 1), 0)),
            once_spec(cotangent.shape),
        ]
        + load.in_specs(),
        out_specs=[pl.BlockSpec(memory_space=pl.ANY)] * len(kept)
        + [
            once_spec((total, 128)),
            once_spec((total, 1)),
            pl.BlockSpec((1, rows, 128), lambda i: (jnp.clip(i - look, 0, count * groups - 1), 0, 0)),
            wide_tile,
            wide_tile,
        ]
        + [once_spec(out.shape) for out in outs[len(kept) + 5 :]]
        + load.out_specs(),
        out_shape=outs + load.outs(),
        scratch_shapes=[
            pltpu.VMEM((total, span), LOW),
            pltpu.VMEM((total, span), LOW),
            pltpu.VMEM((total, span), jnp.float32),
            pltpu.VMEM((2,) + load.outs()[0].shape[1:], LOW),
            pltpu.SemaphoreType.DMA,
            pltpu.SemaphoreType.DMA((len(kept),)),
        ]
        + [pltpu.VMEM(keep.shape, keep.dtype) for keep in kept]
        + load.scratch(),
        compiler_params=params(collective_id=collective_id, has_side_effects=True),
        name="front",
    )(tokens, mask, lengths, memory, cotangent, *load.operands())
    return results[: len(outs)], load.join(results[len(outs) :])


FEED_TILE = 512


def middle_backward(
    reduction, grad_three, unit_two, inverse_two, vectors, hidden, slope, feed_full, cross_full, mixed,
    query, keys, values, lengths, logs, memory, collective_id
):
    count = lengths.shape[0]
    total_rows, span = query.shape
    rows, slots = total_rows // count, keys.shape[0] // count
    groups = span // CROSS_LANES
    split = span // FEED_TILE
    feeds = feed_full.shape[0] // 2 * split
    heads, recall = feeds, feeds + count * groups
    tiles = 2 * count
    tile_rows, tile_lanes = keys.shape[0] // tiles, span // tiles
    last = recall + tiles - 1
    carried, produced = len(reduction.operands()), len(reduction.outs())
    plan = {
        2: (0,),
        3: (0,),
        4: (1,),
        6: (1,),
        7: (2,),
        heads: (3, 0, 1, 2, 3),
        heads + 1: (0,),
        heads + 2: (1,),
        heads + 6: (2,),
        heads + 7: (0,),
        recall: (2, 3),
        recall + 1: (3,),
        last: (1, 2, 3),
    }

    def kernel(*refs):
        lengths, unit_two, inverse_two, vectors, hidden, slope, up, down, mixed = refs[:9]
        query, keys, values, logs, grad_three, memory, cross_full = refs[9:16]
        operands, refs = refs[16 : 16 + carried], refs[16 + carried :]
        bias_grad, grad_two, out_grad, feed_sums, grad_query, sums = refs[:6]
        memory_grad, weight_grad = refs[6:8]
        results, refs = refs[8 : 8 + produced], refs[8 + produced :]
        low, branch, total, memory_low, weights, load_sems, scratch = *refs[:6], refs[6:]
        step = pl.program_id(0)
        rounds, made, *unused = reduction.rounds(operands, results, scratch)

        def load(number, wait=False):
            source, target = (
                (grad_three, total),
                (cross_full.at[3], weights.at[0]),
                (memory, memory_low),
                (cross_full.at[1], weights.at[0]),
                (cross_full.at[2], weights.at[1]),
            )[number]
            copy = pltpu.make_async_copy(source, target, load_sems.at[number])
            copy.wait() if wait else copy.start()

        @pl.when(step == 0)
        def _():
            load(0)
            load(1)
            reduction.greet()

            def begin(at):
                low[at] = (unit_two[at] * vectors[8:9] + vectors[9:10]).astype(LOW)
                branch[at] = total[at].astype(LOW)

            load(0, wait=True)
            for_rows(total_rows, begin)

        @pl.when(step == heads)
        def _():
            for number in (2, 3, 4):
                load(number)

        for start, begins in plan.items():

            @pl.when(step == start)
            def _():
                rounds.move(begins)

        @pl.when(step == recall)
        def _():
            for number in (2, 3, 4):
                load(number, wait=True)

        @pl.when(step < feeds)
        def _():
            lanes = pl.ds(pl.multiple_of(step % split * FEED_TILE, 128), FEED_TILE)
            place = 2 * (step // split % 2)
            inner = dot_nn(branch[...], down[0])
            grad_inner = (slope[...].astype(jnp.float32) * inner).astype(LOW)
            shape = made.shape[1:-1] + (FEED_TILE,)
            made[place, :, :, :, :, lanes] = dot_tn(low[...], grad_inner).astype(LOW).reshape(shape)
            made[place + 1, :, :, :, :, lanes] = (
                dot_tn(branch[...], hidden[...]).astype(LOW).reshape(shape)
            )
            bias_grad[...] = column_sum(grad_inner)
            total[...] += dot_nt(grad_inner, up[0])

        @pl.when(step == feeds - 1)
        def _():
            feed_sums[...] = jnp.zeros_like(feed_sums)

            def second_norm(at):
                grad, unit = total[at], unit_two[at]
                down_grad = norm_back(grad, unit, inverse_two[at], vectors[8:9])
                grad_two[at] = down_grad
                branch[at] = down_grad.astype(LOW)
                add_norm_sums(feed_sums, 0, branch[at], grad, unit)

            for_rows(total_rows, second_norm)
            load(1, wait=True)
            out_grad[...] = dot_tn(mixed[...], branch[...]).astype(LOW)
            low[...] = dot_nt(branch[...], weights[0]).astype(LOW)

        @pl.when((step >= heads) & (step < recall))
        def _():
            s, g = (step - heads) // groups, (step - heads) % groups
            slot = lax.broadcasted_iota(jnp.int32, (1, slots), 1)
            allowed = slot < lengths[s]
            sums[...] = jnp.zeros_like(sums)
            token_at = pl.ds(pl.multiple_of(s * rows, 16), rows)

            @pl.loop(0, CROSS_LANES // PAIR)
            def _(p):
                where = pl.ds(pl.multiple_of(p * PAIR, PAIR), PAIR)
                lanes = pl.ds(pl.multiple_of(g * CROSS_LANES + p * PAIR, PAIR), PAIR)
                columns = [pick_column(logs[0], 2 * p + which) for which in range(2)]
                found = attend_pair_back(
                    query[:, where], keys[:, where], values[:, where], allowed, columns,
                    low[token_at, lanes],
                )
                grad_query[:, where] = found[0]
                shape = made.shape[1:-1] + (PAIR,)
                made[s, :, :, :, :, lanes] = found[1].reshape(shape)
                made[count + s, :, :, :, :, lanes] = found[2].reshape(shape)
                sums[0, 0:1, where] = column_sum(found[0])
                sums[0, 1:2, where] = column_sum(found[2])

        @pl.when(step >= recall)
        def _():
            t = step - recall
            half = made.shape[1] // 2
            at = pl.ds(t % 2 * half, half)
            lanes = pl.ds(pl.multiple_of(t * tile_lanes, 128), tile_lanes)
            memory_grad[...] = dot_nt(
                made[t // 2, at].reshape(tile_rows, span), weights[0]
            ) + dot_nt(made[count + t // 2, at].reshape(tile_rows, span), weights[1])

            @pl.loop(0, 2)
            def _(number):
                part = made[pl.ds(count * number, count), :, :, :, :, lanes]
                product = dot_tn(memory_low[...], part.reshape(count * slots, tile_lanes))
                weight_grad[number] = product.astype(LOW)

        @pl.when(step == last)
        def _():
            rounds.finish()

    def feed(i):
        return jnp.minimum(i, feeds - 1)

    def head(i):
        return jnp.clip(i - heads, 0, recall - heads - 1)

    def later(i):
        return jnp.maximum(i - recall, 0)

    tile = pl.BlockSpec((total_rows, FEED_TILE), lambda i: (0, feed(i)))

    def feed_spec(number):
        return pl.BlockSpec(
            (1, span, FEED_TILE), lambda i: (2 * (feed(i) // split) + number, 0, feed(i) % split)
        )

    token = pl.BlockSpec((rows, CROSS_LANES), lambda i: (head(i) // groups, head(i) % groups))
    held = pl.BlockSpec((slots, CROSS_LANES), lambda i: (head(i) // groups, head(i) % groups))
    anywhere = pl.BlockSpec(memory_space=pl.ANY)
    return pl.pallas_call(
        kernel,
        grid=(last + 1,),
        in_specs=[
            pl.BlockSpec(memory_space=pltpu.SMEM),
            once_spec(unit_two.shape),
            once_spec(inverse_two.shape),
            once_spec(vectors.shape),
            tile,
            tile,
            feed_spec(0),
            feed_spec(1),
            once_spec(mixed.shape),
            token,
            held,
            held,
            pl.BlockSpec((1, rows, 128), lambda i: (head(i), 0, 0)),
            anywhere,
            anywhere,
            anywhere,
        ]
        + reduction.in_specs(),
        out_specs=[
            pl.BlockSpec((1, FEED_TILE), lambda i: (0, feed(i))),
            once_spec((total_rows, span)),
            once_spec((span, span)),
            once_spec((8, span)),
            token,
            pl.BlockSpec((1, 8, CROSS_LANES), lambda i: (head(i) // groups, 0, head(i) % groups)),
            pl.BlockSpec((tile_rows, span), lambda i: (later(i), 0)),
            pl.BlockSpec((2, span, tile_lanes), lambda i: (0, 0, later(i))),
        ]
        + reduction.out_specs(),
        out_shape=[
            jax.ShapeDtypeStruct((1, feeds * FEED_TILE), jnp.float32),
            jax.ShapeDtypeStruct((total_rows, span), jnp.float32),
            jax.ShapeDtypeStruct((span, span), LOW),
            jax.ShapeDtypeStruct((8, span), jnp.float32),
            jax.ShapeDtypeStruct(query.shape, LOW),
            jax.ShapeDtypeStruct((count, 8, span), jnp.float32),
            jax.ShapeDtypeStruct(memory.shape, jnp.float32),
            jax.ShapeDtypeStruct((2, span, span), LOW),
        ]
        + reduction.outs(),
        scratch_shapes=[
            pltpu.VMEM((total_rows, span), LOW),
            pltpu.VMEM((total_rows, span), LOW),
            pltpu.VMEM((total_rows, span), jnp.float32),
            pltpu.VMEM(memory.shape, LOW),
            pltpu.VMEM((2, span, span), LOW),
            pltpu.SemaphoreType.DMA((5,)),
        ]
        + reduction.scratch(),
        compiler_params=params(collective_id=collective_id, has_side_effects=True),
        name="middle_backward",
    )(
        lengths, unit_two, inverse_two, vectors, hidden, slope, feed_full, feed_full, mixed,
        query, keys, values, logs, grad_three, memory, cross_full, *reduction.operands(),
    )


def self_backward(
    reduction, collective_id, tokens, mask, vectors, self_full, cross_full, saved, cross_query_grad,
    grad_two, cross_sums, feed_sums, out_sums, bias_grad
):
    count, length, span = tokens.shape
    qkv, mixed, logs, unit, inverse = saved
    rows, total_rows = padded(length), mixed.shape[0]
    attend = 2
    project = attend + count
    last = project + 2
    carried, produced = len(reduction.operands()), len(reduction.outs())
    fetched = (cross_query_grad, cross_full, unit, grad_two, mixed, qkv, logs, tokens)
    plan = {
        0: (0, 1, 2, 0),
        1: (2,),
        attend: (0, 1, 4),
        attend + 1: (2, 4, 3),
        project: (0, 3, 2),
        project + 1: (4,),
        last: (6, 1, 5, 0, 2, 6, 4),
    }

    def kernel(*refs):
        mask, vectors, weight, inverse, cross_sums, feed_sums, out_sums, bias_grad = refs[:8]
        sources, refs = refs[8 : 8 + len(fetched)], refs[8 + len(fetched) :]
        operands, refs = refs[:carried], refs[carried:]
        input_grad, results, refs = refs[0], refs[1 : 1 + produced], refs[1 + produced :]
        (low, grads, total, load_sems), refs = refs[:4], refs[4:]
        held, scratch = refs[: len(fetched)], refs[len(fetched) :]
        cross_query_grad, query_weight, unit, grad_two, mixed, qkv, logs, tokens = held

        def load(numbers, wait=False):
            for number in numbers:
                source = sources[number]
                if number == 1:
                    source = source.at[0]
                copy = pltpu.make_async_copy(source, held[number], load_sems.at[number])
                copy.wait() if wait else copy.start()

        step = pl.program_id(0)
        rounds, made, terms, vector_flow = reduction.rounds(operands, results, scratch)
        for start, begins in plan.items():

            @pl.when(step == start)
            def _():
                if start == 0:
                    load(range(len(fetched)))
                    reduction.greet()
                if start == project:
                    rounds.first.append(vector_flow)
                rounds.move(begins, reduction.parts)

        def keep(number, product):
            made[number] = product.astype(LOW).reshape(made.shape[1:])

        @pl.when(step == 0)
        def _():
            terms[...] = jnp.zeros_like(terms)
            load(range(4), wait=True)

            def remake(at):
                grads[1, at] = (unit[at] * vectors[3:4] + vectors[4:5]).astype(LOW)

            for_rows(total_rows, remake)
            keep(0, dot_tn(grads[1], cross_query_grad[...]) * SCALE)
            total[...] = dot_nt(cross_query_grad[...], query_weight[...]) * SCALE

            def first_norm(at):
                grad = grad_two[at] + total[at]
                down_grad = norm_back(grad, unit[at], inverse[at], vectors[3:4])
                total[at] = down_grad
                grads[2, at] = down_grad.astype(LOW)
                add_norm_sums(terms, 2, grads[2, at], grad, unit[at])

            for_rows(total_rows, first_norm)
            spread = jnp.sum(cross_sums[...], axis=0)
            terms[5:6] = spread[0:1] * SCALE
            terms[6:7] = spread[1:2]
            terms[7:10] = out_sums[0:3]
            terms[10:13] = feed_sums[0:3]
            for k in range(bias_grad.shape[1] // span):
                terms[13 + k : 14 + k] = bias_grad[:, k * span : (k + 1) * span]

        @pl.when(step == 1)
        def _():
            load(range(4, len(fetched)), wait=True)
            fill_tokens(low, tokens)
            keep(1, dot_tn(mixed[...], grads[2]))
            grads[0] = dot_nt(grads[2], weight[0]).astype(LOW)

        @pl.when((step >= attend) & (step < project))
        def _():
            s = step - attend
            allowed = causal_allowed(rows, mask[pl.ds(s, 1)])
            table_at = pl.ds(pl.multiple_of(s * rows, 16), rows)

            def pair(lane, head):
                where = (table_at, pl.ds(lane, PAIR))
                table = logs[table_at]
                columns = [pick_column(table, head + which) for which in range(2)]
                found = attend_pair_back(
                    qkv[(0,) + where],
                    qkv[(1,) + where],
                    qkv[(2,) + where],
                    allowed,
                    columns,
                    grads[(0,) + where],
                )
                for number in range(3):
                    grads[(1 + number,) + where] = found[number]

            for_head_groups(span, pair)

        @pl.when(step == project - 1)
        def _():
            terms[0:1] = column_sum(grads[1]) * SCALE
            terms[1:2] = column_sum(grads[3])

        @pl.when(step >= project)
        def _():
            factor = jnp.where(step == project, SCALE, 1.0)
            part = grads[step - project + 1]
            keep(step - project + 2, dot_tn(low[...], part) * factor)
            total[...] += dot_nt(part, weight[0]) * factor

        @pl.when(step == last)
        def _():
            store_tokens(input_grad, total[...])
            rounds.finish()

    small = (mask, vectors, self_full, inverse, cross_sums, feed_sums, out_sums, bias_grad)
    specs = [once_spec(operand.shape) for operand in small]
    specs[2] = pl.BlockSpec(
        (1, span, span), lambda i: (jnp.where(i < project, 3, i - project), 0, 0)
    )
    return pl.pallas_call(
        kernel,
        grid=(last + 1,),
        in_specs=specs
        + [pl.BlockSpec(memory_space=pl.ANY)] * len(fetched)
        + reduction.in_specs(),
        out_specs=[once_spec(tokens.shape)] + reduction.out_specs(),
        out_shape=[jax.ShapeDtypeStruct(tokens.shape, jnp.float32)] + reduction.outs(),
        scratch_shapes=[
            pltpu.VMEM((total_rows, span), LOW),
            pltpu.VMEM((4, total_rows, span), LOW),
            pltpu.VMEM((total_rows, span), jnp.float32),
            pltpu.SemaphoreType.DMA((len(fetched),)),
        ]
        + [
            pltpu.VMEM((span, span) if number == 1 else array.shape, array.dtype)
            for number, array in enumerate(fetched)
        ]
        + reduction.scratch(),
        compiler_params=params(collective_id=collective_id, has_side_effects=True),
        name="self_backward",
    )(*small, *fetched, *reduction.operands())


def hand_over(arrays):
    pieces = []
    for number, array in enumerate(arrays):
        parts = 8 if array.shape[0] % 64 == 0 else array.shape[0] if array.ndim == 3 else 1
        size = array.shape[0] // parts
        pieces += [(number, part * size, size) for part in range(parts)]
    count = len(arrays)

    def kernel(*refs):
        sources, targets, rest = refs[:count], refs[count : 2 * count], refs[2 * count :]
        buffers, loads, stores = rest[:-2], rest[-2], rest[-1]

        def load(k):
            number, first, size = pieces[k]
            return pltpu.make_async_copy(sources[number].at[pl.ds(first, size)], buffers[k], loads.at[k])

        def store(k):
            number, first, size = pieces[k]
            return pltpu.make_async_copy(buffers[k], targets[number].at[pl.ds(first, size)], stores.at[k])

        for k in range(len(pieces)):
            load(k).start()
        for k in range(len(pieces)):
            load(k).wait()
            store(k).start()
        for k in range(len(pieces)):
            store(k).wait()

    anywhere = pl.BlockSpec(memory_space=pl.ANY)
    return pl.pallas_call(
        kernel,
        in_specs=[anywhere] * count,
        out_specs=[anywhere] * count,
        out_shape=[jax.ShapeDtypeStruct(array.shape, array.dtype) for array in arrays],
        scratch_shapes=[
            pltpu.VMEM((size,) + arrays[number].shape[1:], arrays[number].dtype)
            for number, first, size in pieces
        ]
        + [pltpu.SemaphoreType.DMA((len(pieces),))] * 2,
        compiler_params=params(),
        name="hand_over",
    )(*arrays)


def per_device(
    wide,
    narrow,
    decoder_input,
    memory,
    decoder_mask,
    memory_length,
    self_weights,
    cross_weights,
    feed_weights,
    vectors,
    hidden_bias,
    cotangent,
):
    seq_count, seq_length, model_width = decoder_input.shape
    mem_span = memory.shape[1]
    memory_low = memory.reshape(seq_count * mem_span, model_width)
    saved, (self_full, cross_full, feed_full, vector_all, unused_bias) = front(
        Gather(
            wide, narrow, [self_weights, cross_weights, feed_weights], [vectors, hidden_bias]
        ),
        decoder_input,
        decoder_mask,
        memory_length,
        memory_low,
        cotangent,
        1,
    )
    qkv, self_mixed, unit_one, cross_query, cross_keys, cross_values, cross_mixed, unit_two = saved[:8]
    self_logs, inverse_one, cross_logs = saved[8:11]
    hidden, slope, layer_output, inverse_two, grad_three, feed_sums = saved[11:]
    parts = feed_full.shape[0] // 2
    (
        bias_part, grad_two, cross_out_grad, out_sums, cross_gq, cross_sums, memory_grad, memory_parts, feed_grad
    ) = middle_backward(
        Reduction(
            wide,
            narrow,
            model_width,
            [],
            1,
            [(0, matrix, part) for part in range(parts) for matrix in range(2)],
            [(2, parts)],
            [2 * (part % 2) + matrix for part in range(parts) for matrix in range(2)],
        ),
        grad_three,
        unit_two,
        inverse_two,
        vector_all,
        hidden,
        slope,
        feed_full,
        cross_full,
        cross_mixed,
        cross_query,
        cross_keys,
        cross_values,
        memory_length,
        cross_logs,
        memory_low,
        2,
    )
    places = [(0, 1), (0, 2), (0, 3), (0, 0), (1, 3), (1, 0), (1, 1), (1, 2)]
    input_grad, cross_grad, self_weight_gradient, vectors_grad, hidden_bias_grad = self_backward(
        Reduction(
            wide,
            narrow,
            model_width,
            [memory_parts, cross_out_grad[None]],
            2,
            [place + (0,) for place in places],
            [(4, 1), (4, 1)],
            range(5),
            [vectors.shape, hidden_bias.shape],
        ),
        3,
        decoder_input,
        decoder_mask,
        vector_all,
        self_full,
        cross_full,
        (qkv, self_mixed, self_logs, unit_one, inverse_one),
        cross_gq,
        grad_two,
        cross_sums,
        feed_sums,
        out_sums,
        bias_part,
    )
    (
        memory_grad, input_grad, layer_output, feed_grad, cross_grad, self_weight_gradient, vectors_grad,
        hidden_bias_grad,
    ) = hand_over(
        [
            memory_grad, input_grad, layer_output, feed_grad, cross_grad, self_weight_gradient,
            vectors_grad, hidden_bias_grad,
        ]
    )
    return (
        layer_output,
        input_grad,
        memory_grad.reshape(seq_count, mem_span, model_width),
        self_weight_gradient,
        cross_grad,
        feed_grad,
        vectors_grad,
        hidden_bias_grad,
    )


def solution(mesh):
    placed = (
        P(("wide", "narrow"), None, None),
        P(("wide", "narrow"), None, None),
        P(("wide", "narrow"), None),
        P(("wide", "narrow")),
        P(None, "wide", "narrow"),
        P(None, "wide", "narrow"),
        P(None, "wide", "narrow"),
        P(None, "narrow"),
        P(None, "narrow"),
        P(("wide", "narrow"), None, None),
    )
    return jax.shard_map(
        functools.partial(per_device, mesh.shape["wide"], mesh.shape["narrow"]),
        mesh=mesh,
        in_specs=placed,
        out_specs=(
            P(("wide", "narrow"), None, None),
            P(("wide", "narrow"), None, None),
            P(("wide", "narrow"), None, None),
            P(None, "wide", "narrow"),
            P(None, "wide", "narrow"),
            P(None, "wide", "narrow"),
            P(None, "narrow"),
            P(None, "narrow"),
        ),
        check_vma=False,
    )
```
